256 devices in a mesh: dp: 64 (over z, x, core), feat: 4 (over y).
Axes of the slice: x: 4, y: 4, z: 8, core: 2. Of those that a mesh axis runs over, the one named last changes fastest.
Arguments:
- embeddings: bfloat16 [262144, 2048], P('dp', 'feat'), may hold values from -6 to 6
- sample_owner: int32 [262144], P('dp'), may hold values from 0 to 1535
- lloyd_assign: int32 [2, 1536], P(None, 'dp'), may hold values from 0 to 1023
- init_centroids: float32 [1024, 2048], P('dp', 'feat'), may hold values from -6 to 6
Outputs:
- centroids: float32 [1024, 2048], P('dp', 'feat')
- spread: float32 [2, 1536], P(None, 'dp')
The draws below stay inside these ranges and needn't reach their ends.
All inputs are finite; a program needn't handle non-finite values.
Results may differ from the reference program's by a relative error of at most 0.0003.
Values sent between devices are 32-bit elements; how exact they have to be, the bound alone decides.
A program may use at most 64 MiB of HBM per device.

```python
import math
import jax
import jax.numpy as jnp
import numpy as np
from jax import lax

D = 2048
SAMPLES = 262144
C = 1536
K = 1024


def plant(array, own_key, least, high):
    longest = array.shape.index(max(array.shape))
    spots = []
    for shift in (0, 1):
        where = [jax.random.randint(jax.random.fold_in(own_key, axis), (), 0, length) for axis, length in enumerate(array.shape)]
        where[longest] = (where[longest] + shift) % array.shape[longest]
        spots.append(tuple(where))
    return array.at[spots[0]].set(least).at[spots[1]].set(high)


def shard_levels(own_key, shape, shards, least, high):
    level, own = 1.0, jax.random.fold_in(own_key, 6)
    for position, blocks in shards:
        draws = jnp.exp(jax.random.uniform(jax.random.fold_in(own, position), (blocks,), jnp.float32, least / len(shards), high / len(shards)))
        level = level * jnp.repeat(draws, shape[position] // blocks).reshape([-1 if axis == position else 1 for axis in range(len(shape))])
    return level


def rank_table(number_of, lean):
    loads = [(1 << 20) // math.isqrt(grade ** lean) + 1 for grade in range(1, number_of + 1)]
    scale = 1 + sum(loads) // (1 << 30)
    return np.cumsum(np.array([max(1, weight // scale) for weight in loads]))


def ranked_ids(key, shape, count, skew):
    listing = rank_table(count, skew)
    ticket = jax.random.randint(jax.random.fold_in(key, 1), shape, 0, int(listing[count - 1]))
    grade = jnp.searchsorted(jnp.asarray(listing, jnp.int32), ticket, side="right")
    return jax.random.permutation(jax.random.fold_in(key, 2), count)[grade].astype(jnp.int32)


def noise(stream_key, shape, scale, bound, pieces=(), kind=jnp.bfloat16):
    drawn = jax.random.normal(stream_key, shape, jnp.float32) * scale
    if len(pieces) > 0:
        drawn = shard_levels(stream_key, shape, pieces, -0.22, 0.18) * drawn
    return jnp.clip(drawn, min=-bound, max=bound).astype(kind)


def setup_inputs(seed: int = 0) -> dict:
    keys = jax.random.split(jax.random.key(seed), 5)
    embeddings = noise(keys[0], (SAMPLES, D), 1.0, 6.0, ((0, 64), (1, 4)))
    sample_owner = plant(ranked_ids(keys[1], (SAMPLES,), C, 2), jax.random.fold_in(keys[1], 3), 0, C - 1).astype(jnp.int32)
    lloyd_assign = plant(ranked_ids(keys[2], (2, C), K, 2), jax.random.fold_in(keys[2], 3), 0, K - 1).astype(jnp.int32)
    init_centroids = noise(keys[3], (K, D), 1.0, 6.0, ((0, 64), (1, 4)), jnp.float32)
    return {"embeddings": embeddings, "sample_owner": sample_owner, "lloyd_assign": lloyd_assign, "init_centroids": init_centroids}


EPS = 1e-06

def normalize(rows):
    return rows * lax.rsqrt(lax.optimization_barrier(jnp.mean(rows * rows, axis=1, keepdims=True)) + EPS)

def reference(embeddings, sample_owner, lloyd_assign, init_centroids):
    sums = jax.ops.segment_sum(embeddings.astype(jnp.float32), sample_owner, C)
    counts = jax.ops.segment_sum(jnp.ones(sample_owner.shape, jnp.float32), sample_owner, C)
    means = normalize(sums)
    weighted = counts[:, None] * means
    prev = init_centroids
    spreads = []
    for step in range(2):
        assign = lloyd_assign[step]
        total = jax.ops.segment_sum(weighted, assign, K)
        weight = jax.ops.segment_sum(counts, assign, K)
        fresh = normalize(total)
        current = jnp.where(weight[:, None] > 0, fresh, prev)
        diff = means - jnp.take(fresh, assign, axis=0)
        spreads.append(lax.optimization_barrier(jnp.mean(diff * diff, axis=1)))
        prev = current
    return (prev, jnp.stack(spreads))
```

```python
import jax
import jax.numpy as jnp
from jax import lax
from jax.experimental import pallas as pl
from jax.experimental.pallas import tpu as pltpu
from jax.sharding import PartitionSpec as P

EPS = 1e-06
MESH = pl.DeviceIdType.MESH

NZ, NX, NC, NY = 8, 4, 2, 4
OWN = 24
ROWS = NX * OWN
BLOCKS = NZ * NC
HEAD = 40
TAIL = ROWS - HEAD
CUT = 64
LANE = 128
ORDER = ((4, 3), (-3, 2), (-2, 1), (-1, 0))


def position(owner):
    slab = lax.shift_right_logical(owner * 21846, 22)
    left = owner - slab * (NX * NC * OWN)
    column = lax.shift_right_logical(left * 1366, 16)
    inner = left - column * (NC * OWN)
    core = jnp.where(inner >= OWN, 1, 0)
    block = slab * NC + core
    return block, column * OWN + inner - core * OWN


def as_rows(columns, pad_ref):
    pad_ref[...] = jnp.zeros_like(pad_ref)
    lane = lax.broadcasted_iota(jnp.int32, (ROWS, LANE), 1)
    filled = jnp.zeros((ROWS, LANE), jnp.float32)
    for j, column in enumerate(columns):
        filled = jnp.where(lane == j, column, filled)
    pad_ref[0:ROWS, :] = filled
    return jnp.transpose(pad_ref[...])[0:8, :]


def as_columns(tile):
    return jnp.transpose(tile)


def kernel(
    depth, width, features,
    owner_ref, assign_ref, init_ref, emb_hbm,
    cent_ref, spread_ref,
    emb, part, other, other_in, xin, zr, zl, qr, ql, hx,
    prow, info, info_x, group, info_z, counts, match, weight, pad, wrows,
    table, sq_own, sq_in, scale, scale2, scaled, final_own, final_in, sel, sel_in, lens,
    load_sem, send_sem, recv_sem,
):
    dp, y = lax.axis_index("dp"), lax.axis_index("feat")
    z, x, c = lax.div(dp, NX * NC), lax.rem(lax.div(dp, NC), NX), lax.rem(dp, NC)

    def zat(d):
        return lax.rem(z + d + NZ, NZ)

    def xat(d):
        return lax.rem(x + d + NX, NX)

    def device(dz=0, dx=0, dc=0, dy=0):
        return (zat(dz) * (NX * NC) + xat(dx) * NC + lax.rem(c + dc, NC), lax.rem(y + dy, NY))

    used = [0]
    sent = []

    def copy_at(slot, src, dst, to):
        return pltpu.make_async_remote_copy(
            src_ref=src, dst_ref=dst, send_sem=send_sem.at[slot], recv_sem=recv_sem.at[slot],
            device_id=to, device_id_type=MESH,
        )

    def go(src, dst, to):
        copy = copy_at(used[0], src, dst, to)
        used[0] += 1
        copy.start()
        sent.append(copy.wait_send)
        return copy

    def go_all(first, last, make):
        base = used[0]
        used[0] += last - first

        def at(j):
            src, dst, to = make(j)
            return copy_at(base + j - first, src, dst, to)

        def run(act):
            def step(j, carry):
                act(at(j))
                return carry
            lax.fori_loop(first, last, step, 0)

        run(lambda copy: copy.start())
        sent.append(lambda: run(lambda copy: copy.wait_send()))
        return lambda: run(lambda copy: copy.wait_recv())

    chunks = emb.shape[0] // depth
    loads = [
        pltpu.make_async_copy(
            emb_hbm.at[pl.ds(k * depth, depth)], emb.at[pl.ds(k * depth, depth)], load_sem.at[k]
        )
        for k in range(chunks)
    ]
    for load in loads:
        load.start()

    barrier = pltpu.get_barrier_semaphore()

    def greet(first, last, to):
        def step(j, carry):
            pl.semaphore_signal(barrier, inc=1, device_id=to(j), device_id_type=MESH)
            return carry
        lax.fori_loop(first, last, step, 0)

    greet(1, 8, lambda j: device(dx=lax.div(j, 2), dc=lax.rem(j, 2)))
    greet(0, 12, lambda j: device(dx=lax.div(j, 3), dy=lax.rem(j, 3) + 1))
    greet(2, 16, lambda j: device(dz=lax.div(j, 2), dc=lax.rem(j, 2)))

    block, place = position(owner_ref[...])
    prow[...] = block * ROWS + place
    samples = owner_ref.shape[1]
    high = lax.broadcasted_iota(jnp.int32, (BLOCKS, samples), 0) == block
    low = lax.broadcasted_iota(jnp.int32, (LANE, samples), 0) == place
    info[0:BLOCKS, :] = lax.dot_general(
        jnp.where(high, 1.0, 0.0).astype(jnp.bfloat16),
        jnp.where(low, 1.0, 0.0).astype(jnp.bfloat16),
        (((1,), (1,)), ((), ())), preferred_element_type=jnp.float32,
    )
    placed = pltpu.roll(assign_ref[...], x * OWN, 1)
    info[BLOCKS : BLOCKS + 8, :] = jnp.where(c == 0, placed, pltpu.roll(placed, 2, 0))
    part[...] = jnp.zeros_like(part)
    other[...] = jnp.zeros_like(other)

    pl.semaphore_wait(barrier, 7 + 12 + 14)

    arrived = go_all(
        1, 8, lambda j: (info, info_x.at[j], device(dx=lax.div(j, 2), dc=lax.rem(j, 2)))
    )
    info_x[0] = info[...]

    def sums(slabs, core, into, waits=()):
        bases = [slab * (NC * ROWS) + core * ROWS for slab in slabs]
        row = lax.broadcasted_iota(jnp.int32, (ROWS, depth), 0)

        def step(k):
            at = pl.ds(pl.multiple_of(k * depth, depth), depth)
            p = prow[:, at]
            hot = jnp.concatenate(
                [jnp.where(row == p - base, 1.0, 0.0).astype(jnp.bfloat16) for base in bases], 0
            )
            got = jnp.dot(hot, emb[at, :], preferred_element_type=jnp.float32)
            for j, ref in enumerate(into):
                for b in range(NX):
                    ref[b] += got[j * ROWS : (j + 1) * ROWS, b * LANE : (b + 1) * LANE]

        if waits:
            for k in range(chunks):
                waits[k].wait()
                step(k)
        else:
            lax.fori_loop(0, chunks, lambda k, carry: (step(k), carry)[1], 0)

    cross = {}

    def work(g):
        slabs = [zat(d) for d in ORDER[g]]
        sums(slabs, 1 - c, [other.at[g, 0], other.at[g, 1]], loads if g == 0 else ())
        cross[g] = go(other.at[g], other_in.at[g], device(dc=1))
        sums(slabs, c, [part.at[slab] for slab in slabs])

    def meet(g):
        cross[g].wait_recv()
        for j, d in enumerate(ORDER[g]):
            part[zat(d)] += other_in[g, j]

    tail = pl.ds(HEAD, TAIL)
    xs = {}

    def x_start(g):
        first, second = (zat(d) for d in ORDER[g])
        right, left = device(dx=1), device(dx=-1)
        xs[g, 0] = go(part.at[first, xat(2), tail], xin.at[g, 0], right)
        xs[g, 3] = go(part.at[second, xat(2), tail], xin.at[g, 3], left)
        xs[g, 1] = go(part.at[second, xat(1), tail], xin.at[g, 1], right)
        xs[g, 4] = go(part.at[first, xat(-1), tail], xin.at[g, 4], left)

    def x_mid(g):
        first, second = (zat(d) for d in ORDER[g])
        xs[g, 0].wait_recv()
        part[first, xat(1), HEAD:ROWS] += xin[g, 0]
        xs[g, 2] = go(part.at[first, xat(1), tail], xin.at[g, 2], device(dx=1))
        xs[g, 3].wait_recv()
        part[second, xat(-1), HEAD:ROWS] += xin[g, 3]
        xs[g, 5] = go(part.at[second, xat(-1), tail], xin.at[g, 5], device(dx=-1))

    def x_end(g):
        first, second = (zat(d) for d in ORDER[g])
        xs[g, 4].wait_recv()
        xs[g, 2].wait_recv()
        part[first, x, HEAD:ROWS] += xin[g, 4] + xin[g, 2]
        xs[g, 1].wait_recv()
        xs[g, 5].wait_recv()
        part[second, x, HEAD:ROWS] += xin[g, 1] + xin[g, 5]

    head = pl.ds(0, HEAD)
    zs = {}

    def z_head(h, way):
        slab = zat((4 - h) * way)
        into, half = (zr, 0) if way > 0 else (zl, 2)
        if h == 0:
            at = pl.ds(half, 2)
            zs[h, way] = go(part.at[slab, at, head], into.at[0, at], device(dz=way))
            return
        zs[h - 1, way].wait_recv()
        if h == 1:
            part[slab, half : half + 2, 0:HEAD] += into[0, half : half + 2]
        else:
            part[slab, :, 0:HEAD] += into[h - 1]
        zs[h, way] = go(part.at[slab, :, head], into.at[h], device(dz=way))

    def z_head_end():
        zs[3, 1].wait_recv()
        zs[3, -1].wait_recv()
        part[z, :, 0:HEAD] += zr[3] + zl[3]

    ts = {}

    def z_tail(h, way):
        slab = zat((4 - h) * way)
        into, start, size = (qr, HEAD, CUT - HEAD) if way > 0 else (ql, CUT, ROWS - CUT)
        if h == 0:
            ts[h, way] = go(
                part.at[slab, x, pl.ds(start, size)], into.at[0, pl.ds(0, size)], device(dz=way)
            )
            return
        ts[h - 1, way].wait_recv()
        if h == 1:
            part[slab, x, start : start + size] += into[0, 0:size]
        else:
            part[slab, x, HEAD:ROWS] += into[h - 1]
        ts[h, way] = go(part.at[slab, x, tail], into.at[h], device(dz=way))

    def z_tail_end():
        ts[3, 1].wait_recv()
        ts[3, -1].wait_recv()
        part[z, x, HEAD:ROWS] += qr[3] + ql[3]

    work(0)
    meet(0)
    z_head(0, 1)
    z_head(0, -1)
    x_start(0)

    arrived()
    whole = info_x[0]
    for j in range(1, NX * NC):
        whole = whole + info_x[j]
    group[...] = whole
    info_z[z] = whole
    arrived_z = go_all(1, NZ, lambda j: (group, info_z.at[z], device(dz=j)))

    work(1)
    meet(1)
    z_head(1, 1)
    z_head(1, -1)
    x_mid(0)
    x_start(1)

    work(2)
    meet(2)
    z_head(2, 1)
    z_head(2, -1)
    x_mid(1)
    x_start(2)
    x_end(0)
    z_tail(0, 1)
    z_tail(0, -1)

    work(3)
    meet(3)
    z_head(3, 1)
    z_head(3, -1)
    x_mid(2)
    x_start(3)
    x_end(1)
    z_tail(1, 1)
    z_tail(1, -1)
    x_mid(3)
    x_end(2)
    z_tail(2, 1)
    z_tail(2, -1)
    z_head_end()
    hop = go(part.at[z, xat(2), head], hx.at[0], device(dx=1))
    back = go(part.at[z, xat(-1), head], hx.at[1], device(dx=-1))
    x_end(3)
    z_tail(3, 1)
    z_tail(3, -1)
    hop.wait_recv()
    part[z, xat(1), 0:HEAD] += hx[0]
    last = go(part.at[z, xat(1), head], hx.at[2], device(dx=1))
    z_tail_end()
    back.wait_recv()
    last.wait_recv()
    part[z, x, 0:HEAD] += hx[1] + hx[2]

    own = part[z, x]
    mine = z * NC + c
    table[mine] = own

    rings = {}

    def blk(dz):
        return zat(dz) * NC + c

    def z_share(h, way):
        at = blk(-h * way)
        if h == 3:
            rows = pl.ds(0, ROWS // 2) if way > 0 else pl.ds(ROWS // 2, ROWS // 2)
        else:
            rows = pl.ds(0, ROWS)
        rings[h, way] = go(table.at[at, rows], table.at[at, rows], device(dz=way))

    pairs = []

    def core_share(dz):
        at = blk(dz)
        pairs.append(go(table.at[at], table.at[at], device(dc=1)))

    z_share(0, 1)
    z_share(0, -1)
    core_share(0)

    square = jnp.sum(own * own, axis=1, keepdims=True)
    sq_own[0] = as_rows([square], pad)[0:1, :]
    sq_arrived = go_all(
        1, NX * NY,
        lambda j: (sq_own.at[0], sq_in.at[j], device(dx=lax.div(j, NY), dy=lax.rem(j, NY))),
    )

    arrived_z()
    total = info_z[0, 0:BLOCKS]
    for j in range(1, NZ):
        total = total + info_z[j, 0:BLOCKS]
    counts[...] = total

    for way in (1, -1):
        rings[0, way].wait_recv()
        z_share(1, way)
    core_share(-1)
    core_share(1)

    keys_all = group[BLOCKS : BLOCKS + 8, :]
    keys = as_columns(jnp.where(c == 0, keys_all, pltpu.roll(keys_all, 6, 0)))
    cents = NX * cent_ref.shape[0]
    r = lax.broadcasted_iota(jnp.int32, (cents, LANE), 0)
    per = cent_ref.shape[0]
    r = z * (cents * NC) + lax.div(r, per) * (per * NC) + c * per + lax.rem(r, per)
    cent_key = r.astype(jnp.float32)
    spread_key = [jnp.broadcast_to(keys[0:ROWS, t : t + 1], (ROWS, LANE)) for t in range(2)]
    parts = [
        (0, cents, cent_key, 0), (cents, cents, cent_key, 1),
        (2 * cents, ROWS, spread_key[0], 0), (2 * cents + ROWS, ROWS, spread_key[1], 1),
    ]
    weight[...] = jnp.zeros_like(weight)
    for b in range(BLOCKS):
        many = counts[b : b + 1, :]
        for at, n, key, t in parts:
            line = BLOCKS + 2 * (b % NC) + t
            same = jnp.where(key == info_z[b // NC, line : line + 1, :], 1.0, 0.0)
            match[at : at + n, b * LANE : (b + 1) * LANE] = same.astype(jnp.bfloat16)
            weight[at : at + n, :] += same * many
    summed = jnp.sum(weight[...], axis=1, keepdims=True)
    weight[...] = jnp.broadcast_to(summed, weight.shape)
    first_row = 2 * cents
    wrows[...] = as_rows(
        [summed[first_row : first_row + ROWS], summed[first_row + ROWS : first_row + 2 * ROWS]], pad
    )

    sq_arrived()
    square_row = sq_own[0]
    for j in range(1, NX * NY):
        square_row = square_row + sq_in[j]
    inverse = lax.rsqrt(square_row / features + EPS)
    scale[mine] = inverse
    scale_arrived = go_all(
        1, NZ * NC,
        lambda j: (scale.at[mine], scale.at[mine], device(dz=lax.div(j, NC), dc=lax.rem(j, NC))),
    )
    means = own * as_columns(jnp.broadcast_to(inverse, (8, LANE)))[0:ROWS, 0:1]

    for way in (1, -1):
        rings[1, way].wait_recv()
        z_share(2, way)
    core_share(-2)
    core_share(2)
    for way in (1, -1):
        rings[2, way].wait_recv()
        z_share(3, way)
    core_share(-3)
    core_share(3)

    scale_arrived()
    for b in range(BLOCKS):
        scale2[b : b + 1, :] = scale[b]
    factor = as_columns(counts[...] * scale2[...])
    rings[3, 1].wait_recv()
    rings[3, -1].wait_recv()
    core_share(4)
    for pair in pairs:
        pair.wait_recv()
    scaled[...] = jnp.zeros_like(scaled)
    for b in range(BLOCKS):
        rows = table[b] * factor[0:ROWS, b : b + 1]
        for piece in range(3):
            near = rows.astype(jnp.bfloat16)
            scaled[b * LANE : b * LANE + ROWS, piece * LANE : (piece + 1) * LANE] = near
            rows = rows - near.astype(jnp.float32)
    tot = jnp.dot(match[...], scaled[...], preferred_element_type=jnp.float32)
    tot = tot[:, 0:LANE] + (tot[:, LANE : 2 * LANE] + tot[:, 2 * LANE : 3 * LANE])

    columns = []
    for t in range(2):
        at = first_row + t * ROWS
        many = weight[at : at + ROWS, :]
        g = tot[at : at + ROWS] * jnp.where(many > 0, 1.0 / jnp.maximum(many, 1.0), 0.0)
        d = means - g
        for v in (d * d, d * g, g * g):
            columns.append(jnp.sum(v, axis=1, keepdims=True))
    chosen = jnp.where(weight[cents : 2 * cents, :] > 0, tot[cents : 2 * cents], tot[0:cents])
    sel[...] = chosen
    squares = jnp.sum(chosen * chosen, axis=1, keepdims=True)
    columns.append(jnp.concatenate([squares, jnp.zeros((ROWS - cents, 1), jnp.float32)], 0))
    final_own[...] = as_rows(columns, pad)
    final_arrived = go_all(
        1, NX * NY,
        lambda j: (final_own, final_in.at[j], device(dx=lax.div(j, NY), dy=lax.rem(j, NY))),
    )
    sel_arrived = go_all(
        1, NX, lambda j: (sel.at[pl.ds(xat(j) * per, per)], sel_in.at[x], device(dx=j))
    )
    here = pl.ds(pl.multiple_of(x * per, per), per)
    sel_in[x] = sel[here, :]

    final_arrived()
    last_sum = final_own[...]
    for j in range(1, NX * NY):
        last_sum = last_sum + final_in[j]
    for t in range(2):
        far, mixed, length = (last_sum[3 * t + j : 3 * t + j + 1] for j in range(3))
        many = wrows[t : t + 1, :]
        s = many * lax.rsqrt(many * many * (length / features) + EPS) - 1.0
        value = (far - 2.0 * s * mixed + s * s * length) / features
        value = pltpu.roll(jnp.broadcast_to(value, (8, LANE)), LANE - x * OWN, 1)
        spread_ref[t : t + 1, :] = value[0:1, 0:OWN]
    lens[...] = as_columns(last_sum)
    length = lens[here, 6:7]
    inverse = lax.rsqrt(length / features + EPS)
    first = weight[here, :]
    second = weight[pl.ds(pl.multiple_of(x * per + cents, per), per), :]
    keep = jnp.maximum(first, second) > 0
    sel_arrived()
    for b in range(NX):
        at = slice(b * LANE, (b + 1) * LANE)
        cent_ref[:, at] = jnp.where(keep, sel_in[b] * inverse, init_ref[:, at])

    for wait in sent:
        wait()


COPIES = 7 + 7 + 4 + 24 + 8 + 8 + 3 + 8 + 8 + 15 + 15 + 15 + 3


def per_device(features, embeddings, sample_owner, lloyd_assign, init_centroids):
    samples, width = embeddings.shape
    per = init_centroids.shape[0]
    depth = 1024
    f32, bf16 = jnp.float32, jnp.bfloat16
    vm = pltpu.VMEM
    cents = NX * per
    lines = 2 * (cents + ROWS)
    scratch = [
        vm((samples, width), bf16),
        vm((NZ, NX, ROWS, LANE), f32),
        vm((4, 2, NX, ROWS, LANE), f32),
        vm((4, 2, NX, ROWS, LANE), f32),
        vm((4, 6, TAIL, LANE), f32),
        vm((4, NX, HEAD, LANE), f32),
        vm((4, NX, HEAD, LANE), f32),
        vm((4, TAIL, LANE), f32),
        vm((4, TAIL, LANE), f32),
        vm((3, HEAD, LANE), f32),
        vm((1, samples), jnp.int32),
        vm((24, LANE), f32),
        vm((NX * NC, 24, LANE), f32),
        vm((24, LANE), f32),
        vm((NZ, 24, LANE), f32),
        vm((BLOCKS, LANE), f32),
        vm((lines, BLOCKS * LANE), bf16),
        vm((lines, LANE), f32),
        vm((LANE, LANE), f32),
        vm((8, LANE), f32),
        vm((BLOCKS, ROWS, LANE), f32),
        vm((1, 1, LANE), f32),
        vm((NX * NY, 1, LANE), f32),
        vm((BLOCKS, 1, LANE), f32),
        vm((BLOCKS, LANE), f32),
        vm((BLOCKS * LANE, 3 * LANE), bf16),
        vm((8, LANE), f32),
        vm((NX * NY, 8, LANE), f32),
        vm((cents, LANE), f32),
        vm((NX, per, LANE), f32),
        vm((LANE, 8), f32),
        pltpu.SemaphoreType.DMA((samples // depth,)),
        pltpu.SemaphoreType.DMA((COPIES,)),
        pltpu.SemaphoreType.DMA((COPIES,)),
    ]
    assign = jnp.pad(lloyd_assign.astype(f32), ((0, 6), (0, LANE - OWN)))
    in_vmem = pl.BlockSpec(memory_space=pltpu.VMEM)

    def body(*refs):
        kernel(depth, width, features, *refs)

    return pl.pallas_call(
        body,
        name="recluster",
        out_shape=(
            jax.ShapeDtypeStruct((per, width), f32),
            jax.ShapeDtypeStruct((2, OWN), f32),
        ),
        in_specs=[in_vmem, in_vmem, in_vmem, pl.BlockSpec(memory_space=pltpu.HBM)],
        out_specs=(in_vmem, in_vmem),
        scratch_shapes=scratch,
        compiler_params=pltpu.CompilerParams(
            collective_id=0, has_side_effects=True, vmem_limit_bytes=48 << 20
        ),
    )(sample_owner.reshape(1, samples), assign, init_centroids, embeddings)


def solution(mesh):
    def run(embeddings, sample_owner, lloyd_assign, init_centroids):
        features = embeddings.shape[1]
        return jax.shard_map(
            lambda *args: per_device(features, *args),
            mesh=mesh,
            in_specs=(P("dp", "feat"), P("dp"), P(None, "dp"), P("dp", "feat")),
            out_specs=(P("dp", "feat"), P(None, "dp")),
            check_vma=False,
        )(embeddings, sample_owner, lloyd_assign, init_centroids)

    return run
```

```python
import jax
import jax.numpy as jnp
from jax import lax
from jax.experimental import pallas as pl
from jax.experimental.pallas import tpu as pltpu
from jax.sharding import PartitionSpec as P

EPS = 1e-06
MESH = pl.DeviceIdType.MESH

NZ, NX, NC, NY = 8, 4, 2, 4
OWN = 24
ROWS = NX * OWN
BLOCKS = NZ * NC
LANE = 128
ORDER = ((4, 3), (-3, 2), (-2, 1), (-1, 0))


def position(owner):
    slab = lax.shift_right_logical(owner * 21846, 22)
    left = owner - slab * (NX * NC * OWN)
    column = lax.shift_right_logical(left * 1366, 16)
    inner = left - column * (NC * OWN)
    core = jnp.where(inner >= OWN, 1, 0)
    block = slab * NC + core
    return block, column * OWN + inner - core * OWN


def as_rows(columns, pad_ref):
    pad_ref[...] = jnp.zeros_like(pad_ref)
    lane = lax.broadcasted_iota(jnp.int32, (ROWS, LANE), 1)
    filled = jnp.zeros((ROWS, LANE), jnp.float32)
    for j, column in enumerate(columns):
        filled = jnp.where(lane == j, column, filled)
    pad_ref[0:ROWS, :] = filled
    return jnp.transpose(pad_ref[...])[0:8, :]


def as_columns(tile):
    return jnp.transpose(tile)


def kernel(
    depth, width, features,
    owner_hbm, assign_hbm, init_hbm, emb_hbm,
    cent_ref, spread_ref,
    owner_ref, assign_ref, init_ref,
    emb, part, other, other_in, xin, zin,
    prow, tile, info, info_x, group, info_z, counts, match, weight, pad, wrows,
    table, sq_own, sq_in, scale, scale2, scaled, final_own, final_in, sel, sel_in, lens,
    load_sem, send_sem, recv_sem,
):
    dp, y = lax.axis_index("dp"), lax.axis_index("feat")
    z, x, c = lax.div(dp, NX * NC), lax.rem(lax.div(dp, NC), NX), lax.rem(dp, NC)

    def zat(d):
        return lax.rem(z + d + NZ, NZ)

    def xat(d):
        return lax.rem(x + d + NX, NX)

    def device(dz=0, dx=0, dc=0, dy=0):
        return (zat(dz) * (NX * NC) + xat(dx) * NC + lax.rem(c + dc, NC), lax.rem(y + dy, NY))

    used = [0]
    sent = []

    def copy_at(slot, src, dst, to):
        return pltpu.make_async_remote_copy(
            src_ref=src, dst_ref=dst, send_sem=send_sem.at[slot], recv_sem=recv_sem.at[slot],
            device_id=to, device_id_type=MESH,
        )

    def go(src, dst, to):
        copy = copy_at(used[0], src, dst, to)
        used[0] += 1
        copy.start()
        sent.append(copy.wait_send)
        return copy

    def go_all(first, last, make):
        base = used[0]
        used[0] += last - first

        def at(j):
            src, dst, to = make(j)
            return copy_at(base + j - first, src, dst, to)

        def run(act):
            def step(j, carry):
                act(at(j))
                return carry
            lax.fori_loop(first, last, step, 0)

        run(lambda copy: copy.start())
        sent.append(lambda: run(lambda copy: copy.wait_send()))
        return lambda: run(lambda copy: copy.wait_recv())

    chunks = emb.shape[0] // depth
    loads = [
        pltpu.make_async_copy(
            emb_hbm.at[pl.ds(k * depth, depth)], emb.at[pl.ds(k * depth, depth)], load_sem.at[k]
        )
        for k in range(chunks)
    ]
    small = [
        pltpu.make_async_copy(src, dst, load_sem.at[chunks + k])
        for k, (src, dst) in enumerate(
            ((owner_hbm, owner_ref), (assign_hbm, assign_ref), (init_hbm, init_ref))
        )
    ]
    for load in small + loads:
        load.start()

    barrier = pltpu.get_barrier_semaphore()

    def greet(first, last, to):
        def step(j, carry):
            pl.semaphore_signal(barrier, inc=1, device_id=to(j), device_id_type=MESH)
            return carry
        lax.fori_loop(first, last, step, 0)

    greet(1, 8, lambda j: device(dx=lax.div(j, 2), dc=lax.rem(j, 2)))
    greet(0, 12, lambda j: device(dx=lax.div(j, 3), dy=lax.rem(j, 3) + 1))
    greet(2, 16, lambda j: device(dz=lax.div(j, 2), dc=lax.rem(j, 2)))

    tile[...] = jnp.zeros_like(tile)
    part[...] = jnp.zeros_like(part)
    other[...] = jnp.zeros_like(other)
    for load in small:
        load.wait()
    block, place = position(owner_ref[...])
    prow[...] = block * ROWS + place

    def count():
        samples = owner_ref.shape[1]
        block, place = position(owner_ref[...])
        high = lax.broadcasted_iota(jnp.int32, (BLOCKS, samples), 0) == block
        low = lax.broadcasted_iota(jnp.int32, (LANE, samples), 0) == place
        info[0:BLOCKS, :] = lax.dot_general(
            jnp.where(high, 1.0, 0.0).astype(jnp.bfloat16),
            jnp.where(low, 1.0, 0.0).astype(jnp.bfloat16),
            (((1,), (1,)), ((), ())), preferred_element_type=jnp.float32,
        )
        tile[0:2, 0:OWN] = assign_ref[...].astype(jnp.float32)
        placed = pltpu.roll(tile[...], x * OWN, 1)
        info[BLOCKS : BLOCKS + 8, :] = jnp.where(c == 0, placed, pltpu.roll(placed, 2, 0))
        info_x[0] = info[...]
        return go_all(
            1, 8, lambda j: (info, info_x.at[j], device(dx=lax.div(j, 2), dc=lax.rem(j, 2)))
        )

    def sums(slabs, core, into, waits=()):
        bases = [slab * (NC * ROWS) + core * ROWS for slab in slabs]
        row = lax.broadcasted_iota(jnp.int32, (ROWS, depth), 0)

        def step(k):
            at = pl.ds(pl.multiple_of(k * depth, depth), depth)
            p = prow[:, at]
            hot = jnp.concatenate(
                [jnp.where(row == p - base, 1.0, 0.0).astype(jnp.bfloat16) for base in bases], 0
            )
            got = jnp.dot(hot, emb[at, :], preferred_element_type=jnp.float32)
            for j, ref in enumerate(into):
                for b in range(NX):
                    ref[b] += got[j * ROWS : (j + 1) * ROWS, b * LANE : (b + 1) * LANE]

        if waits:
            for k in range(chunks):
                waits[k].wait()
                step(k)
        else:
            lax.fori_loop(0, chunks, lambda k, carry: (step(k), carry)[1], 0)

    cross = {}

    def work_other(g):
        slabs = [zat(d) for d in ORDER[g]]
        sums(slabs, 1 - c, [other.at[g, 0], other.at[g, 1]], loads if g == 0 else ())
        if g == 0:
            pl.semaphore_wait(barrier, 7 + 12 + 14)
        cross[g] = go(other.at[g], other_in.at[g], device(dc=1))

    def work_own(g):
        sums([zat(d) for d in ORDER[g]], c, [part.at[g, 0], part.at[g, 1]])

    def meet(g):
        cross[g].wait_recv()
        part[g] += other_in[g]

    xs = {}

    def x_start(g):
        right, left = device(dx=1), device(dx=-1)
        xs[g, 0] = go(part.at[g, 0, xat(2)], xin.at[g, 0], right)
        xs[g, 3] = go(part.at[g, 1, xat(2)], xin.at[g, 3], left)
        xs[g, 1] = go(part.at[g, 1, xat(1)], xin.at[g, 1], right)
        xs[g, 4] = go(part.at[g, 0, xat(-1)], xin.at[g, 4], left)

    def x_mid(g):
        xs[g, 0].wait_recv()
        part[g, 0, xat(1)] += xin[g, 0]
        xs[g, 2] = go(part.at[g, 0, xat(1)], xin.at[g, 2], device(dx=1))
        xs[g, 3].wait_recv()
        part[g, 1, xat(-1)] += xin[g, 3]
        xs[g, 5] = go(part.at[g, 1, xat(-1)], xin.at[g, 5], device(dx=-1))

    def x_direct(g):
        for k, d in enumerate((2, 1, -1)):
            at = pl.ds(2 * k, 2)
            xs[g, k] = go(part.at[g, :, xat(d)], xin.at[g, at], device(dx=d))

    zs = {}

    def z_send(g, j):
        d = ORDER[g][j]
        if d != 0:
            zs[g, j] = go(part.at[g, j, x], zin.at[2 * g + j], device(dz=d))

    def x_end(g):
        xs[g, 4].wait_recv()
        xs[g, 2].wait_recv()
        part[g, 0, x] += xin[g, 4] + xin[g, 2]
        z_send(g, 0)
        xs[g, 1].wait_recv()
        xs[g, 5].wait_recv()
        part[g, 1, x] += xin[g, 1] + xin[g, 5]
        z_send(g, 1)

    def x_direct_end(g):
        for k in range(3):
            xs[g, k].wait_recv()
        for j in range(2):
            part[g, j, x] += xin[g, j] + xin[g, 2 + j] + xin[g, 4 + j]
            z_send(g, j)

    work_other(0)
    arrived = count()
    work_own(0)
    meet(0)
    x_start(0)

    work_other(1)
    arrived()
    whole = info_x[0]
    for j in range(1, NX * NC):
        whole = whole + info_x[j]
    group[...] = whole
    info_z[z] = whole
    arrived_z = go_all(1, NZ, lambda j: (group, info_z.at[z], device(dz=j)))
    work_own(1)
    meet(1)
    x_start(1)

    work_other(2)
    x_mid(0)
    work_own(2)
    meet(2)
    x_start(2)

    work_other(3)
    x_mid(1)
    x_end(0)
    work_own(3)
    meet(3)
    x_direct(3)
    x_mid(2)
    x_end(1)
    x_end(2)
    x_direct_end(3)
    own = part[3, 1, x]
    for g in range(4):
        for j in range(2):
            if (g, j) in zs:
                zs[g, j].wait_recv()
                own = own + zin[2 * g + j]

    mine = z * NC + c
    table[mine] = own
    rings, pairs = {}, []

    def blk(dz):
        return zat(dz) * NC + c

    def core_share(dz):
        at = blk(dz)
        pairs.append(go(table.at[at], table.at[at], device(dc=1)))

    for dz in (4, 3, -3, 2, -2, 1, -1):
        rings[dz] = go(table.at[mine], table.at[mine], device(dz=dz))
    core_share(0)

    square = jnp.sum(own * own, axis=1, keepdims=True)
    sq_own[0] = as_rows([square], pad)[0:1, :]
    sq_arrived = go_all(
        1, NX * NY,
        lambda j: (sq_own.at[0], sq_in.at[j], device(dx=lax.div(j, NY), dy=lax.rem(j, NY))),
    )

    arrived_z()
    total = info_z[0, 0:BLOCKS]
    for j in range(1, NZ):
        total = total + info_z[j, 0:BLOCKS]
    counts[...] = total

    keys_all = group[BLOCKS : BLOCKS + 8, :]
    keys = as_columns(jnp.where(c == 0, keys_all, pltpu.roll(keys_all, 6, 0)))
    cents = NX * cent_ref.shape[0]
    r = lax.broadcasted_iota(jnp.int32, (cents, LANE), 0)
    per = cent_ref.shape[0]
    r = z * (cents * NC) + lax.div(r, per) * (per * NC) + c * per + lax.rem(r, per)
    cent_key = r.astype(jnp.float32)
    spread_key = [jnp.broadcast_to(keys[0:ROWS, t : t + 1], (ROWS, LANE)) for t in range(2)]
    parts = [
        (0, cents, cent_key, 0), (cents, cents, cent_key, 1),
        (2 * cents, ROWS, spread_key[0], 0), (2 * cents + ROWS, ROWS, spread_key[1], 1),
    ]
    weight[...] = jnp.zeros_like(weight)
    for b in range(BLOCKS):
        many = counts[b : b + 1, :]
        for at, n, key, t in parts:
            line = BLOCKS + 2 * (b % NC) + t
            same = jnp.where(key == info_z[b // NC, line : line + 1, :], 1.0, 0.0)
            match[at : at + n, b * LANE : (b + 1) * LANE] = same.astype(jnp.bfloat16)
            weight[at : at + n, :] += same * many
    summed = jnp.sum(weight[...], axis=1, keepdims=True)
    weight[...] = jnp.broadcast_to(summed, weight.shape)
    first_row = 2 * cents
    wrows[...] = as_rows(
        [summed[first_row : first_row + ROWS], summed[first_row + ROWS : first_row + 2 * ROWS]], pad
    )

    sq_arrived()
    square_row = sq_own[0]
    for j in range(1, NX * NY):
        square_row = square_row + sq_in[j]
    inverse = lax.rsqrt(square_row / features + EPS)
    scale[mine] = inverse
    scale_arrived = go_all(
        1, NZ * NC,
        lambda j: (scale.at[mine], scale.at[mine], device(dz=lax.div(j, NC), dc=lax.rem(j, NC))),
    )
    means = own * as_columns(jnp.broadcast_to(inverse, (8, LANE)))[0:ROWS, 0:1]

    for dz in (-1, 1, -2, 2, -3, 3, 4):
        rings[dz].wait_recv()
        core_share(-dz)

    scale_arrived()
    for b in range(BLOCKS):
        scale2[b : b + 1, :] = scale[b]
    factor = as_columns(counts[...] * scale2[...])
    for pair in pairs:
        pair.wait_recv()
    scaled[...] = jnp.zeros_like(scaled)
    for b in range(BLOCKS):
        rows = table[b] * factor[0:ROWS, b : b + 1]
        for piece in range(3):
            near = rows.astype(jnp.bfloat16)
            scaled[b * LANE : b * LANE + ROWS, piece * LANE : (piece + 1) * LANE] = near
            rows = rows - near.astype(jnp.float32)
    tot = jnp.dot(match[...], scaled[...], preferred_element_type=jnp.float32)
    tot = tot[:, 0:LANE] + (tot[:, LANE : 2 * LANE] + tot[:, 2 * LANE : 3 * LANE])

    columns = []
    for t in range(2):
        at = first_row + t * ROWS
        many = weight[at : at + ROWS, :]
        g = tot[at : at + ROWS] * jnp.where(many > 0, 1.0 / jnp.maximum(many, 1.0), 0.0)
        d = means - g
        for v in (d * d, d * g, g * g):
            columns.append(jnp.sum(v, axis=1, keepdims=True))
    chosen = jnp.where(weight[cents : 2 * cents, :] > 0, tot[cents : 2 * cents], tot[0:cents])
    sel[...] = chosen
    squares = jnp.sum(chosen * chosen, axis=1, keepdims=True)
    columns.append(jnp.concatenate([squares, jnp.zeros((ROWS - cents, 1), jnp.float32)], 0))
    final_own[...] = as_rows(columns, pad)
    final_arrived = go_all(
        1, NX * NY,
        lambda j: (final_own, final_in.at[j], device(dx=lax.div(j, NY), dy=lax.rem(j, NY))),
    )
    sel_arrived = go_all(
        1, NX, lambda j: (sel.at[pl.ds(xat(j) * per, per)], sel_in.at[x], device(dx=j))
    )
    here = pl.ds(pl.multiple_of(x * per, per), per)
    sel_in[x] = sel[here, :]

    final_arrived()
    last_sum = final_own[...]
    for j in range(1, NX * NY):
        last_sum = last_sum + final_in[j]
    for t in range(2):
        far, mixed, length = (last_sum[3 * t + j : 3 * t + j + 1] for j in range(3))
        many = wrows[t : t + 1, :]
        s = many * lax.rsqrt(many * many * (length / features) + EPS) - 1.0
        value = (far - 2.0 * s * mixed + s * s * length) / features
        value = pltpu.roll(jnp.broadcast_to(value, (8, LANE)), LANE - x * OWN, 1)
        spread_ref[t : t + 1, :] = value[0:1, 0:OWN]
    lens[...] = as_columns(last_sum)
    length = lens[here, 6:7]
    inverse = lax.rsqrt(length / features + EPS)
    first = weight[here, :]
    second = weight[pl.ds(pl.multiple_of(x * per + cents, per), per), :]
    keep = jnp.maximum(first, second) > 0
    sel_arrived()
    for b in range(NX):
        at = slice(b * LANE, (b + 1) * LANE)
        cent_ref[:, at] = jnp.where(keep, sel_in[b] * inverse, init_ref[:, at])

    for wait in sent:
        wait()


COPIES = 7 + 7 + 4 + 21 + 7 + 7 + 8 + 15 + 15 + 15 + 3


def per_device(features, embeddings, sample_owner, lloyd_assign, init_centroids):
    samples, width = embeddings.shape
    per = init_centroids.shape[0]
    depth = 2048
    f32, bf16 = jnp.float32, jnp.bfloat16
    vm = pltpu.VMEM
    cents = NX * per
    lines = 2 * (cents + ROWS)
    scratch = [
        vm((1, samples), jnp.int32),
        vm((2, OWN), jnp.int32),
        vm((per, width), f32),
        vm((samples, width), bf16),
        vm((4, 2, NX, ROWS, LANE), f32),
        vm((4, 2, NX, ROWS, LANE), f32),
        vm((4, 2, NX, ROWS, LANE), f32),
        vm((4, 6, ROWS, LANE), f32),
        vm((NZ, ROWS, LANE), f32),
        vm((1, samples), jnp.int32),
        vm((8, LANE), f32),
        vm((24, LANE), f32),
        vm((NX * NC, 24, LANE), f32),
        vm((24, LANE), f32),
        vm((NZ, 24, LANE), f32),
        vm((BLOCKS, LANE), f32),
        vm((lines, BLOCKS * LANE), bf16),
        vm((lines, LANE), f32),
        vm((LANE, LANE), f32),
        vm((8, LANE), f32),
        vm((BLOCKS, ROWS, LANE), f32),
        vm((1, 1, LANE), f32),
        vm((NX * NY, 1, LANE), f32),
        vm((BLOCKS, 1, LANE), f32),
        vm((BLOCKS, LANE), f32),
        vm((BLOCKS * LANE, 3 * LANE), bf16),
        vm((8, LANE), f32),
        vm((NX * NY, 8, LANE), f32),
        vm((cents, LANE), f32),
        vm((NX, per, LANE), f32),
        vm((LANE, 8), f32),
        pltpu.SemaphoreType.DMA((samples // depth + 3,)),
        pltpu.SemaphoreType.DMA((COPIES,)),
        pltpu.SemaphoreType.DMA((COPIES,)),
    ]
    in_vmem = pl.BlockSpec(memory_space=pltpu.VMEM)

    def body(*refs):
        kernel(depth, width, features, *refs)

    return pl.pallas_call(
        body,
        name="recluster",
        out_shape=(
            jax.ShapeDtypeStruct((per, width), f32),
            jax.ShapeDtypeStruct((2, OWN), f32),
        ),
        in_specs=[pl.BlockSpec(memory_space=pl.ANY)] * 4,
        out_specs=(in_vmem, in_vmem),
        scratch_shapes=scratch,
        compiler_params=pltpu.CompilerParams(
            collective_id=0, has_side_effects=True, vmem_limit_bytes=60 << 20
        ),
    )(sample_owner.reshape(1, samples), lloyd_assign, init_centroids, embeddings)


def solution(mesh):
    def run(embeddings, sample_owner, lloyd_assign, init_centroids):
        features = embeddings.shape[1]
        return jax.shard_map(
            lambda *args: per_device(features, *args),
            mesh=mesh,
            in_specs=(P("dp", "feat"), P("dp"), P(None, "dp"), P("dp", "feat")),
            out_specs=(P("dp", "feat"), P(None, "dp")),
            check_vma=False,
        )(embeddings, sample_owner, lloyd_assign, init_centroids)

    return run
```

```python
import jax
import jax.numpy as jnp
from jax import lax
from jax.experimental import pallas as pl
from jax.experimental.pallas import tpu as pltpu
from jax.sharding import PartitionSpec as P

EPS = 1e-06
MESH = pl.DeviceIdType.MESH

NZ, NX, NC, NY = 8, 4, 2, 4
OWN = 24
ROWS = NX * OWN
BLOCKS = NZ * NC
LANE = 128
ORDER = (4, 3, -3, 2, -2, 1, -1, 0)


def position(owner):
    slab = lax.shift_right_logical(owner * 21846, 22)
    left = owner - slab * (NX * NC * OWN)
    column = lax.shift_right_logical(left * 1366, 16)
    inner = left - column * (NC * OWN)
    core = jnp.where(inner >= OWN, 1, 0)
    block = slab * NC + core
    return block, column * OWN + inner - core * OWN


def as_rows(columns, pad_ref):
    pad_ref[...] = jnp.zeros_like(pad_ref)
    lane = lax.broadcasted_iota(jnp.int32, (ROWS, LANE), 1)
    filled = jnp.zeros((ROWS, LANE), jnp.float32)
    for j, column in enumerate(columns):
        filled = jnp.where(lane == j, column, filled)
    pad_ref[0:ROWS, :] = filled
    return jnp.transpose(pad_ref[...])[0:8, :]


def as_columns(tile):
    return jnp.transpose(tile)


def kernel(
    depth, width, features,
    owner_hbm, assign_hbm, init_hbm, emb_hbm,
    cent_ref, spread_ref,
    owner_ref, assign_ref, init_ref,
    emb, part, other, other_in, xin, zin,
    prow, tile, info, info_x, group, info_z, counts, match, weight, pad, wrows,
    table, sq_own, sq_in, scale, scale2, scaled, final_own, final_in, sel, sel_in, lens,
    load_sem, send_sem, recv_sem,
):
    dp, y = lax.axis_index("dp"), lax.axis_index("feat")
    z, x, c = lax.div(dp, NX * NC), lax.rem(lax.div(dp, NC), NX), lax.rem(dp, NC)

    def zat(d):
        return lax.rem(z + d + NZ, NZ)

    def xat(d):
        return lax.rem(x + d + NX, NX)

    def device(dz=0, dx=0, dc=0, dy=0):
        return (zat(dz) * (NX * NC) + xat(dx) * NC + lax.rem(c + dc, NC), lax.rem(y + dy, NY))

    used = [0]
    sent = []

    def copy_at(slot, src, dst, to):
        return pltpu.make_async_remote_copy(
            src_ref=src, dst_ref=dst, send_sem=send_sem.at[slot], recv_sem=recv_sem.at[slot],
            device_id=to, device_id_type=MESH,
        )

    def go(src, dst, to):
        copy = copy_at(used[0], src, dst, to)
        used[0] += 1
        copy.start()
        sent.append(copy.wait_send)
        return copy

    def go_all(first, last, make):
        base = used[0]
        used[0] += last - first

        def at(j):
            src, dst, to = make(j)
            return copy_at(base + j - first, src, dst, to)

        def run(act):
            def step(j, carry):
                act(at(j))
                return carry
            lax.fori_loop(first, last, step, 0)

        run(lambda copy: copy.start())
        sent.append(lambda: run(lambda copy: copy.wait_send()))
        return lambda: run(lambda copy: copy.wait_recv())

    chunks = emb.shape[0] // depth
    loads = [
        pltpu.make_async_copy(
            emb_hbm.at[pl.ds(k * depth, depth)], emb.at[pl.ds(k * depth, depth)], load_sem.at[k]
        )
        for k in range(chunks)
    ]
    small = [
        pltpu.make_async_copy(src, dst, load_sem.at[chunks + k])
        for k, (src, dst) in enumerate(
            ((owner_hbm, owner_ref), (assign_hbm, assign_ref), (init_hbm, init_ref))
        )
    ]
    for load in small + loads:
        load.start()

    barrier = pltpu.get_barrier_semaphore()

    def greet(first, last, to):
        def step(j, carry):
            pl.semaphore_signal(barrier, inc=1, device_id=to(j), device_id_type=MESH)
            return carry
        lax.fori_loop(first, last, step, 0)

    greet(1, 8, lambda j: device(dx=lax.div(j, 2), dc=lax.rem(j, 2)))
    greet(0, 12, lambda j: device(dx=lax.div(j, 3), dy=lax.rem(j, 3) + 1))
    greet(2, 16, lambda j: device(dz=lax.div(j, 2), dc=lax.rem(j, 2)))

    tile[...] = jnp.zeros_like(tile)
    part[...] = jnp.zeros_like(part)
    other[...] = jnp.zeros_like(other)
    for load in small:
        load.wait()
    block, place = position(owner_ref[...])
    prow[...] = block * ROWS + place

    def count():
        samples = owner_ref.shape[1]
        block, place = position(owner_ref[...])
        high = lax.broadcasted_iota(jnp.int32, (BLOCKS, samples), 0) == block
        low = lax.broadcasted_iota(jnp.int32, (LANE, samples), 0) == place
        info[0:BLOCKS, :] = lax.dot_general(
            jnp.where(high, 1.0, 0.0).astype(jnp.bfloat16),
            jnp.where(low, 1.0, 0.0).astype(jnp.bfloat16),
            (((1,), (1,)), ((), ())), preferred_element_type=jnp.float32,
        )
        tile[0:2, 0:OWN] = assign_ref[...].astype(jnp.float32)
        placed = pltpu.roll(tile[...], x * OWN, 1)
        info[BLOCKS : BLOCKS + 8, :] = jnp.where(c == 0, placed, pltpu.roll(placed, 2, 0))
        info_x[0] = info[...]
        return go_all(
            1, 8, lambda j: (info, info_x.at[j], device(dx=lax.div(j, 2), dc=lax.rem(j, 2)))
        )

    def sums(bases, into, waits=()):
        row = lax.broadcasted_iota(jnp.int32, (ROWS, depth), 0)

        def step(k):
            at = pl.ds(pl.multiple_of(k * depth, depth), depth)
            p = prow[:, at]
            hot = jnp.concatenate(
                [jnp.where(row == p - base, 1.0, 0.0).astype(jnp.bfloat16) for base in bases], 0
            )
            got = jnp.dot(hot, emb[at, :], preferred_element_type=jnp.float32)
            for j, ref in enumerate(into):
                for b in range(NX):
                    ref[b] += got[j * ROWS : (j + 1) * ROWS, b * LANE : (b + 1) * LANE]

        if waits:
            for k in range(chunks):
                waits[k].wait()
                step(k)
        else:
            lax.fori_loop(0, chunks, lambda k, carry: (step(k), carry)[1], 0)

    cross = {}

    def work(s):
        base = zat(ORDER[s]) * (NC * ROWS)
        bases = [base + (1 - c) * ROWS, base + c * ROWS]
        sums(bases, [other.at[s], part.at[s]], loads if s == 0 else ())

    def give(s):
        cross[s] = go(other.at[s], other_in.at[s], device(dc=1))

    def meet(s):
        cross[s].wait_recv()
        part[s] += other_in[s]

    xs = {}

    def x_start(s):
        xs[s, 0] = go(part.at[s, xat(2)], xin.at[s, 0], device(dx=-1))
        xs[s, 1] = go(part.at[s, xat(1)], xin.at[s, 1], device(dx=1))

    def x_mid(s):
        xs[s, 0].wait_recv()
        part[s, xat(-1)] += xin[s, 0]
        xs[s, 2] = go(part.at[s, xat(-1)], xin.at[s, 2], device(dx=-1))

    def x_direct(s):
        for k, d in enumerate((2, 1, -1)):
            xs[s, k] = go(part.at[s, xat(d)], xin.at[s, k], device(dx=d))

    zs = {}
    hops = {4: 2, 3: 1, -3: -1}

    def x_end(s):
        d = ORDER[s]
        if (s, 0) in direct:
            xs[s, 0].wait_recv()
        xs[s, 1].wait_recv()
        xs[s, 2].wait_recv()
        total = part[s, x] + xin[s, 1] + xin[s, 2]
        if (s, 0) in direct:
            total = total + xin[s, 0]
        for far in {2: (4, 3), -2: (-3,)}.get(d, ()):
            zs[far].wait_recv()
            total = total + zin[ORDER.index(far)]
        part[s, x] = total
        if d != 0:
            zs[d] = go(part.at[s, x], zin.at[s], device(dz=hops.get(d, d)))

    direct = {(s, 0) for s in (0, 1, 6, 7)}

    work(0)
    work(1)
    pl.semaphore_wait(barrier, 7 + 12 + 14)
    give(0)
    give(1)
    arrived = count()

    work(2)
    give(2)
    meet(0)
    x_direct(0)
    meet(1)
    x_direct(1)
    work(3)
    give(3)
    meet(2)
    x_start(2)
    work(4)
    give(4)
    meet(3)
    x_start(3)
    arrived()
    whole = info_x[0]
    for j in range(1, NX * NC):
        whole = whole + info_x[j]
    group[...] = whole
    info_z[z] = whole
    arrived_z = go_all(1, NZ, lambda j: (group, info_z.at[z], device(dz=j)))
    work(5)
    give(5)
    meet(4)
    x_start(4)
    x_mid(2)
    x_end(0)
    work(6)
    give(6)
    meet(5)
    x_start(5)
    x_end(1)
    x_mid(3)
    work(7)
    give(7)
    meet(6)
    x_direct(6)
    x_mid(4)
    x_end(2)
    meet(7)
    x_direct(7)
    x_mid(5)
    x_end(3)
    x_end(4)
    x_end(6)
    x_end(5)
    x_end(7)
    own = part[7, x]
    for d in (2, -2, -1, 1):
        zs[d].wait_recv()
        own = own + zin[ORDER.index(d)]

    mine = z * NC + c
    table[mine] = own
    rings, pairs = {}, []

    def blk(dz):
        return zat(dz) * NC + c

    def core_share(dz):
        at = blk(dz)
        pairs.append(go(table.at[at], table.at[at], device(dc=1)))

    for dz in (4, 3, -3, 2, -2, 1, -1):
        rings[dz] = go(table.at[mine], table.at[mine], device(dz=dz))
    core_share(0)

    square = jnp.sum(own * own, axis=1, keepdims=True)
    sq_own[0] = as_rows([square], pad)[0:1, :]
    sq_arrived = go_all(
        1, NX * NY,
        lambda j: (sq_own.at[0], sq_in.at[j], device(dx=lax.div(j, NY), dy=lax.rem(j, NY))),
    )

    arrived_z()
    total = info_z[0, 0:BLOCKS]
    for j in range(1, NZ):
        total = total + info_z[j, 0:BLOCKS]
    counts[...] = total

    keys_all = group[BLOCKS : BLOCKS + 8, :]
    keys = as_columns(jnp.where(c == 0, keys_all, pltpu.roll(keys_all, 6, 0)))
    cents = NX * cent_ref.shape[0]
    r = lax.broadcasted_iota(jnp.int32, (cents, LANE), 0)
    per = cent_ref.shape[0]
    r = z * (cents * NC) + lax.div(r, per) * (per * NC) + c * per + lax.rem(r, per)
    cent_key = r.astype(jnp.float32)
    spread_key = [jnp.broadcast_to(keys[0:ROWS, t : t + 1], (ROWS, LANE)) for t in range(2)]
    parts = [
        (0, cents, cent_key, 0), (cents, cents, cent_key, 1),
        (2 * cents, ROWS, spread_key[0], 0), (2 * cents + ROWS, ROWS, spread_key[1], 1),
    ]
    weight[...] = jnp.zeros_like(weight)
    for b in range(BLOCKS):
        many = counts[b : b + 1, :]
        for at, n, key, t in parts:
            line = BLOCKS + 2 * (b % NC) + t
            same = jnp.where(key == info_z[b // NC, line : line + 1, :], 1.0, 0.0)
            match[at : at + n, b * LANE : (b + 1) * LANE] = same.astype(jnp.bfloat16)
            weight[at : at + n, :] += same * many
    summed = jnp.sum(weight[...], axis=1, keepdims=True)
    weight[...] = jnp.broadcast_to(summed, weight.shape)
    first_row = 2 * cents
    wrows[...] = as_rows(
        [summed[first_row : first_row + ROWS], summed[first_row + ROWS : first_row + 2 * ROWS]], pad
    )

    sq_arrived()
    square_row = sq_own[0]
    for j in range(1, NX * NY):
        square_row = square_row + sq_in[j]
    inverse = lax.rsqrt(square_row / features + EPS)
    scale[mine] = inverse
    scale_arrived = go_all(
        1, NZ * NC,
        lambda j: (scale.at[mine], scale.at[mine], device(dz=lax.div(j, NC), dc=lax.rem(j, NC))),
    )
    means = own * as_columns(jnp.broadcast_to(inverse, (8, LANE)))[0:ROWS, 0:1]

    for dz in (-1, 1, -2, 2, -3, 3, 4):
        rings[dz].wait_recv()
        core_share(-dz)

    scale_arrived()
    for b in range(BLOCKS):
        scale2[b : b + 1, :] = scale[b]
    factor = as_columns(counts[...] * scale2[...])
    for pair in pairs:
        pair.wait_recv()
    scaled[...] = jnp.zeros_like(scaled)
    for b in range(BLOCKS):
        rows = table[b] * factor[0:ROWS, b : b + 1]
        for piece in range(3):
            near = rows.astype(jnp.bfloat16)
            scaled[b * LANE : b * LANE + ROWS, piece * LANE : (piece + 1) * LANE] = near
            rows = rows - near.astype(jnp.float32)
    tot = jnp.dot(match[...], scaled[...], preferred_element_type=jnp.float32)
    tot = tot[:, 0:LANE] + (tot[:, LANE : 2 * LANE] + tot[:, 2 * LANE : 3 * LANE])

    columns = []
    for t in range(2):
        at = first_row + t * ROWS
        many = weight[at : at + ROWS, :]
        g = tot[at : at + ROWS] * jnp.where(many > 0, 1.0 / jnp.maximum(many, 1.0), 0.0)
        d = means - g
        for v in (d * d, d * g, g * g):
            columns.append(jnp.sum(v, axis=1, keepdims=True))
    chosen = jnp.where(weight[cents : 2 * cents, :] > 0, tot[cents : 2 * cents], tot[0:cents])
    sel[...] = chosen
    squares = jnp.sum(chosen * chosen, axis=1, keepdims=True)
    columns.append(jnp.concatenate([squares, jnp.zeros((ROWS - cents, 1), jnp.float32)], 0))
    final_own[...] = as_rows(columns, pad)
    final_arrived = go_all(
        1, NX * NY,
        lambda j: (final_own, final_in.at[j], device(dx=lax.div(j, NY), dy=lax.rem(j, NY))),
    )
    sel_arrived = go_all(
        1, NX, lambda j: (sel.at[pl.ds(xat(j) * per, per)], sel_in.at[x], device(dx=j))
    )
    here = pl.ds(pl.multiple_of(x * per, per), per)
    sel_in[x] = sel[here, :]

    final_arrived()
    last_sum = final_own[...]
    for j in range(1, NX * NY):
        last_sum = last_sum + final_in[j]
    for t in range(2):
        far, mixed, length = (last_sum[3 * t + j : 3 * t + j + 1] for j in range(3))
        many = wrows[t : t + 1, :]
        s = many * lax.rsqrt(many * many * (length / features) + EPS) - 1.0
        value = (far - 2.0 * s * mixed + s * s * length) / features
        value = pltpu.roll(jnp.broadcast_to(value, (8, LANE)), LANE - x * OWN, 1)
        spread_ref[t : t + 1, :] = value[0:1, 0:OWN]
    lens[...] = as_columns(last_sum)
    length = lens[here, 6:7]
    inverse = lax.rsqrt(length / features + EPS)
    first = weight[here, :]
    second = weight[pl.ds(pl.multiple_of(x * per + cents, per), per), :]
    keep = jnp.maximum(first, second) > 0
    sel_arrived()
    for b in range(NX):
        at = slice(b * LANE, (b + 1) * LANE)
        cent_ref[:, at] = jnp.where(keep, sel_in[b] * inverse, init_ref[:, at])

    for wait in sent:
        wait()


COPIES = 7 + 7 + 8 + 24 + 7 + 7 + 8 + 15 + 15 + 15 + 3


def per_device(features, embeddings, sample_owner, lloyd_assign, init_centroids):
    samples, width = embeddings.shape
    per = init_centroids.shape[0]
    depth = 2048
    f32, bf16 = jnp.float32, jnp.bfloat16
    vm = pltpu.VMEM
    cents = NX * per
    lines = 2 * (cents + ROWS)
    scratch = [
        vm((1, samples), jnp.int32),
        vm((2, OWN), jnp.int32),
        vm((per, width), f32),
        vm((samples, width), bf16),
        vm((NZ, NX, ROWS, LANE), f32),
        vm((NZ, NX, ROWS, LANE), f32),
        vm((NZ, NX, ROWS, LANE), f32),
        vm((NZ, 3, ROWS, LANE), f32),
        vm((NZ, ROWS, LANE), f32),
        vm((1, samples), jnp.int32),
        vm((8, LANE), f32),
        vm((24, LANE), f32),
        vm((NX * NC, 24, LANE), f32),
        vm((24, LANE), f32),
        vm((NZ, 24, LANE), f32),
        vm((BLOCKS, LANE), f32),
        vm((lines, BLOCKS * LANE), bf16),
        vm((lines, LANE), f32),
        vm((LANE, LANE), f32),
        vm((8, LANE), f32),
        vm((BLOCKS, ROWS, LANE), f32),
        vm((1, 1, LANE), f32),
        vm((NX * NY, 1, LANE), f32),
        vm((BLOCKS, 1, LANE), f32),
        vm((BLOCKS, LANE), f32),
        vm((BLOCKS * LANE, 3 * LANE), bf16),
        vm((8, LANE), f32),
        vm((NX * NY, 8, LANE), f32),
        vm((cents, LANE), f32),
        vm((NX, per, LANE), f32),
        vm((LANE, 8), f32),
        pltpu.SemaphoreType.DMA((samples // depth + 3,)),
        pltpu.SemaphoreType.DMA((COPIES,)),
        pltpu.SemaphoreType.DMA((COPIES,)),
    ]
    in_vmem = pl.BlockSpec(memory_space=pltpu.VMEM)

    def body(*refs):
        kernel(depth, width, features, *refs)

    return pl.pallas_call(
        body,
        name="recluster",
        out_shape=(
            jax.ShapeDtypeStruct((per, width), f32),
            jax.ShapeDtypeStruct((2, OWN), f32),
        ),
        in_specs=[pl.BlockSpec(memory_space=pl.ANY)] * 4,
        out_specs=(in_vmem, in_vmem),
        scratch_shapes=scratch,
        compiler_params=pltpu.CompilerParams(
            collective_id=0, has_side_effects=True, vmem_limit_bytes=60 << 20
        ),
    )(sample_owner.reshape(1, samples), lloyd_assign, init_centroids, embeddings)


def solution(mesh):
    def run(embeddings, sample_owner, lloyd_assign, init_centroids):
        features = embeddings.shape[1]
        return jax.shard_map(
            lambda *args: per_device(features, *args),
            mesh=mesh,
            in_specs=(P("dp", "feat"), P("dp"), P(None, "dp"), P("dp", "feat")),
            out_specs=(P("dp", "feat"), P(None, "dp")),
            check_vma=False,
        )(embeddings, sample_owner, lloyd_assign, init_centroids)

    return run
```

```python
import jax
import jax.numpy as jnp
from jax import lax
from jax.experimental import pallas as pl
from jax.experimental.pallas import tpu as pltpu
from jax.sharding import PartitionSpec as P

EPS = 1e-06
MESH = pl.DeviceIdType.MESH

NZ, NX, NC, NY = 8, 4, 2, 4
OWN = 24
ROWS = NX * OWN
BLOCKS = NZ * NC
LANE = 128
ORDER = (4, 3, -3, 1, -1, 2, -2, 0)


def position(owner):
    slab = lax.shift_right_logical(owner * 21846, 22)
    left = owner - slab * (NX * NC * OWN)
    column = lax.shift_right_logical(left * 1366, 16)
    inner = left - column * (NC * OWN)
    core = jnp.where(inner >= OWN, 1, 0)
    block = slab * NC + core
    return block, column * OWN + inner - core * OWN


def as_rows(columns, pad_ref):
    pad_ref[...] = jnp.zeros_like(pad_ref)
    lane = lax.broadcasted_iota(jnp.int32, (ROWS, LANE), 1)
    filled = jnp.zeros((ROWS, LANE), jnp.float32)
    for j, column in enumerate(columns):
        filled = jnp.where(lane == j, column, filled)
    pad_ref[0:ROWS, :] = filled
    return jnp.transpose(pad_ref[...])[0:8, :]


def as_columns(tile):
    return jnp.transpose(tile)


def kernel(
    depth, width, features,
    owner_hbm, assign_hbm, init_hbm, emb_hbm,
    cent_ref, spread_ref,
    owner_ref, assign_ref, init_ref,
    emb, part, other, other_in, xin, zslab, zin,
    prow, tile, info, info_x, group, info_z, counts, match, weight, pad, wrows,
    table, sq_own, sq_in, scale, scale2, scaled, final_own, final_in, sel, sel_in, lens,
    load_sem, send_sem, recv_sem,
):
    dp, y = lax.axis_index("dp"), lax.axis_index("feat")
    z, x, c = lax.div(dp, NX * NC), lax.rem(lax.div(dp, NC), NX), lax.rem(dp, NC)

    def zat(d):
        return lax.rem(z + d + NZ, NZ)

    def xat(d):
        return lax.rem(x + d + NX, NX)

    def device(dz=0, dx=0, dc=0, dy=0):
        return (zat(dz) * (NX * NC) + xat(dx) * NC + lax.rem(c + dc, NC), lax.rem(y + dy, NY))

    used = [0]
    sent = []

    def copy_at(slot, src, dst, to):
        return pltpu.make_async_remote_copy(
            src_ref=src, dst_ref=dst, send_sem=send_sem.at[slot], recv_sem=recv_sem.at[slot],
            device_id=to, device_id_type=MESH,
        )

    def go(src, dst, to):
        copy = copy_at(used[0], src, dst, to)
        used[0] += 1
        copy.start()
        sent.append(copy.wait_send)
        return copy

    def go_all(first, last, make):
        base = used[0]
        used[0] += last - first

        def at(j):
            src, dst, to = make(j)
            return copy_at(base + j - first, src, dst, to)

        def run(act):
            def step(j, carry):
                act(at(j))
                return carry
            lax.fori_loop(first, last, step, 0)

        run(lambda copy: copy.start())
        sent.append(lambda: run(lambda copy: copy.wait_send()))
        return lambda: run(lambda copy: copy.wait_recv())

    chunks = emb.shape[0] // depth
    loads = [
        pltpu.make_async_copy(
            emb_hbm.at[pl.ds(k * depth, depth)], emb.at[pl.ds(k * depth, depth)], load_sem.at[k]
        )
        for k in range(chunks)
    ]
    small = [
        pltpu.make_async_copy(src, dst, load_sem.at[chunks + k])
        for k, (src, dst) in enumerate(
            ((owner_hbm, owner_ref), (assign_hbm, assign_ref), (init_hbm, init_ref))
        )
    ]
    for load in small + loads:
        load.start()

    barrier = pltpu.get_barrier_semaphore()

    def greet(first, last, to):
        def step(j, carry):
            pl.semaphore_signal(barrier, inc=1, device_id=to(j), device_id_type=MESH)
            return carry
        lax.fori_loop(first, last, step, 0)

    greet(1, 8, lambda j: device(dx=lax.div(j, 2), dc=lax.rem(j, 2)))
    greet(0, 12, lambda j: device(dx=lax.div(j, 3), dy=lax.rem(j, 3) + 1))
    greet(2, 16, lambda j: device(dz=lax.div(j, 2), dc=lax.rem(j, 2)))

    tile[...] = jnp.zeros_like(tile)
    part[...] = jnp.zeros_like(part)
    other[...] = jnp.zeros_like(other)
    for load in small:
        load.wait()
    block, place = position(owner_ref[...])
    prow[...] = block * ROWS + place

    def count():
        samples = owner_ref.shape[1]
        block, place = position(owner_ref[...])
        high = lax.broadcasted_iota(jnp.int32, (BLOCKS, samples), 0) == block
        low = lax.broadcasted_iota(jnp.int32, (LANE, samples), 0) == place
        info[0:BLOCKS, :] = lax.dot_general(
            jnp.where(high, 1.0, 0.0).astype(jnp.bfloat16),
            jnp.where(low, 1.0, 0.0).astype(jnp.bfloat16),
            (((1,), (1,)), ((), ())), preferred_element_type=jnp.float32,
        )
        tile[0:2, 0:OWN] = assign_ref[...].astype(jnp.float32)
        placed = pltpu.roll(tile[...], x * OWN, 1)
        info[BLOCKS : BLOCKS + 8, :] = jnp.where(c == 0, placed, pltpu.roll(placed, 2, 0))
        info_x[0] = info[...]
        return go_all(
            1, 8, lambda j: (info, info_x.at[j], device(dx=lax.div(j, 2), dc=lax.rem(j, 2)))
        )

    def sums(bases, into, waits=()):
        row = lax.broadcasted_iota(jnp.int32, (ROWS, depth), 0)

        def step(k):
            at = pl.ds(pl.multiple_of(k * depth, depth), depth)
            p = prow[:, at]
            hot = jnp.concatenate(
                [jnp.where(row == p - base, 1.0, 0.0).astype(jnp.bfloat16) for base in bases], 0
            )
            got = jnp.dot(hot, emb[at, :], preferred_element_type=jnp.float32)
            for j, ref in enumerate(into):
                for b in range(NX):
                    ref[b] += got[j * ROWS : (j + 1) * ROWS, b * LANE : (b + 1) * LANE]

        if waits:
            for k in range(chunks):
                waits[k].wait()
                step(k)
        else:
            lax.fori_loop(0, chunks, lambda k, carry: (step(k), carry)[1], 0)

    cross = {}

    def work(s):
        base = zat(ORDER[s]) * (NC * ROWS)
        bases = [base + (1 - c) * ROWS, base + c * ROWS]
        sums(bases, [other.at[s], part.at[s]], loads if s == 0 else ())

    def give(s):
        cross[s] = go(other.at[s], other_in.at[s], device(dc=1))

    def meet(s):
        cross[s].wait_recv()
        part[s] += other_in[s]

    xs = {}

    def x_start(s):
        xs[s, 0] = go(part.at[s, xat(2)], xin.at[s, 0], device(dx=-1))
        xs[s, 1] = go(part.at[s, xat(1)], xin.at[s, 1], device(dx=1))

    def x_mid(s):
        xs[s, 0].wait_recv()
        part[s, xat(-1)] += xin[s, 0]
        xs[s, 2] = go(part.at[s, xat(-1)], xin.at[s, 2], device(dx=-1))

    def x_direct(s):
        for k, d in enumerate((2, 1, -1)):
            xs[s, k] = go(part.at[s, xat(d)], xin.at[s, k], device(dx=d))

    zs = {}
    hops = {4: 2, 3: 1, -3: -1}

    def x_end(s):
        d = ORDER[s]
        if (s, 0) in direct:
            xs[s, 0].wait_recv()
        xs[s, 1].wait_recv()
        xs[s, 2].wait_recv()
        total = part[s, x] + xin[s, 1] + xin[s, 2]
        if (s, 0) in direct:
            total = total + xin[s, 0]
        for far in {2: (4, 3), -2: (-3,)}.get(d, ()):
            zs[far].wait_recv()
            total = total + zin[ORDER.index(far)]
        part[s, x] = total
        if d != 0:
            zs[d] = go(part.at[s, x], zin.at[s], device(dz=hops.get(d, d)))

    direct = {(s, 0) for s in (6, 7)}

    work(0)
    work(1)
    pl.semaphore_wait(barrier, 7 + 12 + 14)
    give(0)
    give(1)
    arrived = count()

    whole_slab = {}

    def z_whole(s):
        d = ORDER[s]
        whole_slab[s] = go(part.at[s], zslab.at[s - 3], device(dz=d))

    work(2)
    give(2)
    meet(0)
    x_start(0)
    meet(1)
    x_start(1)
    work(3)
    give(3)
    meet(2)
    x_start(2)
    work(4)
    give(4)
    meet(3)
    z_whole(3)
    arrived()
    whole = info_x[0]
    for j in range(1, NX * NC):
        whole = whole + info_x[j]
    group[...] = whole
    info_z[z] = whole
    arrived_z = go_all(1, NZ, lambda j: (group, info_z.at[z], device(dz=j)))
    work(5)
    give(5)
    meet(4)
    z_whole(4)
    x_mid(0)
    x_mid(1)
    work(6)
    give(6)
    meet(5)
    x_start(5)
    x_mid(2)
    work(7)
    give(7)
    meet(6)
    x_direct(6)
    x_end(0)
    x_end(1)
    cross[7].wait_recv()
    whole_slab[3].wait_recv()
    whole_slab[4].wait_recv()
    part[7] += other_in[7] + zslab[0] + zslab[1]
    x_direct(7)
    x_mid(5)
    x_end(2)
    x_end(6)
    x_end(5)
    x_end(7)
    own = part[7, x]
    for d in (2, -2):
        zs[d].wait_recv()
        own = own + zin[ORDER.index(d)]

    mine = z * NC + c
    table[mine] = own
    rings, pairs = {}, []

    def blk(dz):
        return zat(dz) * NC + c

    def core_share(dz):
        at = blk(dz)
        pairs.append(go(table.at[at], table.at[at], device(dc=1)))

    for dz in (2, -2, 1, -1):
        rings[dz] = go(table.at[mine], table.at[mine], device(dz=dz))
    core_share(0)

    square = jnp.sum(own * own, axis=1, keepdims=True)
    sq_own[0] = as_rows([square], pad)[0:1, :]
    sq_arrived = go_all(
        1, NX * NY,
        lambda j: (sq_own.at[0], sq_in.at[j], device(dx=lax.div(j, NY), dy=lax.rem(j, NY))),
    )

    arrived_z()
    total = info_z[0, 0:BLOCKS]
    for j in range(1, NZ):
        total = total + info_z[j, 0:BLOCKS]
    counts[...] = total

    half = ROWS // 2
    for way in (1, -1):
        rings[2 * way].wait_recv()
        at = blk(-2 * way)
        rings[3 * way] = go(table.at[at], table.at[at], device(dz=way))
        rows = pl.ds(0 if way > 0 else half, half)
        rings[4 * way] = go(table.at[at, rows], table.at[at, rows], device(dz=2 * way))
        core_share(-2 * way)
    for way in (1, -1):
        rings[way].wait_recv()
        core_share(-way)

    keys_all = group[BLOCKS : BLOCKS + 8, :]
    keys = as_columns(jnp.where(c == 0, keys_all, pltpu.roll(keys_all, 6, 0)))
    cents = NX * cent_ref.shape[0]
    r = lax.broadcasted_iota(jnp.int32, (cents, LANE), 0)
    per = cent_ref.shape[0]
    r = z * (cents * NC) + lax.div(r, per) * (per * NC) + c * per + lax.rem(r, per)
    cent_key = r.astype(jnp.float32)
    spread_key = [jnp.broadcast_to(keys[0:ROWS, t : t + 1], (ROWS, LANE)) for t in range(2)]
    parts = [
        (0, cents, cent_key, 0), (cents, cents, cent_key, 1),
        (2 * cents, ROWS, spread_key[0], 0), (2 * cents + ROWS, ROWS, spread_key[1], 1),
    ]
    weight[...] = jnp.zeros_like(weight)
    for b in range(BLOCKS):
        many = counts[b : b + 1, :]
        for at, n, key, t in parts:
            line = BLOCKS + 2 * (b % NC) + t
            same = jnp.where(key == info_z[b // NC, line : line + 1, :], 1.0, 0.0)
            match[at : at + n, b * LANE : (b + 1) * LANE] = same.astype(jnp.bfloat16)
            weight[at : at + n, :] += same * many
    summed = jnp.sum(weight[...], axis=1, keepdims=True)
    weight[...] = jnp.broadcast_to(summed, weight.shape)
    first_row = 2 * cents
    wrows[...] = as_rows(
        [summed[first_row : first_row + ROWS], summed[first_row + ROWS : first_row + 2 * ROWS]], pad
    )

    sq_arrived()
    square_row = sq_own[0]
    for j in range(1, NX * NY):
        square_row = square_row + sq_in[j]
    inverse = lax.rsqrt(square_row / features + EPS)
    scale[mine] = inverse
    scale_arrived = go_all(
        1, NZ * NC,
        lambda j: (scale.at[mine], scale.at[mine], device(dz=lax.div(j, NC), dc=lax.rem(j, NC))),
    )
    means = own * as_columns(jnp.broadcast_to(inverse, (8, LANE)))[0:ROWS, 0:1]

    for way in (1, -1):
        rings[3 * way].wait_recv()
        core_share(-3 * way)
    rings[4].wait_recv()
    rings[-4].wait_recv()
    core_share(4)

    scale_arrived()
    for b in range(BLOCKS):
        scale2[b : b + 1, :] = scale[b]
    factor = as_columns(counts[...] * scale2[...])
    for pair in pairs:
        pair.wait_recv()
    scaled[...] = jnp.zeros_like(scaled)
    for b in range(BLOCKS):
        rows = table[b] * factor[0:ROWS, b : b + 1]
        for piece in range(3):
            near = rows.astype(jnp.bfloat16)
            scaled[b * LANE : b * LANE + ROWS, piece * LANE : (piece + 1) * LANE] = near
            rows = rows - near.astype(jnp.float32)
    tot = jnp.dot(match[...], scaled[...], preferred_element_type=jnp.float32)
    tot = tot[:, 0:LANE] + (tot[:, LANE : 2 * LANE] + tot[:, 2 * LANE : 3 * LANE])

    columns = []
    for t in range(2):
        at = first_row + t * ROWS
        many = weight[at : at + ROWS, :]
        g = tot[at : at + ROWS] * jnp.where(many > 0, 1.0 / jnp.maximum(many, 1.0), 0.0)
        d = means - g
        for v in (d * d, d * g, g * g):
            columns.append(jnp.sum(v, axis=1, keepdims=True))
    chosen = jnp.where(weight[cents : 2 * cents, :] > 0, tot[cents : 2 * cents], tot[0:cents])
    sel[...] = chosen
    squares = jnp.sum(chosen * chosen, axis=1, keepdims=True)
    columns.append(jnp.concatenate([squares, jnp.zeros((ROWS - cents, 1), jnp.float32)], 0))
    final_own[...] = as_rows(columns, pad)
    final_arrived = go_all(
        1, NX * NY,
        lambda j: (final_own, final_in.at[j], device(dx=lax.div(j, NY), dy=lax.rem(j, NY))),
    )
    sel_arrived = go_all(
        1, NX, lambda j: (sel.at[pl.ds(xat(j) * per, per)], sel_in.at[x], device(dx=j))
    )
    here = pl.ds(pl.multiple_of(x * per, per), per)
    sel_in[x] = sel[here, :]

    final_arrived()
    last_sum = final_own[...]
    for j in range(1, NX * NY):
        last_sum = last_sum + final_in[j]
    for t in range(2):
        far, mixed, length = (last_sum[3 * t + j : 3 * t + j + 1] for j in range(3))
        many = wrows[t : t + 1, :]
        s = many * lax.rsqrt(many * many * (length / features) + EPS) - 1.0
        value = (far - 2.0 * s * mixed + s * s * length) / features
        value = pltpu.roll(jnp.broadcast_to(value, (8, LANE)), LANE - x * OWN, 1)
        spread_ref[t : t + 1, :] = value[0:1, 0:OWN]
    lens[...] = as_columns(last_sum)
    length = lens[here, 6:7]
    inverse = lax.rsqrt(length / features + EPS)
    first = weight[here, :]
    second = weight[pl.ds(pl.multiple_of(x * per + cents, per), per), :]
    keep = jnp.maximum(first, second) > 0
    sel_arrived()
    for b in range(NX):
        at = slice(b * LANE, (b + 1) * LANE)
        cent_ref[:, at] = jnp.where(keep, sel_in[b] * inverse, init_ref[:, at])

    for wait in sent:
        wait()


COPIES = 7 + 7 + 8 + 18 + 2 + 5 + 8 + 8 + 15 + 15 + 15 + 3


def per_device(features, embeddings, sample_owner, lloyd_assign, init_centroids):
    samples, width = embeddings.shape
    per = init_centroids.shape[0]
    depth = 2048
    f32, bf16 = jnp.float32, jnp.bfloat16
    vm = pltpu.VMEM
    cents = NX * per
    lines = 2 * (cents + ROWS)
    scratch = [
        vm((1, samples), jnp.int32),
        vm((2, OWN), jnp.int32),
        vm((per, width), f32),
        vm((samples, width), bf16),
        vm((NZ, NX, ROWS, LANE), f32),
        vm((NZ, NX, ROWS, LANE), f32),
        vm((NZ, NX, ROWS, LANE), f32),
        vm((NZ, 3, ROWS, LANE), f32),
        vm((2, NX, ROWS, LANE), f32),
        vm((NZ, ROWS, LANE), f32),
        vm((1, samples), jnp.int32),
        vm((8, LANE), f32),
        vm((24, LANE), f32),
        vm((NX * NC, 24, LANE), f32),
        vm((24, LANE), f32),
        vm((NZ, 24, LANE), f32),
        vm((BLOCKS, LANE), f32),
        vm((lines, BLOCKS * LANE), bf16),
        vm((lines, LANE), f32),
        vm((LANE, LANE), f32),
        vm((8, LANE), f32),
        vm((BLOCKS, ROWS, LANE), f32),
        vm((1, 1, LANE), f32),
        vm((NX * NY, 1, LANE), f32),
        vm((BLOCKS, 1, LANE), f32),
        vm((BLOCKS, LANE), f32),
        vm((BLOCKS * LANE, 3 * LANE), bf16),
        vm((8, LANE), f32),
        vm((NX * NY, 8, LANE), f32),
        vm((cents, LANE), f32),
        vm((NX, per, LANE), f32),
        vm((LANE, 8), f32),
        pltpu.SemaphoreType.DMA((samples // depth + 3,)),
        pltpu.SemaphoreType.DMA((COPIES,)),
        pltpu.SemaphoreType.DMA((COPIES,)),
    ]
    in_vmem = pl.BlockSpec(memory_space=pltpu.VMEM)

    def body(*refs):
        kernel(depth, width, features, *refs)

    packed = pl.pallas_call(
        body,
        name="recluster",
        out_shape=(
            jax.ShapeDtypeStruct((per, width), f32),
            jax.ShapeDtypeStruct((2, OWN), f32),
        ),
        in_specs=[pl.BlockSpec(memory_space=pl.ANY)] * 4,
        out_specs=(in_vmem, in_vmem),
        scratch_shapes=scratch,
        compiler_params=pltpu.CompilerParams(
            collective_id=0, has_side_effects=True, vmem_limit_bytes=60 << 20
        ),
    )(sample_owner.reshape(1, samples), lloyd_assign, init_centroids, embeddings)

    def hand_out(cent_in, spread_in, cent_out, spread_out, sem):
        copies = [
            pltpu.make_async_copy(cent_in, cent_out, sem.at[0]),
            pltpu.make_async_copy(spread_in, spread_out, sem.at[1]),
        ]
        for copy in copies:
            copy.start()
        for copy in copies:
            copy.wait()

    anywhere = pl.BlockSpec(memory_space=pl.ANY)
    return pl.pallas_call(
        hand_out,
        name="hand_out",
        out_shape=(
            jax.ShapeDtypeStruct((per, width), f32),
            jax.ShapeDtypeStruct((2, OWN), f32),
        ),
        in_specs=[anywhere] * 2,
        out_specs=(anywhere, anywhere),
        scratch_shapes=[pltpu.SemaphoreType.DMA((2,))],
    )(*packed)


def solution(mesh):
    def run(embeddings, sample_owner, lloyd_assign, init_centroids):
        features = embeddings.shape[1]
        return jax.shard_map(
            lambda *args: per_device(features, *args),
            mesh=mesh,
            in_specs=(P("dp", "feat"), P("dp"), P(None, "dp"), P("dp", "feat")),
            out_specs=(P("dp", "feat"), P(None, "dp")),
            check_vma=False,
        )(embeddings, sample_owner, lloyd_assign, init_centroids)

    return run
```

```python
import jax
import jax.numpy as jnp
from jax import lax
from jax.experimental import pallas as pl
from jax.experimental.pallas import tpu as pltpu
from jax.sharding import PartitionSpec as P

EPS = 1e-06
MESH = pl.DeviceIdType.MESH

NZ, NX, NC, NY = 8, 4, 2, 4
OWN = 24
ROWS = NX * OWN
BLOCKS = NZ * NC
LANE = 128
ORDER = (4, 3, -3, 1, -1, 2, -2, 0)


def position(owner):
    slab = lax.shift_right_logical(owner * 21846, 22)
    left = owner - slab * (NX * NC * OWN)
    column = lax.shift_right_logical(left * 1366, 16)
    inner = left - column * (NC * OWN)
    core = jnp.where(inner >= OWN, 1, 0)
    block = slab * NC + core
    return block, column * OWN + inner - core * OWN


def as_rows(columns, pad_ref):
    pad_ref[...] = jnp.zeros_like(pad_ref)
    lane = lax.broadcasted_iota(jnp.int32, (ROWS, LANE), 1)
    filled = jnp.zeros((ROWS, LANE), jnp.float32)
    for j, column in enumerate(columns):
        filled = jnp.where(lane == j, column, filled)
    pad_ref[0:ROWS, :] = filled
    return jnp.transpose(pad_ref[...])[0:8, :]


def as_columns(tile):
    return jnp.transpose(tile)


def kernel(
    depth, width, features,
    owner_hbm, assign_hbm, init_hbm, emb_hbm,
    cent_ref, spread_ref,
    owner_ref, assign_ref, init_ref,
    emb, part, other, other_in, xin, zslab, zin,
    prow, tile, info, info_x, group, info_z, counts, match, weight, pad, wrows,
    table, sq_own, sq_in, scale, scale2, scaled, final_own, final_in, sel, sel_in, lens,
    load_sem, send_sem, recv_sem,
):
    dp, y = lax.axis_index("dp"), lax.axis_index("feat")
    z = lax.div(dp, NX * NC)
    x = lax.div(dp - z * (NX * NC), NC)
    c = dp - z * (NX * NC) - x * NC

    def around(at, size):
        steps = [at]
        for d in range(1, size):
            steps.append(jnp.where(at + d >= size, at + (d - size), at + d))
        return steps

    z_at, x_at, c_at, y_at = around(z, NZ), around(x, NX), around(c, NC), around(y, NY)
    z_first = [at * (NX * NC) for at in z_at]
    x_first = [at * NC for at in x_at]

    def zat(d):
        return z_at[d % NZ]

    def xat(d):
        return x_at[d % NX]

    def device(dz=0, dx=0, dc=0, dy=0):
        return (z_first[dz % NZ] + (x_first[dx % NX] + c_at[dc % NC]), y_at[dy % NY])

    used = [0]
    sent = []

    def go(src, dst, to):
        slot = used[0]
        used[0] += 1
        copy = pltpu.make_async_remote_copy(
            src_ref=src, dst_ref=dst, send_sem=send_sem.at[slot], recv_sem=recv_sem.at[slot],
            device_id=to, device_id_type=MESH,
        )
        copy.start()
        sent.append(copy.wait_send)
        return copy

    def go_all(makes):
        copies = [go(*make) for make in makes]

        def wait():
            for copy in copies:
                copy.wait_recv()

        return wait

    group_xc = [(dx, dc) for dx in (2, 1, 3, 0) for dc in range(NC) if (dx, dc) != (0, 0)]
    group_xy = [
        (dx, dy) for dx in (2, 1, 3, 0) for dy in (2, 1, 3, 0) if (dx, dy) != (0, 0)
    ]
    group_zc = [
        (dz, dc) for dz in (4, 3, 5, 2, 6, 1, 7, 0) for dc in range(NC) if (dz, dc) != (0, 0)
    ]

    chunks = emb.shape[0] // depth
    loads = [
        pltpu.make_async_copy(
            emb_hbm.at[pl.ds(k * depth, depth)], emb.at[pl.ds(k * depth, depth)], load_sem.at[k]
        )
        for k in range(chunks)
    ]
    small = [
        pltpu.make_async_copy(src, dst, load_sem.at[chunks + k])
        for k, (src, dst) in enumerate(
            ((owner_hbm, owner_ref), (assign_hbm, assign_ref), (init_hbm, init_ref))
        )
    ]
    for load in small + loads:
        load.start()

    barrier = pltpu.get_barrier_semaphore()

    greeted = {(dz, 0, dc, 0) for dz, dc in group_zc}
    greeted |= {(0, dx, 0, dy) for dx, dy in group_xy} | {(0, dx, dc, 0) for dx, dc in group_xc}
    for steps in sorted(greeted, key=lambda v: (-sum(min(a, b - a) for a, b in zip(v, (NZ, NX, NC, NY))), v)):
        pl.semaphore_signal(barrier, inc=1, device_id=device(*steps), device_id_type=MESH)

    tile[...] = jnp.zeros_like(tile)
    part[...] = jnp.zeros_like(part)
    other[...] = jnp.zeros_like(other)
    for load in small:
        load.wait()
    block, place = position(owner_ref[...])
    prow[...] = block * ROWS + place

    def count():
        samples = owner_ref.shape[1]
        block, place = position(owner_ref[...])
        high = lax.broadcasted_iota(jnp.int32, (BLOCKS, samples), 0) == block
        low = lax.broadcasted_iota(jnp.int32, (LANE, samples), 0) == place
        info[0:BLOCKS, :] = lax.dot_general(
            jnp.where(high, 1.0, 0.0).astype(jnp.bfloat16),
            jnp.where(low, 1.0, 0.0).astype(jnp.bfloat16),
            (((1,), (1,)), ((), ())), preferred_element_type=jnp.float32,
        )
        tile[0:2, 0:OWN] = assign_ref[...].astype(jnp.float32)
        placed = pltpu.roll(tile[...], x * OWN, 1)
        info[BLOCKS : BLOCKS + 8, :] = jnp.where(c == 0, placed, pltpu.roll(placed, 2, 0))
        info_x[0] = info[...]
        return go_all(
            (info, info_x.at[dx * NC + dc], device(dx=dx, dc=dc)) for dx, dc in group_xc
        )

    def sums(bases, into, waits=()):
        row = lax.broadcasted_iota(jnp.int32, (ROWS, depth), 0)

        def step(k):
            at = pl.ds(pl.multiple_of(k * depth, depth), depth)
            p = prow[:, at]
            hot = jnp.concatenate(
                [jnp.where(row == p - base, 1.0, 0.0).astype(jnp.bfloat16) for base in bases], 0
            )
            got = jnp.dot(hot, emb[at, :], preferred_element_type=jnp.float32)
            for j, ref in enumerate(into):
                for b in range(NX):
                    ref[b] += got[j * ROWS : (j + 1) * ROWS, b * LANE : (b + 1) * LANE]

        if waits:
            for k in range(chunks):
                waits[k].wait()
                step(k)
        else:
            lax.fori_loop(0, chunks, lambda k, carry: (step(k), carry)[1], 0)

    cross = {}

    def work(s):
        base = zat(ORDER[s]) * (NC * ROWS)
        bases = [base + (1 - c) * ROWS, base + c * ROWS]
        sums(bases, [other.at[s], part.at[s]], loads if s == 0 else ())

    def give(s):
        cross[s] = go(other.at[s], other_in.at[s], device(dc=1))

    def meet(s):
        cross[s].wait_recv()
        part[s] += other_in[s]

    xs = {}

    def x_start(s):
        xs[s, 0] = go(part.at[s, xat(2)], xin.at[s, 0], device(dx=-1))
        xs[s, 1] = go(part.at[s, xat(1)], xin.at[s, 1], device(dx=1))

    def x_mid(s):
        xs[s, 0].wait_recv()
        part[s, xat(-1)] += xin[s, 0]
        xs[s, 2] = go(part.at[s, xat(-1)], xin.at[s, 2], device(dx=-1))

    def x_direct(s):
        for k, d in enumerate((2, 1, -1)):
            xs[s, k] = go(part.at[s, xat(d)], xin.at[s, k], device(dx=d))

    zs = {}
    hops = {4: 2, 3: 1, -3: -1}

    def x_end(s):
        d = ORDER[s]
        if (s, 0) in direct:
            xs[s, 0].wait_recv()
        xs[s, 1].wait_recv()
        xs[s, 2].wait_recv()
        total = part[s, x] + xin[s, 1] + xin[s, 2]
        if (s, 0) in direct:
            total = total + xin[s, 0]
        for far in {2: (4, 3), -2: (-3,)}.get(d, ()):
            zs[far].wait_recv()
            total = total + zin[ORDER.index(far)]
        part[s, x] = total
        if d != 0:
            zs[d] = go(part.at[s, x], zin.at[s], device(dz=hops.get(d, d)))

    direct = {(s, 0) for s in (6, 7)}

    work(0)
    work(1)
    pl.semaphore_wait(barrier, len(greeted))
    give(0)
    give(1)
    arrived = count()

    whole_slab = {}

    def z_whole(s):
        d = ORDER[s]
        whole_slab[s] = go(part.at[s], zslab.at[s - 3], device(dz=d))

    work(2)
    give(2)
    meet(0)
    x_start(0)
    meet(1)
    x_start(1)
    work(3)
    give(3)
    meet(2)
    x_start(2)
    work(4)
    give(4)
    meet(3)
    z_whole(3)
    arrived()
    whole = info_x[0]
    for j in range(1, NX * NC):
        whole = whole + info_x[j]
    group[...] = whole
    info_z[z] = whole
    arrived_z = go_all(
        (group, info_z.at[z], device(dz=dz)) for dz in (4, 3, 5, 2, 6, 1, 7)
    )
    work(5)
    give(5)
    meet(4)
    z_whole(4)
    x_mid(0)
    x_mid(1)
    work(6)
    give(6)
    meet(5)
    x_start(5)
    x_mid(2)
    work(7)
    give(7)
    meet(6)
    x_direct(6)
    x_end(0)
    x_end(1)
    cross[7].wait_recv()
    whole_slab[3].wait_recv()
    whole_slab[4].wait_recv()
    part[7] += other_in[7] + zslab[0] + zslab[1]
    x_direct(7)
    x_mid(5)
    x_end(2)
    x_end(6)
    x_end(5)
    x_end(7)
    own = part[7, x]
    for d in (2, -2):
        zs[d].wait_recv()
        own = own + zin[ORDER.index(d)]

    mine = z * NC + c
    table[mine] = own
    rings, pairs = {}, []

    def blk(dz):
        return zat(dz) * NC + c

    def core_share(dz):
        at = blk(dz)
        pairs.append(go(table.at[at], table.at[at], device(dc=1)))

    for dz in (2, -2, 1, -1):
        rings[dz] = go(table.at[mine], table.at[mine], device(dz=dz))
    core_share(0)

    square = jnp.sum(own * own, axis=1, keepdims=True)
    sq_own[0] = as_rows([square], pad)[0:1, :]
    sq_arrived = go_all(
        (sq_own.at[0], sq_in.at[dx * NY + dy], device(dx=dx, dy=dy)) for dx, dy in group_xy
    )

    arrived_z()
    total = info_z[0, 0:BLOCKS]
    for j in range(1, NZ):
        total = total + info_z[j, 0:BLOCKS]
    counts[...] = total

    half = ROWS // 2
    for way in (1, -1):
        rings[2 * way].wait_recv()
        at = blk(-2 * way)
        rings[3 * way] = go(table.at[at], table.at[at], device(dz=way))
        rows = pl.ds(0 if way > 0 else half, half)
        rings[4 * way] = go(table.at[at, rows], table.at[at, rows], device(dz=2 * way))
        core_share(-2 * way)
    for way in (1, -1):
        rings[way].wait_recv()
        core_share(-way)

    keys_all = group[BLOCKS : BLOCKS + 8, :]
    keys = as_columns(jnp.where(c == 0, keys_all, pltpu.roll(keys_all, 6, 0)))
    cents = NX * cent_ref.shape[0]
    r = lax.broadcasted_iota(jnp.int32, (cents, LANE), 0)
    per = cent_ref.shape[0]
    r = z * (cents * NC) + lax.div(r, per) * (per * NC) + c * per + lax.rem(r, per)
    cent_key = r.astype(jnp.float32)
    spread_key = [jnp.broadcast_to(keys[0:ROWS, t : t + 1], (ROWS, LANE)) for t in range(2)]
    parts = [
        (0, cents, cent_key, 0), (cents, cents, cent_key, 1),
        (2 * cents, ROWS, spread_key[0], 0), (2 * cents + ROWS, ROWS, spread_key[1], 1),
    ]
    weight[...] = jnp.zeros_like(weight)
    for b in range(BLOCKS):
        many = counts[b : b + 1, :]
        for at, n, key, t in parts:
            line = BLOCKS + 2 * (b % NC) + t
            same = jnp.where(key == info_z[b // NC, line : line + 1, :], 1.0, 0.0)
            match[at : at + n, b * LANE : (b + 1) * LANE] = same.astype(jnp.bfloat16)
            weight[at : at + n, :] += same * many
    summed = jnp.sum(weight[...], axis=1, keepdims=True)
    weight[...] = jnp.broadcast_to(summed, weight.shape)
    first_row = 2 * cents
    wrows[...] = as_rows(
        [summed[first_row : first_row + ROWS], summed[first_row + ROWS : first_row + 2 * ROWS]], pad
    )

    sq_arrived()
    square_row = sq_own[0]
    for j in range(1, NX * NY):
        square_row = square_row + sq_in[j]
    inverse = lax.rsqrt(square_row / features + EPS)
    scale[mine] = inverse
    scale_arrived = go_all(
        (scale.at[mine], scale.at[mine], device(dz=dz, dc=dc)) for dz, dc in group_zc
    )
    means = own * as_columns(jnp.broadcast_to(inverse, (8, LANE)))[0:ROWS, 0:1]

    for way in (1, -1):
        rings[3 * way].wait_recv()
        core_share(-3 * way)
    rings[4].wait_recv()
    rings[-4].wait_recv()
    core_share(4)

    scale_arrived()
    for b in range(BLOCKS):
        scale2[b : b + 1, :] = scale[b]
    factor = as_columns(counts[...] * scale2[...])
    for pair in pairs:
        pair.wait_recv()
    scaled[...] = jnp.zeros_like(scaled)
    for b in range(BLOCKS):
        rows = table[b] * factor[0:ROWS, b : b + 1]
        for piece in range(3):
            near = rows.astype(jnp.bfloat16)
            scaled[b * LANE : b * LANE + ROWS, piece * LANE : (piece + 1) * LANE] = near
            rows = rows - near.astype(jnp.float32)
    tot = jnp.dot(match[...], scaled[...], preferred_element_type=jnp.float32)
    tot = tot[:, 0:LANE] + (tot[:, LANE : 2 * LANE] + tot[:, 2 * LANE : 3 * LANE])

    columns = []
    for t in range(2):
        at = first_row + t * ROWS
        many = weight[at : at + ROWS, :]
        g = tot[at : at + ROWS] * jnp.where(many > 0, 1.0 / jnp.maximum(many, 1.0), 0.0)
        d = means - g
        for v in (d * d, d * g, g * g):
            columns.append(jnp.sum(v, axis=1, keepdims=True))
    chosen = jnp.where(weight[cents : 2 * cents, :] > 0, tot[cents : 2 * cents], tot[0:cents])
    sel[...] = chosen
    squares = jnp.sum(chosen * chosen, axis=1, keepdims=True)
    columns.append(jnp.concatenate([squares, jnp.zeros((ROWS - cents, 1), jnp.float32)], 0))
    final_own[...] = as_rows(columns, pad)
    final_arrived = go_all(
        (final_own, final_in.at[dx * NY + dy], device(dx=dx, dy=dy)) for dx, dy in group_xy
    )
    sel_arrived = go_all(
        (sel.at[pl.ds(pl.multiple_of(xat(dx) * per, per), per)], sel_in.at[x], device(dx=dx))
        for dx in (2, 1, 3)
    )
    here = pl.ds(pl.multiple_of(x * per, per), per)
    sel_in[x] = sel[here, :]

    final_arrived()
    last_sum = final_own[...]
    for j in range(1, NX * NY):
        last_sum = last_sum + final_in[j]
    for t in range(2):
        far, mixed, length = (last_sum[3 * t + j : 3 * t + j + 1] for j in range(3))
        many = wrows[t : t + 1, :]
        s = many * lax.rsqrt(many * many * (length / features) + EPS) - 1.0
        value = (far - 2.0 * s * mixed + s * s * length) / features
        value = pltpu.roll(jnp.broadcast_to(value, (8, LANE)), LANE - x * OWN, 1)
        spread_ref[t : t + 1, :] = value[0:1, 0:OWN]
    lens[...] = as_columns(last_sum)
    length = lens[here, 6:7]
    inverse = lax.rsqrt(length / features + EPS)
    first = weight[here, :]
    second = weight[pl.ds(pl.multiple_of(x * per + cents, per), per), :]
    keep = jnp.maximum(first, second) > 0
    sel_arrived()
    for b in range(NX):
        at = slice(b * LANE, (b + 1) * LANE)
        cent_ref[:, at] = jnp.where(keep, sel_in[b] * inverse, init_ref[:, at])

    for wait in sent:
        wait()


COPIES = 7 + 7 + 8 + 18 + 2 + 5 + 8 + 8 + 15 + 15 + 15 + 3


def per_device(features, embeddings, sample_owner, lloyd_assign, init_centroids):
    samples, width = embeddings.shape
    per = init_centroids.shape[0]
    depth = 2048
    f32, bf16 = jnp.float32, jnp.bfloat16
    vm = pltpu.VMEM
    cents = NX * per
    lines = 2 * (cents + ROWS)
    scratch = [
        vm((1, samples), jnp.int32),
        vm((2, OWN), jnp.int32),
        vm((per, width), f32),
        vm((samples, width), bf16),
        vm((NZ, NX, ROWS, LANE), f32),
        vm((NZ, NX, ROWS, LANE), f32),
        vm((NZ, NX, ROWS, LANE), f32),
        vm((NZ, 3, ROWS, LANE), f32),
        vm((2, NX, ROWS, LANE), f32),
        vm((NZ, ROWS, LANE), f32),
        vm((1, samples), jnp.int32),
        vm((8, LANE), f32),
        vm((24, LANE), f32),
        vm((NX * NC, 24, LANE), f32),
        vm((24, LANE), f32),
        vm((NZ, 24, LANE), f32),
        vm((BLOCKS, LANE), f32),
        vm((lines, BLOCKS * LANE), bf16),
        vm((lines, LANE), f32),
        vm((LANE, LANE), f32),
        vm((8, LANE), f32),
        vm((BLOCKS, ROWS, LANE), f32),
        vm((1, 1, LANE), f32),
        vm((NX * NY, 1, LANE), f32),
        vm((BLOCKS, 1, LANE), f32),
        vm((BLOCKS, LANE), f32),
        vm((BLOCKS * LANE, 3 * LANE), bf16),
        vm((8, LANE), f32),
        vm((NX * NY, 8, LANE), f32),
        vm((cents, LANE), f32),
        vm((NX, per, LANE), f32),
        vm((LANE, 8), f32),
        pltpu.SemaphoreType.DMA((samples // depth + 3,)),
        pltpu.SemaphoreType.DMA((COPIES,)),
        pltpu.SemaphoreType.DMA((COPIES,)),
    ]
    in_vmem = pl.BlockSpec(memory_space=pltpu.VMEM)

    def body(*refs):
        kernel(depth, width, features, *refs)

    packed = pl.pallas_call(
        body,
        name="recluster",
        out_shape=(
            jax.ShapeDtypeStruct((per, width), f32),
            jax.ShapeDtypeStruct((2, OWN), f32),
        ),
        in_specs=[pl.BlockSpec(memory_space=pl.ANY)] * 4,
        out_specs=(in_vmem, in_vmem),
        scratch_shapes=scratch,
        compiler_params=pltpu.CompilerParams(
            collective_id=0, has_side_effects=True, vmem_limit_bytes=60 << 20
        ),
    )(sample_owner.reshape(1, samples), lloyd_assign, init_centroids, embeddings)

    def hand_out(cent_in, spread_in, cent_out, spread_out, sem):
        copies = [
            pltpu.make_async_copy(cent_in, cent_out, sem.at[0]),
            pltpu.make_async_copy(spread_in, spread_out, sem.at[1]),
        ]
        for copy in copies:
            copy.start()
        for copy in copies:
            copy.wait()

    anywhere = pl.BlockSpec(memory_space=pl.ANY)
    return pl.pallas_call(
        hand_out,
        name="hand_out",
        out_shape=(
            jax.ShapeDtypeStruct((per, width), f32),
            jax.ShapeDtypeStruct((2, OWN), f32),
        ),
        in_specs=[anywhere] * 2,
        out_specs=(anywhere, anywhere),
        scratch_shapes=[pltpu.SemaphoreType.DMA((2,))],
    )(*packed)


def solution(mesh):
    def run(embeddings, sample_owner, lloyd_assign, init_centroids):
        features = embeddings.shape[1]
        return jax.shard_map(
            lambda *args: per_device(features, *args),
            mesh=mesh,
            in_specs=(P("dp", "feat"), P("dp"), P(None, "dp"), P("dp", "feat")),
            out_specs=(P("dp", "feat"), P(None, "dp")),
            check_vma=False,
        )(embeddings, sample_owner, lloyd_assign, init_centroids)

    return run
```

```python
import jax
import jax.numpy as jnp
from jax import lax
from jax.experimental import pallas as pl
from jax.experimental.pallas import tpu as pltpu
from jax.sharding import PartitionSpec as P

EPS = 1e-06
MESH = pl.DeviceIdType.MESH

NZ, NX, NC, NY = 8, 4, 2, 4
OWN = 24
ROWS = NX * OWN
BLOCKS = NZ * NC
LANE = 128
ORDER = (4, 3, 1, -1, -3, 2, -2, 0)


def position(owner):
    slab = lax.shift_right_logical(owner * 21846, 22)
    left = owner - slab * (NX * NC * OWN)
    column = lax.shift_right_logical(left * 1366, 16)
    inner = left - column * (NC * OWN)
    core = jnp.where(inner >= OWN, 1, 0)
    block = slab * NC + core
    return block, column * OWN + inner - core * OWN


def as_rows(columns, pad_ref):
    pad_ref[...] = jnp.zeros_like(pad_ref)
    lane = lax.broadcasted_iota(jnp.int32, (ROWS, LANE), 1)
    filled = jnp.zeros((ROWS, LANE), jnp.float32)
    for j, column in enumerate(columns):
        filled = jnp.where(lane == j, column, filled)
    pad_ref[0:ROWS, :] = filled
    return jnp.transpose(pad_ref[...])[0:8, :]


def as_columns(tile):
    return jnp.transpose(tile)


def kernel(
    depth, width, features,
    owner_hbm, assign_hbm, init_hbm, emb_hbm,
    cent_ref, spread_ref,
    owner_ref, assign_ref, init_ref,
    emb, part, other, other_in, xin, zslab, zin,
    prow, tile, info, info_x, group, info_z, counts, match, weight, pad, wrows,
    table, sq_own, sq_in, scale, scale2, scaled, final_own, final_in, sel, sel_in, lens,
    load_sem, send_sem, recv_sem,
):
    dp, y = lax.axis_index("dp"), lax.axis_index("feat")
    z = lax.div(dp, NX * NC)
    x = lax.div(dp - z * (NX * NC), NC)
    c = dp - z * (NX * NC) - x * NC

    def around(at, size):
        steps = [at]
        for d in range(1, size):
            steps.append(jnp.where(at + d >= size, at + (d - size), at + d))
        return steps

    z_at, x_at, c_at, y_at = around(z, NZ), around(x, NX), around(c, NC), around(y, NY)
    z_first = [at * (NX * NC) for at in z_at]
    x_first = [at * NC for at in x_at]

    def zat(d):
        return z_at[d % NZ]

    def xat(d):
        return x_at[d % NX]

    def device(dz=0, dx=0, dc=0, dy=0):
        return (z_first[dz % NZ] + (x_first[dx % NX] + c_at[dc % NC]), y_at[dy % NY])

    used = [0]
    sent = []

    def go(src, dst, to):
        slot = used[0]
        used[0] += 1
        copy = pltpu.make_async_remote_copy(
            src_ref=src, dst_ref=dst, send_sem=send_sem.at[slot], recv_sem=recv_sem.at[slot],
            device_id=to, device_id_type=MESH,
        )
        copy.start()
        sent.append(copy.wait_send)
        return copy

    def go_all(makes):
        copies = [go(*make) for make in makes]

        def wait():
            for copy in copies:
                copy.wait_recv()

        return wait

    group_xc = [(dx, dc) for dx in (2, 1, 3, 0) for dc in range(NC) if (dx, dc) != (0, 0)]
    group_xy = [
        (dx, dy) for dx in (2, 1, 3, 0) for dy in (2, 1, 3, 0) if (dx, dy) != (0, 0)
    ]
    group_zc = [
        (dz, dc) for dz in (4, 3, 5, 2, 6, 1, 7, 0) for dc in range(NC) if (dz, dc) != (0, 0)
    ]

    chunks = emb.shape[0] // depth
    loads = [
        pltpu.make_async_copy(
            emb_hbm.at[pl.ds(k * depth, depth)], emb.at[pl.ds(k * depth, depth)], load_sem.at[k]
        )
        for k in range(chunks)
    ]
    small = [
        pltpu.make_async_copy(src, dst, load_sem.at[chunks + k])
        for k, (src, dst) in enumerate(
            ((owner_hbm, owner_ref), (assign_hbm, assign_ref), (init_hbm, init_ref))
        )
    ]
    for load in small + loads:
        load.start()

    barrier = pltpu.get_barrier_semaphore()

    greeted = {(dz, 0, dc, 0) for dz, dc in group_zc}
    greeted |= {(0, dx, 0, dy) for dx, dy in group_xy} | {(0, dx, dc, 0) for dx, dc in group_xc}
    for steps in sorted(greeted, key=lambda v: (-sum(min(a, b - a) for a, b in zip(v, (NZ, NX, NC, NY))), v)):
        pl.semaphore_signal(barrier, inc=1, device_id=device(*steps), device_id_type=MESH)

    tile[...] = jnp.zeros_like(tile)
    part[...] = jnp.zeros_like(part)
    other[...] = jnp.zeros_like(other)
    for load in small:
        load.wait()
    block, place = position(owner_ref[...])
    prow[...] = block * ROWS + place

    def count():
        samples = owner_ref.shape[1]
        block, place = position(owner_ref[...])
        high = lax.broadcasted_iota(jnp.int32, (BLOCKS, samples), 0) == block
        low = lax.broadcasted_iota(jnp.int32, (LANE, samples), 0) == place
        info[0:BLOCKS, :] = lax.dot_general(
            jnp.where(high, 1.0, 0.0).astype(jnp.bfloat16),
            jnp.where(low, 1.0, 0.0).astype(jnp.bfloat16),
            (((1,), (1,)), ((), ())), preferred_element_type=jnp.float32,
        )
        tile[0:2, 0:OWN] = assign_ref[...].astype(jnp.float32)
        placed = pltpu.roll(tile[...], x * OWN, 1)
        info[BLOCKS : BLOCKS + 8, :] = jnp.where(c == 0, placed, pltpu.roll(placed, 2, 0))
        info_x[0] = info[...]
        return go_all(
            (info, info_x.at[dx * NC + dc], device(dx=dx, dc=dc)) for dx, dc in group_xc
        )

    def sums(bases, into, waits=()):
        row = lax.broadcasted_iota(jnp.int32, (ROWS, depth), 0)

        def step(k):
            at = pl.ds(pl.multiple_of(k * depth, depth), depth)
            p = prow[:, at]
            hot = jnp.concatenate(
                [jnp.where(row == p - base, 1.0, 0.0).astype(jnp.bfloat16) for base in bases], 0
            )
            got = jnp.dot(hot, emb[at, :], preferred_element_type=jnp.float32)
            for j, ref in enumerate(into):
                for b in range(NX):
                    ref[b] += got[j * ROWS : (j + 1) * ROWS, b * LANE : (b + 1) * LANE]

        if waits:
            for k in range(chunks):
                waits[k].wait()
                step(k)
        else:
            lax.fori_loop(0, chunks, lambda k, carry: (step(k), carry)[1], 0)

    cross = {}

    def work(*slabs):
        bases, into = [], []
        for s in slabs:
            base = zat(ORDER[s]) * (NC * ROWS)
            bases += [base + (1 - c) * ROWS, base + c * ROWS]
            into += [other.at[s], part.at[s]]
        sums(bases, into, loads if 0 in slabs else ())

    def give(s):
        cross[s] = go(other.at[s], other_in.at[s], device(dc=1))

    def meet(s):
        cross[s].wait_recv()
        part[s] += other_in[s]

    xs = {}

    def way_of(s):
        return 1 if s == 1 else -1

    def x_start(s):
        way = way_of(s)
        xs[s, 0] = go(part.at[s, xat(2)], xin.at[s, 0], device(dx=way))
        xs[s, 1] = go(part.at[s, xat(-way)], xin.at[s, 1], device(dx=-way))

    def x_mid(s):
        way = way_of(s)
        xs[s, 0].wait_recv()
        part[s, xat(way)] += xin[s, 0]
        xs[s, 2] = go(part.at[s, xat(way)], xin.at[s, 2], device(dx=way))

    def x_direct(s):
        for k, d in enumerate((2, 1, -1)):
            xs[s, k] = go(part.at[s, xat(d)], xin.at[s, k], device(dx=d))

    zs = {}
    hops = {4: 2, 3: 1}

    def x_end(s):
        d = ORDER[s]
        if (s, 0) in direct:
            xs[s, 0].wait_recv()
        xs[s, 1].wait_recv()
        xs[s, 2].wait_recv()
        total = part[s, x] + xin[s, 1] + xin[s, 2]
        if (s, 0) in direct:
            total = total + xin[s, 0]
        for far in (4, 3) if d == 2 else ():
            zs[far].wait_recv()
            total = total + zin[ORDER.index(far)]
        part[s, x] = total
        if d != 0:
            zs[d] = go(part.at[s, x], zin.at[s], device(dz=hops.get(d, d)))

    direct = {(6, 0)}

    work(0, 1)
    scaled[...] = jnp.zeros_like(scaled)
    pl.semaphore_wait(barrier, len(greeted))
    give(0)
    give(1)
    arrived = count()

    whole_slab = {}

    def z_whole(s):
        d = ORDER[s]
        whole_slab[s] = go(part.at[s], zslab.at[s - 2], device(dz=d))

    work(2, 3)
    give(2)
    give(3)
    meet(0)
    x_start(0)
    meet(1)
    x_start(1)
    work(4)
    give(4)
    meet(2)
    z_whole(2)
    meet(3)
    z_whole(3)
    work(5)
    give(5)
    meet(4)
    x_start(4)
    x_mid(0)
    x_mid(1)
    arrived()
    whole = info_x[0]
    for j in range(1, NX * NC):
        whole = whole + info_x[j]
    group[...] = whole
    info_z[z] = whole
    arrived_z = go_all(
        (group, info_z.at[z], device(dz=dz)) for dz in (4, 3, 5, 2, 6, 1, 7)
    )
    work(6)
    give(6)
    meet(5)
    x_start(5)
    work(7)
    give(7)
    meet(6)
    x_direct(6)
    x_mid(4)
    x_end(0)
    x_end(1)
    cross[7].wait_recv()
    whole_slab[2].wait_recv()
    whole_slab[3].wait_recv()
    part[7] += other_in[7] + zslab[0] + zslab[1]
    x_start(7)
    x_mid(5)
    x_end(4)
    x_mid(7)
    x_end(5)
    x_end(6)
    x_end(7)
    own = part[7, x]
    for d in (-3, 2, -2):
        zs[d].wait_recv()
        own = own + zin[ORDER.index(d)]

    mine = z * NC + c
    table[mine] = own
    rings, pairs = {}, []

    def blk(dz):
        return zat(dz) * NC + c

    def core_share(dz):
        at = blk(dz)
        pairs.append(go(table.at[at], table.at[at], device(dc=1)))

    square = jnp.sum(own * own, axis=1, keepdims=True)
    sq_own[0] = as_rows([square], pad)[0:1, :]
    sq_arrived = go_all(
        (sq_own.at[0], sq_in.at[dx * NY + dy], device(dx=dx, dy=dy)) for dx, dy in group_xy
    )

    for dz in (2, -2, 1, -1):
        rings[dz] = go(table.at[mine], table.at[mine], device(dz=dz))
    core_share(0)

    arrived_z()
    total = info_z[0, 0:BLOCKS]
    for j in range(1, NZ):
        total = total + info_z[j, 0:BLOCKS]
    counts[...] = total

    half = ROWS // 2
    for way in (1, -1):
        rings[2 * way].wait_recv()
        at = blk(-2 * way)
        rings[3 * way] = go(table.at[at], table.at[at], device(dz=way))
        rows = pl.ds(0 if way > 0 else half, half)
        rings[4 * way] = go(table.at[at, rows], table.at[at, rows], device(dz=2 * way))
        core_share(-2 * way)
    for way in (1, -1):
        rings[way].wait_recv()
        core_share(-way)

    sq_arrived()
    square_row = sq_own[0]
    for j in range(1, NX * NY):
        square_row = square_row + sq_in[j]
    inverse = lax.rsqrt(square_row / features + EPS)
    scale[mine] = inverse
    scale_arrived = go_all(
        (scale.at[mine], scale.at[mine], device(dz=dz, dc=dc)) for dz, dc in group_zc
    )
    means = own * as_columns(jnp.broadcast_to(inverse, (8, LANE)))[0:ROWS, 0:1]

    keys_all = group[BLOCKS : BLOCKS + 8, :]
    keys = as_columns(jnp.where(c == 0, keys_all, pltpu.roll(keys_all, 6, 0)))
    cents = NX * cent_ref.shape[0]
    r = lax.broadcasted_iota(jnp.int32, (cents, LANE), 0)
    per = cent_ref.shape[0]
    r = z * (cents * NC) + lax.div(r, per) * (per * NC) + c * per + lax.rem(r, per)
    cent_key = r.astype(jnp.float32)
    spread_key = [jnp.broadcast_to(keys[0:ROWS, t : t + 1], (ROWS, LANE)) for t in range(2)]
    parts = [
        (0, cents, cent_key, 0), (cents, cents, cent_key, 1),
        (2 * cents, ROWS, spread_key[0], 0), (2 * cents + ROWS, ROWS, spread_key[1], 1),
    ]
    weight[...] = jnp.zeros_like(weight)
    for b in range(BLOCKS):
        many = counts[b : b + 1, :]
        for at, n, key, t in parts:
            line = BLOCKS + 2 * (b % NC) + t
            same = jnp.where(key == info_z[b // NC, line : line + 1, :], 1.0, 0.0)
            match[at : at + n, b * LANE : (b + 1) * LANE] = same.astype(jnp.bfloat16)
            weight[at : at + n, :] += same * many
    summed = jnp.sum(weight[...], axis=1, keepdims=True)
    weight[...] = jnp.broadcast_to(summed, weight.shape)
    first_row = 2 * cents
    wrows[...] = as_rows(
        [summed[first_row : first_row + ROWS], summed[first_row + ROWS : first_row + 2 * ROWS]], pad
    )

    for way in (1, -1):
        rings[3 * way].wait_recv()
        core_share(-3 * way)
    rings[4].wait_recv()
    rings[-4].wait_recv()
    core_share(4)

    scale_arrived()
    for b in range(BLOCKS):
        scale2[b : b + 1, :] = scale[b]
    factor = as_columns(counts[...] * scale2[...])
    for pair in pairs:
        pair.wait_recv()
    for b in range(BLOCKS):
        rows = table[b] * factor[0:ROWS, b : b + 1]
        for piece in range(3):
            near = rows.astype(jnp.bfloat16)
            scaled[b * LANE : b * LANE + ROWS, piece * LANE : (piece + 1) * LANE] = near
            rows = rows - near.astype(jnp.float32)
    tot = jnp.dot(match[...], scaled[...], preferred_element_type=jnp.float32)
    tot = tot[:, 0:LANE] + (tot[:, LANE : 2 * LANE] + tot[:, 2 * LANE : 3 * LANE])

    columns = []
    for t in range(2):
        at = first_row + t * ROWS
        many = weight[at : at + ROWS, :]
        g = tot[at : at + ROWS] * jnp.where(many > 0, 1.0 / jnp.maximum(many, 1.0), 0.0)
        d = means - g
        for v in (d * d, d * g, g * g):
            columns.append(jnp.sum(v, axis=1, keepdims=True))
    chosen = jnp.where(weight[cents : 2 * cents, :] > 0, tot[cents : 2 * cents], tot[0:cents])
    sel[...] = chosen
    squares = jnp.sum(chosen * chosen, axis=1, keepdims=True)
    columns.append(jnp.concatenate([squares, jnp.zeros((ROWS - cents, 1), jnp.float32)], 0))
    final_own[...] = as_rows(columns, pad)
    final_arrived = go_all(
        (final_own, final_in.at[dx * NY + dy], device(dx=dx, dy=dy)) for dx, dy in group_xy
    )
    sel_arrived = go_all(
        (sel.at[pl.ds(pl.multiple_of(xat(dx) * per, per), per)], sel_in.at[x], device(dx=dx))
        for dx in (2, 1, 3)
    )
    here = pl.ds(pl.multiple_of(x * per, per), per)
    sel_in[x] = sel[here, :]

    final_arrived()
    last_sum = final_own[...]
    for j in range(1, NX * NY):
        last_sum = last_sum + final_in[j]
    for t in range(2):
        far, mixed, length = (last_sum[3 * t + j : 3 * t + j + 1] for j in range(3))
        many = wrows[t : t + 1, :]
        s = many * lax.rsqrt(many * many * (length / features) + EPS) - 1.0
        value = (far - 2.0 * s * mixed + s * s * length) / features
        value = pltpu.roll(jnp.broadcast_to(value, (8, LANE)), LANE - x * OWN, 1)
        spread_ref[t : t + 1, :] = value[0:1, 0:OWN]
    lens[...] = as_columns(last_sum)
    length = lens[here, 6:7]
    inverse = lax.rsqrt(length / features + EPS)
    first = weight[here, :]
    second = weight[pl.ds(pl.multiple_of(x * per + cents, per), per), :]
    keep = jnp.maximum(first, second) > 0
    sel_arrived()
    for b in range(NX):
        at = slice(b * LANE, (b + 1) * LANE)
        cent_ref[:, at] = jnp.where(keep, sel_in[b] * inverse, init_ref[:, at])

    for wait in sent:
        wait()


COPIES = 7 + 7 + 8 + 18 + 2 + 5 + 8 + 8 + 15 + 15 + 15 + 3


def per_device(features, embeddings, sample_owner, lloyd_assign, init_centroids):
    samples, width = embeddings.shape
    per = init_centroids.shape[0]
    depth = 2048
    f32, bf16 = jnp.float32, jnp.bfloat16
    vm = pltpu.VMEM
    cents = NX * per
    lines = 2 * (cents + ROWS)
    scratch = [
        vm((1, samples), jnp.int32),
        vm((2, OWN), jnp.int32),
        vm((per, width), f32),
        vm((samples, width), bf16),
        vm((NZ, NX, ROWS, LANE), f32),
        vm((NZ, NX, ROWS, LANE), f32),
        vm((NZ, NX, ROWS, LANE), f32),
        vm((NZ, 3, ROWS, LANE), f32),
        vm((2, NX, ROWS, LANE), f32),
        vm((NZ, ROWS, LANE), f32),
        vm((1, samples), jnp.int32),
        vm((8, LANE), f32),
        vm((24, LANE), f32),
        vm((NX * NC, 24, LANE), f32),
        vm((24, LANE), f32),
        vm((NZ, 24, LANE), f32),
        vm((BLOCKS, LANE), f32),
        vm((lines, BLOCKS * LANE), bf16),
        vm((lines, LANE), f32),
        vm((LANE, LANE), f32),
        vm((8, LANE), f32),
        vm((BLOCKS, ROWS, LANE), f32),
        vm((1, 1, LANE), f32),
        vm((NX * NY, 1, LANE), f32),
        vm((BLOCKS, 1, LANE), f32),
        vm((BLOCKS, LANE), f32),
        vm((BLOCKS * LANE, 3 * LANE), bf16),
        vm((8, LANE), f32),
        vm((NX * NY, 8, LANE), f32),
        vm((cents, LANE), f32),
        vm((NX, per, LANE), f32),
        vm((LANE, 8), f32),
        pltpu.SemaphoreType.DMA((samples // depth + 3,)),
        pltpu.SemaphoreType.DMA((COPIES,)),
        pltpu.SemaphoreType.DMA((COPIES,)),
    ]
    in_vmem = pl.BlockSpec(memory_space=pltpu.VMEM)

    def body(*refs):
        kernel(depth, width, features, *refs)

    packed = pl.pallas_call(
        body,
        name="recluster",
        out_shape=(
            jax.ShapeDtypeStruct((per, width), f32),
            jax.ShapeDtypeStruct((2, OWN), f32),
        ),
        in_specs=[pl.BlockSpec(memory_space=pl.ANY)] * 4,
        out_specs=(in_vmem, in_vmem),
        scratch_shapes=scratch,
        compiler_params=pltpu.CompilerParams(
            collective_id=0, has_side_effects=True, vmem_limit_bytes=60 << 20
        ),
    )(sample_owner.reshape(1, samples), lloyd_assign, init_centroids, embeddings)

    def hand_out(cent_in, spread_in, cent_out, spread_out, cent_mid, spread_mid, sem):
        through = ((cent_in, cent_mid, cent_out), (spread_in, spread_mid, spread_out))
        first = [pltpu.make_async_copy(v[0], v[1], sem.at[k]) for k, v in enumerate(through)]
        last = [pltpu.make_async_copy(v[1], v[2], sem.at[2 + k]) for k, v in enumerate(through)]
        for copy in first:
            copy.start()
        for k in range(2):
            first[k].wait()
            last[k].start()
        for copy in last:
            copy.wait()

    anywhere = pl.BlockSpec(memory_space=pl.ANY)
    return pl.pallas_call(
        hand_out,
        name="hand_out",
        out_shape=(
            jax.ShapeDtypeStruct((per, width), f32),
            jax.ShapeDtypeStruct((2, OWN), f32),
        ),
        in_specs=[anywhere] * 2,
        out_specs=(anywhere, anywhere),
        scratch_shapes=[vm((per, width), f32), vm((2, OWN), f32), pltpu.SemaphoreType.DMA((4,))],
    )(*packed)


def solution(mesh):
    def run(embeddings, sample_owner, lloyd_assign, init_centroids):
        features = embeddings.shape[1]
        return jax.shard_map(
            lambda *args: per_device(features, *args),
            mesh=mesh,
            in_specs=(P("dp", "feat"), P("dp"), P(None, "dp"), P("dp", "feat")),
            out_specs=(P("dp", "feat"), P(None, "dp")),
            check_vma=False,
        )(embeddings, sample_owner, lloyd_assign, init_centroids)

    return run
```

```python
import jax
import jax.numpy as jnp
from jax import lax
from jax.experimental import pallas as pl
from jax.experimental.pallas import tpu as pltpu
from jax.sharding import PartitionSpec as P

EPS = 1e-06
MESH = pl.DeviceIdType.MESH

NZ, NX, NC, NY = 8, 4, 2, 4
OWN = 24
ROWS = NX * OWN
BLOCKS = NZ * NC
LANE = 128
ORDER = (4, 3, 1, -1, -3, 2, -2, 0)


def position(owner):
    slab = lax.shift_right_logical(owner * 21846, 22)
    left = owner - slab * (NX * NC * OWN)
    column = lax.shift_right_logical(left * 1366, 16)
    inner = left - column * (NC * OWN)
    core = jnp.where(inner >= OWN, 1, 0)
    block = slab * NC + core
    return block, column * OWN + inner - core * OWN


def as_rows(columns, pad_ref):
    pad_ref[...] = jnp.zeros_like(pad_ref)
    lane = lax.broadcasted_iota(jnp.int32, (ROWS, LANE), 1)
    filled = jnp.zeros((ROWS, LANE), jnp.float32)
    for j, column in enumerate(columns):
        filled = jnp.where(lane == j, column, filled)
    pad_ref[0:ROWS, :] = filled
    return jnp.transpose(pad_ref[...])[0:8, :]


def as_columns(tile):
    return jnp.transpose(tile)


def kernel(
    depth, width, features,
    owner_hbm, assign_hbm, init_hbm, emb_hbm,
    cent_ref, spread_ref,
    owner_ref, assign_ref, init_ref,
    emb, part, other, other_in, xin, zslab, zin,
    prow, tile, info, info_x, group, info_z, counts, match, weight, pad, wrows,
    table, sq_own, sq_in, scale, scale2, scaled, final_own, final_in, sel, sel_in, lens,
    load_sem, send_sem, recv_sem,
):
    dp, y = lax.axis_index("dp"), lax.axis_index("feat")
    z = lax.div(dp, NX * NC)
    x = lax.div(dp - z * (NX * NC), NC)
    c = dp - z * (NX * NC) - x * NC

    def around(at, size):
        steps = [at]
        for d in range(1, size):
            steps.append(jnp.where(at + d >= size, at + (d - size), at + d))
        return steps

    z_at, x_at, c_at, y_at = around(z, NZ), around(x, NX), around(c, NC), around(y, NY)
    z_first = [at * (NX * NC) for at in z_at]
    x_first = [at * NC for at in x_at]

    def zat(d):
        return z_at[d % NZ]

    def xat(d):
        return x_at[d % NX]

    def device(dz=0, dx=0, dc=0, dy=0):
        return (z_first[dz % NZ] + (x_first[dx % NX] + c_at[dc % NC]), y_at[dy % NY])

    used = [0]
    sent = []

    def go(src, dst, to):
        slot = used[0]
        used[0] += 1
        copy = pltpu.make_async_remote_copy(
            src_ref=src, dst_ref=dst, send_sem=send_sem.at[slot], recv_sem=recv_sem.at[slot],
            device_id=to, device_id_type=MESH,
        )
        copy.start()
        sent.append(copy.wait_send)
        return copy

    def go_all(makes):
        copies = [go(*make) for make in makes]

        def wait():
            for copy in copies:
                copy.wait_recv()

        return wait

    group_xc = [(dx, dc) for dx in (2, 1, 3, 0) for dc in range(NC) if (dx, dc) != (0, 0)]
    group_xy = [
        (dx, dy) for dx in (2, 1, 3, 0) for dy in (2, 1, 3, 0) if (dx, dy) != (0, 0)
    ]
    group_zc = [
        (dz, dc) for dz in (4, 3, 5, 2, 6, 1, 7, 0) for dc in range(NC) if (dz, dc) != (0, 0)
    ]

    chunks = emb.shape[0] // depth
    loads = [
        pltpu.make_async_copy(
            emb_hbm.at[pl.ds(k * depth, depth)], emb.at[pl.ds(k * depth, depth)], load_sem.at[k]
        )
        for k in range(chunks)
    ]
    small = [
        pltpu.make_async_copy(src, dst, load_sem.at[chunks + k])
        for k, (src, dst) in enumerate(
            ((owner_hbm, owner_ref), (assign_hbm, assign_ref), (init_hbm, init_ref))
        )
    ]
    for load in small + loads:
        load.start()

    barrier = pltpu.get_barrier_semaphore()

    greeted = {(dz, 0, dc, 0) for dz, dc in group_zc}
    greeted |= {(0, dx, 0, dy) for dx, dy in group_xy} | {(0, dx, dc, 0) for dx, dc in group_xc}
    for steps in sorted(greeted, key=lambda v: (-sum(min(a, b - a) for a, b in zip(v, (NZ, NX, NC, NY))), v)):
        pl.semaphore_signal(barrier, inc=1, device_id=device(*steps), device_id_type=MESH)

    tile[...] = jnp.zeros_like(tile)
    part[...] = jnp.zeros_like(part)
    other[...] = jnp.zeros_like(other)
    for load in small:
        load.wait()
    block, place = position(owner_ref[...])
    prow[...] = block * ROWS + place

    def count():
        samples = owner_ref.shape[1]
        block, place = position(owner_ref[...])
        high = lax.broadcasted_iota(jnp.int32, (BLOCKS, samples), 0) == block
        low = lax.broadcasted_iota(jnp.int32, (LANE, samples), 0) == place
        info[0:BLOCKS, :] = lax.dot_general(
            jnp.where(high, 1.0, 0.0).astype(jnp.bfloat16),
            jnp.where(low, 1.0, 0.0).astype(jnp.bfloat16),
            (((1,), (1,)), ((), ())), preferred_element_type=jnp.float32,
        )
        tile[0:2, 0:OWN] = assign_ref[...].astype(jnp.float32)
        placed = pltpu.roll(tile[...], x * OWN, 1)
        info[BLOCKS : BLOCKS + 8, :] = jnp.where(c == 0, placed, pltpu.roll(placed, 2, 0))
        info_x[0] = info[...]
        return go_all(
            (info, info_x.at[dx * NC + dc], device(dx=dx, dc=dc)) for dx, dc in group_xc
        )

    def sums(bases, into, waits=()):
        row = lax.broadcasted_iota(jnp.int32, (ROWS, depth), 0)

        def step(k):
            at = pl.ds(pl.multiple_of(k * depth, depth), depth)
            p = prow[:, at]
            hot = jnp.concatenate(
                [jnp.where(row == p - base, 1.0, 0.0).astype(jnp.bfloat16) for base in bases], 0
            )
            got = jnp.dot(hot, emb[at, :], preferred_element_type=jnp.float32)
            for j, ref in enumerate(into):
                for b in range(NX):
                    ref[b] += got[j * ROWS : (j + 1) * ROWS, b * LANE : (b + 1) * LANE]

        if waits:
            for k in range(chunks):
                waits[k].wait()
                step(k)
        else:
            lax.fori_loop(0, chunks, lambda k, carry: (step(k), carry)[1], 0)

    cross = {}

    def work(*slabs):
        bases, into = [], []
        for s in slabs:
            base = zat(ORDER[s]) * (NC * ROWS)
            bases += [base + (1 - c) * ROWS, base + c * ROWS]
            into += [other.at[s], part.at[s]]
        sums(bases, into, loads if 0 in slabs else ())

    def give(s):
        cross[s] = go(other.at[s], other_in.at[s], device(dc=1))

    def meet(s):
        cross[s].wait_recv()
        part[s] += other_in[s]

    xs = {}

    def way_of(s):
        return 1 if s == 1 else -1

    def x_start(s):
        way = way_of(s)
        xs[s, 0] = go(part.at[s, xat(2)], xin.at[s, 0], device(dx=way))
        xs[s, 1] = go(part.at[s, xat(-way)], xin.at[s, 1], device(dx=-way))

    def x_mid(s):
        way = way_of(s)
        xs[s, 0].wait_recv()
        part[s, xat(way)] += xin[s, 0]
        xs[s, 2] = go(part.at[s, xat(way)], xin.at[s, 2], device(dx=way))

    def x_direct(s):
        for k, d in enumerate((2, 1, -1)):
            xs[s, k] = go(part.at[s, xat(d)], xin.at[s, k], device(dx=d))

    zs = {}
    hops = {4: 2, 3: 1}

    def x_end(s):
        d = ORDER[s]
        if (s, 0) in direct:
            xs[s, 0].wait_recv()
        xs[s, 1].wait_recv()
        xs[s, 2].wait_recv()
        total = part[s, x] + xin[s, 1] + xin[s, 2]
        if (s, 0) in direct:
            total = total + xin[s, 0]
        for far in (4, 3) if d == 2 else ():
            zs[far].wait_recv()
            total = total + zin[ORDER.index(far)]
        part[s, x] = total
        if d != 0:
            zs[d] = go(part.at[s, x], zin.at[s], device(dz=hops.get(d, d)))

    direct = {(6, 0)}

    work(0)
    pl.semaphore_wait(barrier, len(greeted))
    give(0)
    arrived = count()

    whole_slab = {}

    def z_whole(s):
        d = ORDER[s]
        whole_slab[s] = go(part.at[s], zslab.at[s - 2], device(dz=d))

    work(1)
    give(1)
    meet(0)
    x_start(0)
    work(2)
    give(2)
    meet(1)
    x_start(1)
    work(3)
    give(3)
    meet(2)
    z_whole(2)
    work(4)
    give(4)
    meet(3)
    z_whole(3)
    x_mid(0)
    arrived()
    whole = info_x[0]
    for j in range(1, NX * NC):
        whole = whole + info_x[j]
    group[...] = whole
    info_z[z] = whole
    arrived_z = go_all(
        (group, info_z.at[z], device(dz=dz)) for dz in (4, 3, 5, 2, 6, 1, 7)
    )
    work(5)
    give(5)
    meet(4)
    x_start(4)
    x_mid(1)
    work(6)
    give(6)
    meet(5)
    x_start(5)
    work(7)
    give(7)
    meet(6)
    x_direct(6)
    x_end(0)
    x_mid(4)
    cross[7].wait_recv()
    whole_slab[2].wait_recv()
    whole_slab[3].wait_recv()
    part[7] += other_in[7] + zslab[0] + zslab[1]
    x_start(7)
    x_end(1)
    x_mid(5)
    x_mid(7)
    x_end(4)
    x_end(6)
    x_end(5)
    x_end(7)
    own = part[7, x]
    for d in (-3, 2, -2):
        zs[d].wait_recv()
        own = own + zin[ORDER.index(d)]

    mine = z * NC + c
    table[mine] = own
    rings, pairs = {}, []

    def blk(dz):
        return zat(dz) * NC + c

    def core_share(dz):
        at = blk(dz)
        pairs.append(go(table.at[at], table.at[at], device(dc=1)))

    square = jnp.sum(own * own, axis=1, keepdims=True)
    sq_own[0] = as_rows([square], pad)[0:1, :]
    sq_arrived = go_all(
        (sq_own.at[0], sq_in.at[dx * NY + dy], device(dx=dx, dy=dy)) for dx, dy in group_xy
    )

    for dz in (2, -2, 1, -1):
        rings[dz] = go(table.at[mine], table.at[mine], device(dz=dz))
    core_share(0)

    arrived_z()
    total = info_z[0, 0:BLOCKS]
    for j in range(1, NZ):
        total = total + info_z[j, 0:BLOCKS]
    counts[...] = total

    scaled[...] = jnp.zeros_like(scaled)

    half = ROWS // 2
    for way in (1, -1):
        rings[2 * way].wait_recv()
        at = blk(-2 * way)
        rings[3 * way] = go(table.at[at], table.at[at], device(dz=way))
        rows = pl.ds(0 if way > 0 else half, half)
        rings[4 * way] = go(table.at[at, rows], table.at[at, rows], device(dz=2 * way))
        core_share(-2 * way)
    for way in (1, -1):
        rings[way].wait_recv()
        core_share(-way)

    sq_arrived()
    square_row = sq_own[0]
    for j in range(1, NX * NY):
        square_row = square_row + sq_in[j]
    inverse = lax.rsqrt(square_row / features + EPS)
    scale[mine] = inverse
    scale_arrived = go_all(
        (scale.at[mine], scale.at[mine], device(dz=dz, dc=dc)) for dz, dc in group_zc
    )
    means = own * as_columns(jnp.broadcast_to(inverse, (8, LANE)))[0:ROWS, 0:1]

    keys_all = group[BLOCKS : BLOCKS + 8, :]
    keys = as_columns(jnp.where(c == 0, keys_all, pltpu.roll(keys_all, 6, 0)))
    cents = NX * cent_ref.shape[0]
    r = lax.broadcasted_iota(jnp.int32, (cents, LANE), 0)
    per = cent_ref.shape[0]
    r = z * (cents * NC) + lax.div(r, per) * (per * NC) + c * per + lax.rem(r, per)
    cent_key = r.astype(jnp.float32)
    spread_key = [jnp.broadcast_to(keys[0:ROWS, t : t + 1], (ROWS, LANE)) for t in range(2)]
    parts = [
        (0, cents, cent_key, 0), (cents, cents, cent_key, 1),
        (2 * cents, ROWS, spread_key[0], 0), (2 * cents + ROWS, ROWS, spread_key[1], 1),
    ]
    weight[...] = jnp.zeros_like(weight)
    for b in range(BLOCKS):
        many = counts[b : b + 1, :]
        for at, n, key, t in parts:
            line = BLOCKS + 2 * (b % NC) + t
            same = jnp.where(key == info_z[b // NC, line : line + 1, :], 1.0, 0.0)
            match[at : at + n, b * LANE : (b + 1) * LANE] = same.astype(jnp.bfloat16)
            weight[at : at + n, :] += same * many
    summed = jnp.sum(weight[...], axis=1, keepdims=True)
    weight[...] = jnp.broadcast_to(summed, weight.shape)
    first_row = 2 * cents
    wrows[...] = as_rows(
        [summed[first_row : first_row + ROWS], summed[first_row + ROWS : first_row + 2 * ROWS]], pad
    )

    for way in (1, -1):
        rings[3 * way].wait_recv()
        core_share(-3 * way)
    rings[4].wait_recv()
    rings[-4].wait_recv()
    core_share(4)

    scale_arrived()
    for b in range(BLOCKS):
        scale2[b : b + 1, :] = scale[b]
    factor = as_columns(counts[...] * scale2[...])
    for pair in pairs:
        pair.wait_recv()
    for b in range(BLOCKS):
        rows = table[b] * factor[0:ROWS, b : b + 1]
        for piece in range(3):
            near = rows.astype(jnp.bfloat16)
            scaled[b * LANE : b * LANE + ROWS, piece * LANE : (piece + 1) * LANE] = near
            rows = rows - near.astype(jnp.float32)
    tot = jnp.dot(match[...], scaled[...], preferred_element_type=jnp.float32)
    tot = tot[:, 0:LANE] + (tot[:, LANE : 2 * LANE] + tot[:, 2 * LANE : 3 * LANE])

    columns = []
    for t in range(2):
        at = first_row + t * ROWS
        many = weight[at : at + ROWS, :]
        g = tot[at : at + ROWS] * jnp.where(many > 0, 1.0 / jnp.maximum(many, 1.0), 0.0)
        d = means - g
        for v in (d * d, d * g, g * g):
            columns.append(jnp.sum(v, axis=1, keepdims=True))
    chosen = jnp.where(weight[cents : 2 * cents, :] > 0, tot[cents : 2 * cents], tot[0:cents])
    sel[...] = chosen
    squares = jnp.sum(chosen * chosen, axis=1, keepdims=True)
    columns.append(jnp.concatenate([squares, jnp.zeros((ROWS - cents, 1), jnp.float32)], 0))
    final_own[...] = as_rows(columns, pad)
    final_arrived = go_all(
        (final_own, final_in.at[dx * NY + dy], device(dx=dx, dy=dy)) for dx, dy in group_xy
    )
    sel_arrived = go_all(
        (sel.at[pl.ds(pl.multiple_of(xat(dx) * per, per), per)], sel_in.at[x], device(dx=dx))
        for dx in (2, 1, 3)
    )
    here = pl.ds(pl.multiple_of(x * per, per), per)
    sel_in[x] = sel[here, :]

    final_arrived()
    last_sum = final_own[...]
    for j in range(1, NX * NY):
        last_sum = last_sum + final_in[j]
    for t in range(2):
        far, mixed, length = (last_sum[3 * t + j : 3 * t + j + 1] for j in range(3))
        many = wrows[t : t + 1, :]
        s = many * lax.rsqrt(many * many * (length / features) + EPS) - 1.0
        value = (far - 2.0 * s * mixed + s * s * length) / features
        value = pltpu.roll(jnp.broadcast_to(value, (8, LANE)), LANE - x * OWN, 1)
        spread_ref[t : t + 1, :] = value[0:1, 0:OWN]
    lens[...] = as_columns(last_sum)
    length = lens[here, 6:7]
    inverse = lax.rsqrt(length / features + EPS)
    first = weight[here, :]
    second = weight[pl.ds(pl.multiple_of(x * per + cents, per), per), :]
    keep = jnp.maximum(first, second) > 0
    sel_arrived()
    for b in range(NX):
        at = slice(b * LANE, (b + 1) * LANE)
        cent_ref[:, at] = jnp.where(keep, sel_in[b] * inverse, init_ref[:, at])

    for wait in sent:
        wait()


COPIES = 7 + 7 + 8 + 18 + 2 + 5 + 8 + 8 + 15 + 15 + 15 + 3


def per_device(features, embeddings, sample_owner, lloyd_assign, init_centroids):
    samples, width = embeddings.shape
    per = init_centroids.shape[0]
    depth = 2048
    f32, bf16 = jnp.float32, jnp.bfloat16
    vm = pltpu.VMEM
    cents = NX * per
    lines = 2 * (cents + ROWS)
    scratch = [
        vm((1, samples), jnp.int32),
        vm((2, OWN), jnp.int32),
        vm((per, width), f32),
        vm((samples, width), bf16),
        vm((NZ, NX, ROWS, LANE), f32),
        vm((NZ, NX, ROWS, LANE), f32),
        vm((NZ, NX, ROWS, LANE), f32),
        vm((NZ, 3, ROWS, LANE), f32),
        vm((2, NX, ROWS, LANE), f32),
        vm((NZ, ROWS, LANE), f32),
        vm((1, samples), jnp.int32),
        vm((8, LANE), f32),
        vm((24, LANE), f32),
        vm((NX * NC, 24, LANE), f32),
        vm((24, LANE), f32),
        vm((NZ, 24, LANE), f32),
        vm((BLOCKS, LANE), f32),
        vm((lines, BLOCKS * LANE), bf16),
        vm((lines, LANE), f32),
        vm((LANE, LANE), f32),
        vm((8, LANE), f32),
        vm((BLOCKS, ROWS, LANE), f32),
        vm((1, 1, LANE), f32),
        vm((NX * NY, 1, LANE), f32),
        vm((BLOCKS, 1, LANE), f32),
        vm((BLOCKS, LANE), f32),
        vm((BLOCKS * LANE, 3 * LANE), bf16),
        vm((8, LANE), f32),
        vm((NX * NY, 8, LANE), f32),
        vm((cents, LANE), f32),
        vm((NX, per, LANE), f32),
        vm((LANE, 8), f32),
        pltpu.SemaphoreType.DMA((samples // depth + 3,)),
        pltpu.SemaphoreType.DMA((COPIES,)),
        pltpu.SemaphoreType.DMA((COPIES,)),
    ]
    in_vmem = pl.BlockSpec(memory_space=pltpu.VMEM)

    def body(*refs):
        kernel(depth, width, features, *refs)

    packed = pl.pallas_call(
        body,
        name="recluster",
        out_shape=(
            jax.ShapeDtypeStruct((per, width), f32),
            jax.ShapeDtypeStruct((2, OWN), f32),
        ),
        in_specs=[pl.BlockSpec(memory_space=pl.ANY)] * 4,
        out_specs=(in_vmem, in_vmem),
        scratch_shapes=scratch,
        compiler_params=pltpu.CompilerParams(
            collective_id=0, has_side_effects=True, vmem_limit_bytes=60 << 20
        ),
    )(sample_owner.reshape(1, samples), lloyd_assign, init_centroids, embeddings)

    def hand_out(cent_in, spread_in, cent_out, spread_out, cent_mid, spread_mid, sem):
        through = ((cent_in, cent_mid, cent_out), (spread_in, spread_mid, spread_out))
        first = [pltpu.make_async_copy(v[0], v[1], sem.at[k]) for k, v in enumerate(through)]
        last = [pltpu.make_async_copy(v[1], v[2], sem.at[2 + k]) for k, v in enumerate(through)]
        for copy in first:
            copy.start()
        for k in range(2):
            first[k].wait()
            last[k].start()
        for copy in last:
            copy.wait()

    anywhere = pl.BlockSpec(memory_space=pl.ANY)
    return pl.pallas_call(
        hand_out,
        name="hand_out",
        out_shape=(
            jax.ShapeDtypeStruct((per, width), f32),
            jax.ShapeDtypeStruct((2, OWN), f32),
        ),
        in_specs=[anywhere] * 2,
        out_specs=(anywhere, anywhere),
        scratch_shapes=[vm((per, width), f32), vm((2, OWN), f32), pltpu.SemaphoreType.DMA((4,))],
    )(*packed)


def solution(mesh):
    def run(embeddings, sample_owner, lloyd_assign, init_centroids):
        features = embeddings.shape[1]
        return jax.shard_map(
            lambda *args: per_device(features, *args),
            mesh=mesh,
            in_specs=(P("dp", "feat"), P("dp"), P(None, "dp"), P("dp", "feat")),
            out_specs=(P("dp", "feat"), P(None, "dp")),
            check_vma=False,
        )(embeddings, sample_owner, lloyd_assign, init_centroids)

    return run
```

```python
import jax
import jax.numpy as jnp
from jax import lax
from jax.experimental import pallas as pl
from jax.experimental.pallas import tpu as pltpu
from jax.sharding import PartitionSpec as P

EPS = 1e-06
MESH = pl.DeviceIdType.MESH

NZ, NX, NC, NY = 8, 4, 2, 4
OWN = 24
ROWS = NX * OWN
BLOCKS = NZ * NC
LANE = 128
ORDER = (4, 3, 1, -1, -3, 2, -2, 0)


def position(owner):
    slab = lax.shift_right_logical(owner * 21846, 22)
    left = owner - slab * (NX * NC * OWN)
    column = lax.shift_right_logical(left * 1366, 16)
    inner = left - column * (NC * OWN)
    core = jnp.where(inner >= OWN, 1, 0)
    block = slab * NC + core
    return block, column * OWN + inner - core * OWN


def as_rows(columns, pad_ref):
    pad_ref[...] = jnp.zeros_like(pad_ref)
    lane = lax.broadcasted_iota(jnp.int32, (ROWS, LANE), 1)
    filled = jnp.zeros((ROWS, LANE), jnp.float32)
    for j, column in enumerate(columns):
        filled = jnp.where(lane == j, column, filled)
    pad_ref[0:ROWS, :] = filled
    return jnp.transpose(pad_ref[...])[0:8, :]


def as_columns(tile):
    return jnp.transpose(tile)


def kernel(
    depth, width, features,
    owner_hbm, assign_hbm, init_hbm, emb_hbm,
    cent_ref, spread_ref,
    owner_ref, assign_ref, init_ref,
    emb, part, other, other_in, xin, zslab, zin,
    prow, tile, info, info_x, group, info_z, counts, match, weight, pad, wrows,
    table, sq_own, sq_in, scale, scale2, scaled, final_own, final_in, sel, sel_in, lens,
    load_sem, send_sem, recv_sem,
):
    dp, y = lax.axis_index("dp"), lax.axis_index("feat")
    z = lax.div(dp, NX * NC)
    x = lax.div(dp - z * (NX * NC), NC)
    c = dp - z * (NX * NC) - x * NC

    def around(at, size):
        steps = [at]
        for d in range(1, size):
            steps.append(jnp.where(at + d >= size, at + (d - size), at + d))
        return steps

    z_at, x_at, c_at, y_at = around(z, NZ), around(x, NX), around(c, NC), around(y, NY)
    z_first = [at * (NX * NC) for at in z_at]
    x_first = [at * NC for at in x_at]

    def zat(d):
        return z_at[d % NZ]

    def xat(d):
        return x_at[d % NX]

    def device(dz=0, dx=0, dc=0, dy=0):
        return (z_first[dz % NZ] + (x_first[dx % NX] + c_at[dc % NC]), y_at[dy % NY])

    used = [0]
    sent = []

    def go(src, dst, to):
        slot = used[0]
        used[0] += 1
        copy = pltpu.make_async_remote_copy(
            src_ref=src, dst_ref=dst, send_sem=send_sem.at[slot], recv_sem=recv_sem.at[slot],
            device_id=to, device_id_type=MESH,
        )
        copy.start()
        sent.append(copy.wait_send)
        return copy

    def go_all(makes):
        copies = [go(*make) for make in makes]

        def wait():
            for copy in copies:
                copy.wait_recv()

        return wait

    group_xc = [(dx, dc) for dx in (2, 1, 3, 0) for dc in range(NC) if (dx, dc) != (0, 0)]
    group_xy = [
        (dx, dy) for dx in (2, 1, 3, 0) for dy in (2, 1, 3, 0) if (dx, dy) != (0, 0)
    ]
    group_zc = [
        (dz, dc) for dz in (4, 3, 5, 2, 6, 1, 7, 0) for dc in range(NC) if (dz, dc) != (0, 0)
    ]

    chunks = emb.shape[0] // depth
    loads = [
        pltpu.make_async_copy(
            emb_hbm.at[pl.ds(k * depth, depth)], emb.at[pl.ds(k * depth, depth)], load_sem.at[k]
        )
        for k in range(chunks)
    ]
    small = [
        pltpu.make_async_copy(src, dst, load_sem.at[chunks + k])
        for k, (src, dst) in enumerate(
            ((owner_hbm, owner_ref), (assign_hbm, assign_ref), (init_hbm, init_ref))
        )
    ]
    for load in small + loads:
        load.start()

    barrier = pltpu.get_barrier_semaphore()

    greeted = {(dz, 0, dc, 0) for dz, dc in group_zc}
    greeted |= {(0, dx, 0, dy) for dx, dy in group_xy} | {(0, dx, dc, 0) for dx, dc in group_xc}
    for steps in sorted(greeted, key=lambda v: (-sum(min(a, b - a) for a, b in zip(v, (NZ, NX, NC, NY))), v)):
        pl.semaphore_signal(barrier, inc=1, device_id=device(*steps), device_id_type=MESH)

    tile[...] = jnp.zeros_like(tile)
    for load in small:
        load.wait()
    block, place = position(owner_ref[...])
    prow[...] = block * ROWS + place

    def count():
        samples = owner_ref.shape[1]
        block, place = position(owner_ref[...])
        high = lax.broadcasted_iota(jnp.int32, (BLOCKS, samples), 0) == block
        low = lax.broadcasted_iota(jnp.int32, (LANE, samples), 0) == place
        info[0:BLOCKS, :] = lax.dot_general(
            jnp.where(high, 1.0, 0.0).astype(jnp.bfloat16),
            jnp.where(low, 1.0, 0.0).astype(jnp.bfloat16),
            (((1,), (1,)), ((), ())), preferred_element_type=jnp.float32,
        )
        tile[0:2, 0:OWN] = assign_ref[...].astype(jnp.float32)
        placed = pltpu.roll(tile[...], x * OWN, 1)
        info[BLOCKS : BLOCKS + 8, :] = jnp.where(c == 0, placed, pltpu.roll(placed, 2, 0))
        info_x[0] = info[...]
        return go_all(
            (info, info_x.at[dx * NC + dc], device(dx=dx, dc=dc)) for dx, dc in group_xc
        )

    def sums(bases, into, start, size):
        row = lax.broadcasted_iota(jnp.int32, (ROWS, size), 0)
        p = prow[:, start : start + size]
        hot = jnp.concatenate(
            [jnp.where(row == p - base, 1.0, 0.0).astype(jnp.bfloat16) for base in bases], 0
        )
        got = jnp.dot(hot, emb[start : start + size, :], preferred_element_type=jnp.float32)
        for j, ref in enumerate(into):
            for b in range(NX):
                new = got[j * ROWS : (j + 1) * ROWS, b * LANE : (b + 1) * LANE]
                ref[b] = new if start == 0 else ref[b] + new

    cross = {}

    def work(s):
        base = zat(ORDER[s]) * (NC * ROWS)
        bases, into = [base + (1 - c) * ROWS, base + c * ROWS], [other.at[s], part.at[s]]
        if s > 0:
            sums(bases, into, 0, chunks * depth)
            return
        for k in range(chunks):
            loads[k].wait()
            sums(bases, into, k * depth, depth)

    def give(s):
        cross[s] = go(other.at[s], other_in.at[s], device(dc=1))

    def meet(s):
        cross[s].wait_recv()
        part[s] += other_in[s]

    xs = {}

    def way_of(s):
        return 1 if s == 1 else -1

    def x_start(s):
        way = way_of(s)
        xs[s, 0] = go(part.at[s, xat(2)], xin.at[s, 0], device(dx=way))
        xs[s, 1] = go(part.at[s, xat(-way)], xin.at[s, 1], device(dx=-way))

    def x_mid(s):
        way = way_of(s)
        xs[s, 0].wait_recv()
        part[s, xat(way)] += xin[s, 0]
        xs[s, 2] = go(part.at[s, xat(way)], xin.at[s, 2], device(dx=way))

    def x_direct(s):
        for k, d in enumerate((2, 1, -1)):
            xs[s, k] = go(part.at[s, xat(d)], xin.at[s, k], device(dx=d))

    zs = {}
    hops = {4: 2, 3: 1}

    def x_end(s):
        d = ORDER[s]
        if (s, 0) in direct:
            xs[s, 0].wait_recv()
        xs[s, 1].wait_recv()
        xs[s, 2].wait_recv()
        total = part[s, x] + xin[s, 1] + xin[s, 2]
        if (s, 0) in direct:
            total = total + xin[s, 0]
        for far in (4, 3) if d == 2 else ():
            zs[far].wait_recv()
            total = total + zin[ORDER.index(far)]
        part[s, x] = total
        if d != 0:
            zs[d] = go(part.at[s, x], zin.at[s], device(dz=hops.get(d, d)))

    direct = {(6, 0)}

    work(0)
    pl.semaphore_wait(barrier, len(greeted))
    give(0)
    arrived = count()

    whole_slab = {}

    def z_whole(s):
        d = ORDER[s]
        whole_slab[s] = go(part.at[s], zslab.at[s - 2], device(dz=d))

    work(1)
    give(1)
    meet(0)
    x_start(0)
    work(2)
    give(2)
    meet(1)
    x_start(1)
    work(3)
    give(3)
    meet(2)
    z_whole(2)
    work(4)
    give(4)
    meet(3)
    z_whole(3)
    x_mid(0)
    arrived()
    whole = info_x[0]
    for j in range(1, NX * NC):
        whole = whole + info_x[j]
    group[...] = whole
    info_z[z] = whole
    arrived_z = go_all(
        (group, info_z.at[z], device(dz=dz)) for dz in (4, 3, 5, 2, 6, 1, 7)
    )
    work(5)
    give(5)
    meet(4)
    x_start(4)
    x_mid(1)
    work(6)
    give(6)
    meet(5)
    x_start(5)
    work(7)
    give(7)
    meet(6)
    x_direct(6)
    x_end(0)
    x_mid(4)
    cross[7].wait_recv()
    whole_slab[2].wait_recv()
    whole_slab[3].wait_recv()
    part[7] += other_in[7] + zslab[0] + zslab[1]
    x_start(7)
    x_end(1)
    x_mid(5)
    x_mid(7)
    x_end(4)
    x_end(6)
    x_end(5)
    x_end(7)
    own = part[7, x]
    for d in (-3, 2, -2):
        zs[d].wait_recv()
        own = own + zin[ORDER.index(d)]

    mine = z * NC + c
    table[mine] = own
    rings, pairs = {}, []

    def blk(dz):
        return zat(dz) * NC + c

    def core_share(dz):
        at = blk(dz)
        pairs.append(go(table.at[at], table.at[at], device(dc=1)))

    square = jnp.sum(own * own, axis=1, keepdims=True)
    sq_own[0] = as_rows([square], pad)[0:1, :]
    sq_arrived = go_all(
        (sq_own.at[0], sq_in.at[dx * NY + dy], device(dx=dx, dy=dy)) for dx, dy in group_xy
    )

    for dz in (2, -2, 1, -1):
        rings[dz] = go(table.at[mine], table.at[mine], device(dz=dz))
    core_share(0)

    arrived_z()
    total = info_z[0, 0:BLOCKS]
    for j in range(1, NZ):
        total = total + info_z[j, 0:BLOCKS]
    counts[...] = total

    scaled[...] = jnp.zeros_like(scaled)

    half = ROWS // 2
    for way in (1, -1):
        rings[2 * way].wait_recv()
        at = blk(-2 * way)
        rings[3 * way] = go(table.at[at], table.at[at], device(dz=way))
        rows = pl.ds(0 if way > 0 else half, half)
        rings[4 * way] = go(table.at[at, rows], table.at[at, rows], device(dz=2 * way))
        core_share(-2 * way)
    for way in (1, -1):
        rings[way].wait_recv()
        core_share(-way)

    sq_arrived()
    square_row = sq_own[0]
    for j in range(1, NX * NY):
        square_row = square_row + sq_in[j]
    inverse = lax.rsqrt(square_row / features + EPS)
    scale[mine] = inverse
    scale_arrived = go_all(
        (scale.at[mine], scale.at[mine], device(dz=dz, dc=dc)) for dz, dc in group_zc
    )
    means = own * as_columns(jnp.broadcast_to(inverse, (8, LANE)))[0:ROWS, 0:1]

    keys_all = group[BLOCKS : BLOCKS + 8, :]
    keys = as_columns(jnp.where(c == 0, keys_all, pltpu.roll(keys_all, 6, 0)))
    cents = NX * cent_ref.shape[0]
    r = lax.broadcasted_iota(jnp.int32, (cents, LANE), 0)
    per = cent_ref.shape[0]
    r = z * (cents * NC) + lax.div(r, per) * (per * NC) + c * per + lax.rem(r, per)
    cent_key = r.astype(jnp.float32)
    spread_key = [jnp.broadcast_to(keys[0:ROWS, t : t + 1], (ROWS, LANE)) for t in range(2)]
    parts = [
        (0, cents, cent_key, 0), (cents, cents, cent_key, 1),
        (2 * cents, ROWS, spread_key[0], 0), (2 * cents + ROWS, ROWS, spread_key[1], 1),
    ]
    weight[...] = jnp.zeros_like(weight)
    for b in range(BLOCKS):
        many = counts[b : b + 1, :]
        for at, n, key, t in parts:
            line = BLOCKS + 2 * (b % NC) + t
            same = jnp.where(key == info_z[b // NC, line : line + 1, :], 1.0, 0.0)
            match[at : at + n, b * LANE : (b + 1) * LANE] = same.astype(jnp.bfloat16)
            weight[at : at + n, :] += same * many
    summed = jnp.sum(weight[...], axis=1, keepdims=True)
    weight[...] = jnp.broadcast_to(summed, weight.shape)
    first_row = 2 * cents
    wrows[...] = as_rows(
        [summed[first_row : first_row + ROWS], summed[first_row + ROWS : first_row + 2 * ROWS]], pad
    )

    for way in (1, -1):
        rings[3 * way].wait_recv()
        core_share(-3 * way)
    rings[4].wait_recv()
    rings[-4].wait_recv()
    core_share(4)

    scale_arrived()
    for b in range(BLOCKS):
        scale2[b : b + 1, :] = scale[b]
    factor = as_columns(counts[...] * scale2[...])
    for pair in pairs:
        pair.wait_recv()
    for b in range(BLOCKS):
        rows = table[b] * factor[0:ROWS, b : b + 1]
        for piece in range(3):
            near = rows.astype(jnp.bfloat16)
            scaled[b * LANE : b * LANE + ROWS, piece * LANE : (piece + 1) * LANE] = near
            rows = rows - near.astype(jnp.float32)
    tot = jnp.dot(match[...], scaled[...], preferred_element_type=jnp.float32)
    tot = tot[:, 0:LANE] + (tot[:, LANE : 2 * LANE] + tot[:, 2 * LANE : 3 * LANE])

    columns = []
    for t in range(2):
        at = first_row + t * ROWS
        many = weight[at : at + ROWS, :]
        g = tot[at : at + ROWS] * jnp.where(many > 0, 1.0 / jnp.maximum(many, 1.0), 0.0)
        d = means - g
        for v in (d * d, d * g, g * g):
            columns.append(jnp.sum(v, axis=1, keepdims=True))
    chosen = jnp.where(weight[cents : 2 * cents, :] > 0, tot[cents : 2 * cents], tot[0:cents])
    sel[...] = chosen
    squares = jnp.sum(chosen * chosen, axis=1, keepdims=True)
    columns.append(jnp.concatenate([squares, jnp.zeros((ROWS - cents, 1), jnp.float32)], 0))
    final_own[...] = as_rows(columns, pad)
    final_arrived = go_all(
        (final_own, final_in.at[dx * NY + dy], device(dx=dx, dy=dy)) for dx, dy in group_xy
    )
    sel_arrived = go_all(
        (sel.at[pl.ds(pl.multiple_of(xat(dx) * per, per), per)], sel_in.at[x], device(dx=dx))
        for dx in (2, 1, 3)
    )
    here = pl.ds(pl.multiple_of(x * per, per), per)
    sel_in[x] = sel[here, :]

    final_arrived()
    last_sum = final_own[...]
    for j in range(1, NX * NY):
        last_sum = last_sum + final_in[j]
    for t in range(2):
        far, mixed, length = (last_sum[3 * t + j : 3 * t + j + 1] for j in range(3))
        many = wrows[t : t + 1, :]
        s = many * lax.rsqrt(many * many * (length / features) + EPS) - 1.0
        value = (far - 2.0 * s * mixed + s * s * length) / features
        value = pltpu.roll(jnp.broadcast_to(value, (8, LANE)), LANE - x * OWN, 1)
        spread_ref[t : t + 1, :] = value[0:1, 0:OWN]
    lens[...] = as_columns(last_sum)
    length = lens[here, 6:7]
    inverse = lax.rsqrt(length / features + EPS)
    first = weight[here, :]
    second = weight[pl.ds(pl.multiple_of(x * per + cents, per), per), :]
    keep = jnp.maximum(first, second) > 0
    sel_arrived()
    for b in range(NX):
        at = slice(b * LANE, (b + 1) * LANE)
        cent_ref[:, at] = jnp.where(keep, sel_in[b] * inverse, init_ref[:, at])

    for wait in sent:
        wait()


COPIES = 7 + 7 + 8 + 18 + 2 + 5 + 8 + 8 + 15 + 15 + 15 + 3


def per_device(features, embeddings, sample_owner, lloyd_assign, init_centroids):
    samples, width = embeddings.shape
    per = init_centroids.shape[0]
    depth = 1024
    f32, bf16 = jnp.float32, jnp.bfloat16
    vm = pltpu.VMEM
    cents = NX * per
    lines = 2 * (cents + ROWS)
    scratch = [
        vm((1, samples), jnp.int32),
        vm((2, OWN), jnp.int32),
        vm((per, width), f32),
        vm((samples, width), bf16),
        vm((NZ, NX, ROWS, LANE), f32),
        vm((NZ, NX, ROWS, LANE), f32),
        vm((NZ, NX, ROWS, LANE), f32),
        vm((NZ, 3, ROWS, LANE), f32),
        vm((2, NX, ROWS, LANE), f32),
        vm((NZ, ROWS, LANE), f32),
        vm((1, samples), jnp.int32),
        vm((8, LANE), f32),
        vm((24, LANE), f32),
        vm((NX * NC, 24, LANE), f32),
        vm((24, LANE), f32),
        vm((NZ, 24, LANE), f32),
        vm((BLOCKS, LANE), f32),
        vm((lines, BLOCKS * LANE), bf16),
        vm((lines, LANE), f32),
        vm((LANE, LANE), f32),
        vm((8, LANE), f32),
        vm((BLOCKS, ROWS, LANE), f32),
        vm((1, 1, LANE), f32),
        vm((NX * NY, 1, LANE), f32),
        vm((BLOCKS, 1, LANE), f32),
        vm((BLOCKS, LANE), f32),
        vm((BLOCKS * LANE, 3 * LANE), bf16),
        vm((8, LANE), f32),
        vm((NX * NY, 8, LANE), f32),
        vm((cents, LANE), f32),
        vm((NX, per, LANE), f32),
        vm((LANE, 8), f32),
        pltpu.SemaphoreType.DMA((samples // depth + 3,)),
        pltpu.SemaphoreType.DMA((COPIES,)),
        pltpu.SemaphoreType.DMA((COPIES,)),
    ]
    in_vmem = pl.BlockSpec(memory_space=pltpu.VMEM)

    def body(*refs):
        kernel(depth, width, features, *refs)

    packed = pl.pallas_call(
        body,
        name="recluster",
        out_shape=(
            jax.ShapeDtypeStruct((per, width), f32),
            jax.ShapeDtypeStruct((2, OWN), f32),
        ),
        in_specs=[pl.BlockSpec(memory_space=pl.ANY)] * 4,
        out_specs=(in_vmem, in_vmem),
        scratch_shapes=scratch,
        compiler_params=pltpu.CompilerParams(
            collective_id=0, has_side_effects=True, vmem_limit_bytes=60 << 20
        ),
    )(sample_owner.reshape(1, samples), lloyd_assign, init_centroids, embeddings)

    def hand_out(cent_in, spread_in, cent_out, spread_out, cent_mid, spread_mid, sem):
        through = ((cent_in, cent_mid, cent_out), (spread_in, spread_mid, spread_out))
        first = [pltpu.make_async_copy(v[0], v[1], sem.at[k]) for k, v in enumerate(through)]
        last = [pltpu.make_async_copy(v[1], v[2], sem.at[2 + k]) for k, v in enumerate(through)]
        for copy in first:
            copy.start()
        for k in range(2):
            first[k].wait()
            last[k].start()
        for copy in last:
            copy.wait()

    anywhere = pl.BlockSpec(memory_space=pl.ANY)
    return pl.pallas_call(
        hand_out,
        name="hand_out",
        out_shape=(
            jax.ShapeDtypeStruct((per, width), f32),
            jax.ShapeDtypeStruct((2, OWN), f32),
        ),
        in_specs=[anywhere] * 2,
        out_specs=(anywhere, anywhere),
        scratch_shapes=[vm((per, width), f32), vm((2, OWN), f32), pltpu.SemaphoreType.DMA((4,))],
    )(*packed)


def solution(mesh):
    def run(embeddings, sample_owner, lloyd_assign, init_centroids):
        features = embeddings.shape[1]
        return jax.shard_map(
            lambda *args: per_device(features, *args),
            mesh=mesh,
            in_specs=(P("dp", "feat"), P("dp"), P(None, "dp"), P("dp", "feat")),
            out_specs=(P("dp", "feat"), P(None, "dp")),
            check_vma=False,
        )(embeddings, sample_owner, lloyd_assign, init_centroids)

    return run
```

```python
import jax
import jax.numpy as jnp
from jax import lax
from jax.experimental import pallas as pl
from jax.experimental.pallas import tpu as pltpu
from jax.sharding import PartitionSpec as P

EPS = 1e-06
MESH = pl.DeviceIdType.MESH

NZ, NX, NC, NY = 8, 4, 2, 4
OWN = 24
ROWS = NX * OWN
BLOCKS = NZ * NC
LANE = 128
ORDER = (4, 3, 1, -1, -3, 2, -2, 0)


def position(owner):
    slab = lax.shift_right_logical(owner * 21846, 22)
    left = owner - slab * (NX * NC * OWN)
    column = lax.shift_right_logical(left * 1366, 16)
    inner = left - column * (NC * OWN)
    core = jnp.where(inner >= OWN, 1, 0)
    block = slab * NC + core
    return block, column * OWN + inner - core * OWN


def as_rows(columns, pad_ref):
    pad_ref[...] = jnp.zeros_like(pad_ref)
    lane = lax.broadcasted_iota(jnp.int32, (ROWS, LANE), 1)
    filled = jnp.zeros((ROWS, LANE), jnp.float32)
    for j, column in enumerate(columns):
        filled = jnp.where(lane == j, column, filled)
    pad_ref[0:ROWS, :] = filled
    return jnp.transpose(pad_ref[...])[0:8, :]


def as_columns(tile):
    return jnp.transpose(tile)


def kernel(
    depth, width, features,
    owner_hbm, assign_hbm, init_hbm, emb_hbm,
    cent_ref, spread_ref,
    owner_ref, assign_ref, init_ref,
    emb, part, other, other_in, xin, zslab, zin,
    prow, tile, info, info_x, both, group, info_z, counts, match, weight, pad, wrows,
    table, sq_own, sq_in, scale, scale2, scaled, final_own, final_in, sel, sel_in, lens,
    load_sem, send_sem, recv_sem,
):
    dp, y = lax.axis_index("dp"), lax.axis_index("feat")
    z = lax.div(dp, NX * NC)
    x = lax.div(dp - z * (NX * NC), NC)
    c = dp - z * (NX * NC) - x * NC

    def around(at, size):
        steps = [at]
        for d in range(1, size):
            steps.append(jnp.where(at + d >= size, at + (d - size), at + d))
        return steps

    z_at, x_at, c_at, y_at = around(z, NZ), around(x, NX), around(c, NC), around(y, NY)
    z_first = [at * (NX * NC) for at in z_at]
    x_first = [at * NC for at in x_at]

    def zat(d):
        return z_at[d % NZ]

    def xat(d):
        return x_at[d % NX]

    def device(dz=0, dx=0, dc=0, dy=0):
        return (z_first[dz % NZ] + (x_first[dx % NX] + c_at[dc % NC]), y_at[dy % NY])

    used = [0]
    sent = []

    def go(src, dst, to):
        slot = used[0]
        used[0] += 1
        copy = pltpu.make_async_remote_copy(
            src_ref=src, dst_ref=dst, send_sem=send_sem.at[slot], recv_sem=recv_sem.at[slot],
            device_id=to, device_id_type=MESH,
        )
        copy.start()
        sent.append(copy.wait_send)
        return copy

    def go_all(makes):
        copies = [go(*make) for make in makes]

        def wait():
            for copy in copies:
                copy.wait_recv()

        return wait

    group_xy = [
        (dx, dy) for dx in (2, 1, 3, 0) for dy in (2, 1, 3, 0) if (dx, dy) != (0, 0)
    ]
    group_zc = [
        (dz, dc) for dz in (4, 3, 5, 2, 6, 1, 7, 0) for dc in range(NC) if (dz, dc) != (0, 0)
    ]

    chunks = emb.shape[0] // depth
    loads = [
        pltpu.make_async_copy(
            emb_hbm.at[pl.ds(k * depth, depth)], emb.at[pl.ds(k * depth, depth)], load_sem.at[k]
        )
        for k in range(chunks)
    ]
    small = [
        pltpu.make_async_copy(src, dst, load_sem.at[chunks + k])
        for k, (src, dst) in enumerate(
            ((owner_hbm, owner_ref), (assign_hbm, assign_ref), (init_hbm, init_ref))
        )
    ]
    for load in small + loads:
        load.start()

    barrier = pltpu.get_barrier_semaphore()

    greeted = {(dz, 0, dc, 0) for dz, dc in group_zc}
    greeted |= {(0, dx, 0, dy) for dx, dy in group_xy}
    for steps in sorted(greeted, key=lambda v: (-sum(min(a, b - a) for a, b in zip(v, (NZ, NX, NC, NY))), v)):
        pl.semaphore_signal(barrier, inc=1, device_id=device(*steps), device_id_type=MESH)

    tile[...] = jnp.zeros_like(tile)
    part[...] = jnp.zeros_like(part)
    other[...] = jnp.zeros_like(other)
    for load in small:
        load.wait()
    block, place = position(owner_ref[...])
    prow[...] = block * ROWS + place

    def count():
        samples = owner_ref.shape[1]
        block, place = position(owner_ref[...])
        high = lax.broadcasted_iota(jnp.int32, (BLOCKS, samples), 0) == block
        low = lax.broadcasted_iota(jnp.int32, (LANE, samples), 0) == place
        info[0:BLOCKS, :] = lax.dot_general(
            jnp.where(high, 1.0, 0.0).astype(jnp.bfloat16),
            jnp.where(low, 1.0, 0.0).astype(jnp.bfloat16),
            (((1,), (1,)), ((), ())), preferred_element_type=jnp.float32,
        )
        tile[0:2, 0:OWN] = assign_ref[...].astype(jnp.float32)
        placed = pltpu.roll(tile[...], x * OWN, 1)
        info[BLOCKS : BLOCKS + 8, :] = jnp.where(c == 0, placed, pltpu.roll(placed, 2, 0))
        return go(info, info_x.at[NX], device(dc=1))

    def sums(bases, into, waits=()):
        row = lax.broadcasted_iota(jnp.int32, (ROWS, depth), 0)

        def step(k):
            at = pl.ds(pl.multiple_of(k * depth, depth), depth)
            p = prow[:, at]
            hot = jnp.concatenate(
                [jnp.where(row == p - base, 1.0, 0.0).astype(jnp.bfloat16) for base in bases], 0
            )
            got = jnp.dot(hot, emb[at, :], preferred_element_type=jnp.float32)
            for j, ref in enumerate(into):
                for b in range(NX):
                    ref[b] += got[j * ROWS : (j + 1) * ROWS, b * LANE : (b + 1) * LANE]

        if waits:
            for k in range(chunks):
                waits[k].wait()
                step(k)
        else:
            lax.fori_loop(0, chunks, lambda k, carry: (step(k), carry)[1], 0)

    cross = {}

    def work(*slabs):
        bases, into = [], []
        for s in slabs:
            base = zat(ORDER[s]) * (NC * ROWS)
            bases += [base + (1 - c) * ROWS, base + c * ROWS]
            into += [other.at[s], part.at[s]]
        sums(bases, into, loads if 0 in slabs else ())

    def give(s):
        cross[s] = go(other.at[s], other_in.at[s], device(dc=1))

    def meet(s):
        cross[s].wait_recv()
        part[s] += other_in[s]

    xs = {}

    def way_of(s):
        return 1 if s == 1 else -1

    def x_start(s):
        way = way_of(s)
        xs[s, 0] = go(part.at[s, xat(2)], xin.at[s, 0], device(dx=way))
        xs[s, 1] = go(part.at[s, xat(-way)], xin.at[s, 1], device(dx=-way))

    def x_mid(s):
        way = way_of(s)
        xs[s, 0].wait_recv()
        part[s, xat(way)] += xin[s, 0]
        xs[s, 2] = go(part.at[s, xat(way)], xin.at[s, 2], device(dx=way))

    def x_direct(s):
        for k, d in enumerate((2, 1, -1)):
            xs[s, k] = go(part.at[s, xat(d)], xin.at[s, k], device(dx=d))

    zs = {}
    hops = {4: 2, 3: 1}

    def x_end(s):
        d = ORDER[s]
        if (s, 0) in direct:
            xs[s, 0].wait_recv()
        xs[s, 1].wait_recv()
        xs[s, 2].wait_recv()
        total = part[s, x] + xin[s, 1] + xin[s, 2]
        if (s, 0) in direct:
            total = total + xin[s, 0]
        for far in (4, 3) if d == 2 else ():
            zs[far].wait_recv()
            total = total + zin[ORDER.index(far)]
        part[s, x] = total
        if d != 0:
            zs[d] = go(part.at[s, x], zin.at[s], device(dz=hops.get(d, d)))

    direct = {(6, 0)}

    work(0)
    pl.semaphore_wait(barrier, len(greeted))
    give(0)
    arrived = count()

    whole_slab = {}

    def z_whole(s):
        d = ORDER[s]
        whole_slab[s] = go(part.at[s], zslab.at[s - 2], device(dz=d))

    work(1)
    give(1)
    meet(0)
    x_start(0)
    work(2)
    give(2)
    meet(1)
    x_start(1)
    arrived.wait_recv()
    both[...] = info[...] + info_x[NX]
    arrived = go_all((both, info_x.at[dx], device(dx=dx)) for dx in (2, 1, 3))
    work(3)
    give(3)
    meet(2)
    z_whole(2)
    work(4)
    give(4)
    meet(3)
    z_whole(3)
    x_mid(0)
    work(5)
    give(5)
    meet(4)
    x_start(4)
    x_mid(1)
    work(6)
    give(6)
    meet(5)
    x_start(5)
    work(7)
    give(7)
    meet(6)
    x_direct(6)
    x_end(0)
    x_mid(4)
    cross[7].wait_recv()
    whole_slab[2].wait_recv()
    whole_slab[3].wait_recv()
    part[7] += other_in[7] + zslab[0] + zslab[1]
    x_start(7)
    x_end(1)
    x_mid(5)
    x_mid(7)
    x_end(4)
    x_end(6)
    x_end(5)
    arrived()
    whole = both[...] + info_x[1] + info_x[2] + info_x[3]
    group[...] = whole
    info_z[z] = whole
    arrived_z = go_all(
        (group, info_z.at[z], device(dz=dz)) for dz in (4, 3, 5, 2, 6, 1, 7)
    )
    x_end(7)
    own = part[7, x]
    for d in (-3, 2, -2):
        zs[d].wait_recv()
        own = own + zin[ORDER.index(d)]

    mine = z * NC + c
    table[mine] = own
    rings, pairs = {}, []

    def blk(dz):
        return zat(dz) * NC + c

    def core_share(dz):
        at = blk(dz)
        pairs.append(go(table.at[at], table.at[at], device(dc=1)))

    square = jnp.sum(own * own, axis=1, keepdims=True)
    sq_own[0] = as_rows([square], pad)[0:1, :]
    sq_arrived = go_all(
        (sq_own.at[0], sq_in.at[dx * NY + dy], device(dx=dx, dy=dy)) for dx, dy in group_xy
    )

    for dz in (2, -2, 1, -1):
        rings[dz] = go(table.at[mine], table.at[mine], device(dz=dz))
    core_share(0)

    scaled[...] = jnp.zeros_like(scaled)

    half = ROWS // 2
    for way in (1, -1):
        rings[2 * way].wait_recv()
        at = blk(-2 * way)
        rings[3 * way] = go(table.at[at], table.at[at], device(dz=way))
        rows = pl.ds(0 if way > 0 else half, half)
        rings[4 * way] = go(table.at[at, rows], table.at[at, rows], device(dz=2 * way))
        core_share(-2 * way)
    for way in (1, -1):
        rings[way].wait_recv()
        core_share(-way)

    sq_arrived()
    square_row = sq_own[0]
    for j in range(1, NX * NY):
        square_row = square_row + sq_in[j]
    inverse = lax.rsqrt(square_row / features + EPS)
    scale[mine] = inverse
    scale_arrived = go_all(
        (scale.at[mine], scale.at[mine], device(dz=dz, dc=dc)) for dz, dc in group_zc
    )
    means = own * as_columns(jnp.broadcast_to(inverse, (8, LANE)))[0:ROWS, 0:1]

    arrived_z()
    total = info_z[0, 0:BLOCKS]
    for j in range(1, NZ):
        total = total + info_z[j, 0:BLOCKS]
    counts[...] = total

    keys_all = group[BLOCKS : BLOCKS + 8, :]
    keys = as_columns(jnp.where(c == 0, keys_all, pltpu.roll(keys_all, 6, 0)))
    cents = NX * cent_ref.shape[0]
    r = lax.broadcasted_iota(jnp.int32, (cents, LANE), 0)
    per = cent_ref.shape[0]
    r = z * (cents * NC) + lax.div(r, per) * (per * NC) + c * per + lax.rem(r, per)
    cent_key = r.astype(jnp.float32)
    spread_key = [jnp.broadcast_to(keys[0:ROWS, t : t + 1], (ROWS, LANE)) for t in range(2)]
    parts = [
        (0, cents, cent_key, 0), (cents, cents, cent_key, 1),
        (2 * cents, ROWS, spread_key[0], 0), (2 * cents + ROWS, ROWS, spread_key[1], 1),
    ]
    weight[...] = jnp.zeros_like(weight)
    for b in range(BLOCKS):
        many = counts[b : b + 1, :]
        for at, n, key, t in parts:
            line = BLOCKS + 2 * (b % NC) + t
            same = jnp.where(key == info_z[b // NC, line : line + 1, :], 1.0, 0.0)
            match[at : at + n, b * LANE : (b + 1) * LANE] = same.astype(jnp.bfloat16)
            weight[at : at + n, :] += same * many
    summed = jnp.sum(weight[...], axis=1, keepdims=True)
    weight[...] = jnp.broadcast_to(summed, weight.shape)
    first_row = 2 * cents
    wrows[...] = as_rows(
        [summed[first_row : first_row + ROWS], summed[first_row + ROWS : first_row + 2 * ROWS]], pad
    )

    for way in (1, -1):
        rings[3 * way].wait_recv()
        core_share(-3 * way)
    rings[4].wait_recv()
    rings[-4].wait_recv()
    core_share(4)

    scale_arrived()
    for b in range(BLOCKS):
        scale2[b : b + 1, :] = scale[b]
    factor = as_columns(counts[...] * scale2[...])
    for pair in pairs:
        pair.wait_recv()
    for b in range(BLOCKS):
        rows = table[b] * factor[0:ROWS, b : b + 1]
        for piece in range(3):
            near = rows.astype(jnp.bfloat16)
            scaled[b * LANE : b * LANE + ROWS, piece * LANE : (piece + 1) * LANE] = near
            rows = rows - near.astype(jnp.float32)
    tot = jnp.dot(match[...], scaled[...], preferred_element_type=jnp.float32)
    tot = tot[:, 0:LANE] + (tot[:, LANE : 2 * LANE] + tot[:, 2 * LANE : 3 * LANE])

    columns = []
    for t in range(2):
        at = first_row + t * ROWS
        many = weight[at : at + ROWS, :]
        g = tot[at : at + ROWS] * jnp.where(many > 0, 1.0 / jnp.maximum(many, 1.0), 0.0)
        d = means - g
        for v in (d * d, d * g, g * g):
            columns.append(jnp.sum(v, axis=1, keepdims=True))
    chosen = jnp.where(weight[cents : 2 * cents, :] > 0, tot[cents : 2 * cents], tot[0:cents])
    sel[...] = chosen
    squares = jnp.sum(chosen * chosen, axis=1, keepdims=True)
    columns.append(jnp.concatenate([squares, jnp.zeros((ROWS - cents, 1), jnp.float32)], 0))
    final_own[...] = as_rows(columns, pad)
    final_arrived = go_all(
        (final_own, final_in.at[dx * NY + dy], device(dx=dx, dy=dy)) for dx, dy in group_xy
    )
    sel_arrived = go_all(
        (sel.at[pl.ds(pl.multiple_of(xat(dx) * per, per), per)], sel_in.at[x], device(dx=dx))
        for dx in (2, 1, 3)
    )
    here = pl.ds(pl.multiple_of(x * per, per), per)
    sel_in[x] = sel[here, :]

    final_arrived()
    last_sum = final_own[...]
    for j in range(1, NX * NY):
        last_sum = last_sum + final_in[j]
    for t in range(2):
        far, mixed, length = (last_sum[3 * t + j : 3 * t + j + 1] for j in range(3))
        many = wrows[t : t + 1, :]
        s = many * lax.rsqrt(many * many * (length / features) + EPS) - 1.0
        value = (far - 2.0 * s * mixed + s * s * length) / features
        value = pltpu.roll(jnp.broadcast_to(value, (8, LANE)), LANE - x * OWN, 1)
        spread_ref[t : t + 1, :] = value[0:1, 0:OWN]
    lens[...] = as_columns(last_sum)
    length = lens[here, 6:7]
    inverse = lax.rsqrt(length / features + EPS)
    first = weight[here, :]
    second = weight[pl.ds(pl.multiple_of(x * per + cents, per), per), :]
    keep = jnp.maximum(first, second) > 0
    sel_arrived()
    for b in range(NX):
        at = slice(b * LANE, (b + 1) * LANE)
        cent_ref[:, at] = jnp.where(keep, sel_in[b] * inverse, init_ref[:, at])

    for wait in sent:
        wait()


COPIES = 4 + 7 + 8 + 18 + 2 + 5 + 8 + 8 + 15 + 15 + 15 + 3


def per_device(features, embeddings, sample_owner, lloyd_assign, init_centroids):
    samples, width = embeddings.shape
    per = init_centroids.shape[0]
    depth = 2048
    f32, bf16 = jnp.float32, jnp.bfloat16
    vm = pltpu.VMEM
    cents = NX * per
    lines = 2 * (cents + ROWS)
    scratch = [
        vm((1, samples), jnp.int32),
        vm((2, OWN), jnp.int32),
        vm((per, width), f32),
        vm((samples, width), bf16),
        vm((NZ, NX, ROWS, LANE), f32),
        vm((NZ, NX, ROWS, LANE), f32),
        vm((NZ, NX, ROWS, LANE), f32),
        vm((NZ, 3, ROWS, LANE), f32),
        vm((2, NX, ROWS, LANE), f32),
        vm((NZ, ROWS, LANE), f32),
        vm((1, samples), jnp.int32),
        vm((8, LANE), f32),
        vm((24, LANE), f32),
        vm((NX + 1, 24, LANE), f32),
        vm((24, LANE), f32),
        vm((24, LANE), f32),
        vm((NZ, 24, LANE), f32),
        vm((BLOCKS, LANE), f32),
        vm((lines, BLOCKS * LANE), bf16),
        vm((lines, LANE), f32),
        vm((LANE, LANE), f32),
        vm((8, LANE), f32),
        vm((BLOCKS, ROWS, LANE), f32),
        vm((1, 1, LANE), f32),
        vm((NX * NY, 1, LANE), f32),
        vm((BLOCKS, 1, LANE), f32),
        vm((BLOCKS, LANE), f32),
        vm((BLOCKS * LANE, 3 * LANE), bf16),
        vm((8, LANE), f32),
        vm((NX * NY, 8, LANE), f32),
        vm((cents, LANE), f32),
        vm((NX, per, LANE), f32),
        vm((LANE, 8), f32),
        pltpu.SemaphoreType.DMA((samples // depth + 3,)),
        pltpu.SemaphoreType.DMA((COPIES,)),
        pltpu.SemaphoreType.DMA((COPIES,)),
    ]
    in_vmem = pl.BlockSpec(memory_space=pltpu.VMEM)

    def body(*refs):
        kernel(depth, width, features, *refs)

    packed = pl.pallas_call(
        body,
        name="recluster",
        out_shape=(
            jax.ShapeDtypeStruct((per, width), f32),
            jax.ShapeDtypeStruct((2, OWN), f32),
        ),
        in_specs=[pl.BlockSpec(memory_space=pl.ANY)] * 4,
        out_specs=(in_vmem, in_vmem),
        scratch_shapes=scratch,
        compiler_params=pltpu.CompilerParams(
            collective_id=0, has_side_effects=True, vmem_limit_bytes=60 << 20
        ),
    )(sample_owner.reshape(1, samples), lloyd_assign, init_centroids, embeddings)

    def hand_out(cent_in, spread_in, cent_out, spread_out, cent_mid, spread_mid, sem):
        through = ((cent_in, cent_mid, cent_out), (spread_in, spread_mid, spread_out))
        first = [pltpu.make_async_copy(v[0], v[1], sem.at[k]) for k, v in enumerate(through)]
        last = [pltpu.make_async_copy(v[1], v[2], sem.at[2 + k]) for k, v in enumerate(through)]
        for copy in first:
            copy.start()
        for k in range(2):
            first[k].wait()
            last[k].start()
        for copy in last:
            copy.wait()

    anywhere = pl.BlockSpec(memory_space=pl.ANY)
    return pl.pallas_call(
        hand_out,
        name="hand_out",
        out_shape=(
            jax.ShapeDtypeStruct((per, width), f32),
            jax.ShapeDtypeStruct((2, OWN), f32),
        ),
        in_specs=[anywhere] * 2,
        out_specs=(anywhere, anywhere),
        scratch_shapes=[vm((per, width), f32), vm((2, OWN), f32), pltpu.SemaphoreType.DMA((4,))],
    )(*packed)


def solution(mesh):
    def run(embeddings, sample_owner, lloyd_assign, init_centroids):
        features = embeddings.shape[1]
        return jax.shard_map(
            lambda *args: per_device(features, *args),
            mesh=mesh,
            in_specs=(P("dp", "feat"), P("dp"), P(None, "dp"), P("dp", "feat")),
            out_specs=(P("dp", "feat"), P(None, "dp")),
            check_vma=False,
        )(embeddings, sample_owner, lloyd_assign, init_centroids)

    return run
```

```python
import jax
import jax.numpy as jnp
from jax import lax
from jax.experimental import pallas as pl
from jax.experimental.pallas import tpu as pltpu
from jax.sharding import PartitionSpec as P

EPS = 1e-06
MESH = pl.DeviceIdType.MESH

NZ, NX, NC, NY = 8, 4, 2, 4
OWN = 24
ROWS = NX * OWN
BLOCKS = NZ * NC
LANE = 128
ORDER = (4, 3, 1, -1, -3, 2, -2, 0)


def position(owner):
    slab = lax.shift_right_logical(owner * 21846, 22)
    left = owner - slab * (NX * NC * OWN)
    column = lax.shift_right_logical(left * 1366, 16)
    inner = left - column * (NC * OWN)
    core = jnp.where(inner >= OWN, 1, 0)
    block = slab * NC + core
    return block, column * OWN + inner - core * OWN


def as_rows(columns, pad_ref):
    pad_ref[...] = jnp.zeros_like(pad_ref)
    lane = lax.broadcasted_iota(jnp.int32, (ROWS, LANE), 1)
    filled = jnp.zeros((ROWS, LANE), jnp.float32)
    for j, column in enumerate(columns):
        filled = jnp.where(lane == j, column, filled)
    pad_ref[0:ROWS, :] = filled
    return jnp.transpose(pad_ref[...])[0:8, :]


def as_columns(tile):
    return jnp.transpose(tile)


def kernel(
    depth, width, features,
    owner_hbm, assign_hbm, init_hbm, emb_hbm,
    cent_ref, spread_ref,
    owner_ref, assign_ref, init_ref,
    emb, part, other, other_in, xin, zslab, zin,
    prow, tile, info, info_x, group, info_z, counts, match, weight, pad, wrows,
    table, sq_own, sq_in, scale, scale2, scaled, final_own, final_in, sel, sel_in, lens,
    load_sem, send_sem, recv_sem,
):
    dp, y = lax.axis_index("dp"), lax.axis_index("feat")
    z = lax.div(dp, NX * NC)
    x = lax.div(dp - z * (NX * NC), NC)
    c = dp - z * (NX * NC) - x * NC

    def around(at, size):
        steps = [at]
        for d in range(1, size):
            steps.append(jnp.where(at + d >= size, at + (d - size), at + d))
        return steps

    z_at, x_at, c_at, y_at = around(z, NZ), around(x, NX), around(c, NC), around(y, NY)
    z_first = [at * (NX * NC) for at in z_at]
    x_first = [at * NC for at in x_at]

    def zat(d):
        return z_at[d % NZ]

    def xat(d):
        return x_at[d % NX]

    def device(dz=0, dx=0, dc=0, dy=0):
        return (z_first[dz % NZ] + (x_first[dx % NX] + c_at[dc % NC]), y_at[dy % NY])

    used = [0]
    sent = []

    def go(src, dst, to):
        slot = used[0]
        used[0] += 1
        copy = pltpu.make_async_remote_copy(
            src_ref=src, dst_ref=dst, send_sem=send_sem.at[slot], recv_sem=recv_sem.at[slot],
            device_id=to, device_id_type=MESH,
        )
        copy.start()
        sent.append(copy.wait_send)
        return copy

    def go_all(makes):
        copies = [go(*make) for make in makes]

        def wait():
            for copy in copies:
                copy.wait_recv()

        return wait

    group_xc = [(dx, dc) for dx in (2, 1, 3, 0) for dc in range(NC) if (dx, dc) != (0, 0)]
    group_xy = [
        (dx, dy) for dx in (2, 1, 3, 0) for dy in (2, 1, 3, 0) if (dx, dy) != (0, 0)
    ]
    group_zc = [
        (dz, dc) for dz in (4, 3, 5, 2, 6, 1, 7, 0) for dc in range(NC) if (dz, dc) != (0, 0)
    ]

    chunks = emb.shape[0] // depth
    loads = [
        pltpu.make_async_copy(
            emb_hbm.at[pl.ds(k * depth, depth)], emb.at[pl.ds(k * depth, depth)], load_sem.at[k]
        )
        for k in range(chunks)
    ]
    small = [
        pltpu.make_async_copy(src, dst, load_sem.at[chunks + k])
        for k, (src, dst) in enumerate(
            ((owner_hbm, owner_ref), (assign_hbm, assign_ref), (init_hbm, init_ref))
        )
    ]
    for load in small + loads:
        load.start()

    barrier = pltpu.get_barrier_semaphore()

    greeted = {(dz, 0, dc, 0) for dz, dc in group_zc}
    greeted |= {(0, dx, 0, dy) for dx, dy in group_xy} | {(0, dx, dc, 0) for dx, dc in group_xc}
    for steps in sorted(greeted, key=lambda v: (-sum(min(a, b - a) for a, b in zip(v, (NZ, NX, NC, NY))), v)):
        pl.semaphore_signal(barrier, inc=1, device_id=device(*steps), device_id_type=MESH)

    tile[...] = jnp.zeros_like(tile)
    part[...] = jnp.zeros_like(part)
    other[...] = jnp.zeros_like(other)
    for load in small:
        load.wait()
    block, place = position(owner_ref[...])
    prow[...] = block * ROWS + place

    def count():
        samples = owner_ref.shape[1]
        block, place = position(owner_ref[...])
        high = lax.broadcasted_iota(jnp.int32, (BLOCKS, samples), 0) == block
        low = lax.broadcasted_iota(jnp.int32, (LANE, samples), 0) == place
        info[0:BLOCKS, :] = lax.dot_general(
            jnp.where(high, 1.0, 0.0).astype(jnp.bfloat16),
            jnp.where(low, 1.0, 0.0).astype(jnp.bfloat16),
            (((1,), (1,)), ((), ())), preferred_element_type=jnp.float32,
        )
        tile[0:2, 0:OWN] = assign_ref[...].astype(jnp.float32)
        placed = pltpu.roll(tile[...], x * OWN, 1)
        info[BLOCKS : BLOCKS + 8, :] = jnp.where(c == 0, placed, pltpu.roll(placed, 2, 0))
        info_x[0] = info[...]
        return go_all(
            (info, info_x.at[dx * NC + dc], device(dx=dx, dc=dc)) for dx, dc in group_xc
        )

    def sums(bases, into, waits=()):
        row = lax.broadcasted_iota(jnp.int32, (ROWS, depth), 0)

        def step(k):
            at = pl.ds(pl.multiple_of(k * depth, depth), depth)
            p = prow[:, at]
            hot = jnp.concatenate(
                [jnp.where(row == p - base, 1.0, 0.0).astype(jnp.bfloat16) for base in bases], 0
            )
            got = jnp.dot(hot, emb[at, :], preferred_element_type=jnp.float32)
            for j, ref in enumerate(into):
                for b in range(NX):
                    ref[b] += got[j * ROWS : (j + 1) * ROWS, b * LANE : (b + 1) * LANE]

        if waits:
            for k in range(chunks):
                waits[k].wait()
                step(k)
        else:
            lax.fori_loop(0, chunks, lambda k, carry: (step(k), carry)[1], 0)

    cross = {}

    def work(*slabs):
        bases, into = [], []
        for s in slabs:
            base = zat(ORDER[s]) * (NC * ROWS)
            bases += [base + (1 - c) * ROWS, base + c * ROWS]
            into += [other.at[s], part.at[s]]
        sums(bases, into, loads if 0 in slabs else ())

    def give(s):
        cross[s] = go(other.at[s], other_in.at[s], device(dc=1))

    def meet(s):
        cross[s].wait_recv()
        part[s] += other_in[s]

    xs = {}

    def way_of(s):
        return 1 if s == 1 else -1

    def x_start(s):
        way = way_of(s)
        xs[s, 0] = go(part.at[s, xat(2)], xin.at[s, 0], device(dx=way))
        xs[s, 1] = go(part.at[s, xat(-way)], xin.at[s, 1], device(dx=-way))

    def x_mid(s):
        way = way_of(s)
        xs[s, 0].wait_recv()
        part[s, xat(way)] += xin[s, 0]
        xs[s, 2] = go(part.at[s, xat(way)], xin.at[s, 2], device(dx=way))

    def x_direct(s):
        for k, d in enumerate((2, 1, -1)):
            xs[s, k] = go(part.at[s, xat(d)], xin.at[s, k], device(dx=d))

    zs = {}
    hops = {4: 2, 3: 1}

    def x_end(s):
        d = ORDER[s]
        if (s, 0) in direct:
            xs[s, 0].wait_recv()
        xs[s, 1].wait_recv()
        xs[s, 2].wait_recv()
        total = part[s, x] + xin[s, 1] + xin[s, 2]
        if (s, 0) in direct:
            total = total + xin[s, 0]
        for far in (4, 3) if d == 2 else ():
            zs[far].wait_recv()
            total = total + zin[ORDER.index(far)]
        part[s, x] = total
        if d != 0:
            zs[d] = go(part.at[s, x], zin.at[s], device(dz=hops.get(d, d)))

    direct = {(6, 0)}

    work(0)
    pl.semaphore_wait(barrier, len(greeted))
    give(0)
    arrived = count()

    whole_slab = {}

    def z_whole(s):
        d = ORDER[s]
        whole_slab[s] = go(part.at[s], zslab.at[s - 2], device(dz=d))

    work(1)
    give(1)
    meet(0)
    x_start(0)
    work(2)
    give(2)
    meet(1)
    x_start(1)
    work(3)
    give(3)
    meet(2)
    z_whole(2)
    work(4)
    give(4)
    meet(3)
    z_whole(3)
    x_mid(0)
    arrived()
    whole = info_x[0]
    for j in range(1, NX * NC):
        whole = whole + info_x[j]
    group[...] = whole
    info_z[z] = whole
    arrived_z = go_all(
        (group, info_z.at[z], device(dz=dz)) for dz in (4, 3, 5, 2, 6, 1, 7)
    )
    work(5)
    give(5)
    meet(4)
    x_start(4)
    x_mid(1)
    work(6)
    give(6)
    meet(5)
    x_start(5)
    work(7)
    give(7)
    meet(6)
    x_direct(6)
    x_end(0)
    x_mid(4)
    cross[7].wait_recv()
    whole_slab[2].wait_recv()
    whole_slab[3].wait_recv()
    part[7] += other_in[7] + zslab[0] + zslab[1]
    x_start(7)
    x_end(1)
    x_mid(5)
    x_mid(7)
    x_end(4)
    x_end(6)
    x_end(5)
    x_end(7)
    own = part[7, x]
    for d in (-3, 2, -2):
        zs[d].wait_recv()
        own = own + zin[ORDER.index(d)]

    mine = z * NC + c
    table[mine] = own
    rings, pairs = {}, []

    def blk(dz):
        return zat(dz) * NC + c

    def core_share(dz):
        at = blk(dz)
        pairs.append(go(table.at[at], table.at[at], device(dc=1)))

    square = jnp.sum(own * own, axis=1, keepdims=True)
    sq_own[0] = as_rows([square], pad)[0:1, :]
    sq_arrived = go_all(
        (sq_own.at[0], sq_in.at[dx * NY + dy], device(dx=dx, dy=dy)) for dx, dy in group_xy
    )

    for dz in (2, -2, 1, -1):
        rings[dz] = go(table.at[mine], table.at[mine], device(dz=dz))
    core_share(0)

    arrived_z()
    total = info_z[0, 0:BLOCKS]
    for j in range(1, NZ):
        total = total + info_z[j, 0:BLOCKS]
    counts[...] = total

    scaled[...] = jnp.zeros_like(scaled)

    half = ROWS // 2
    for way in (1, -1):
        rings[2 * way].wait_recv()
        at = blk(-2 * way)
        rings[3 * way] = go(table.at[at], table.at[at], device(dz=way))
        rows = pl.ds(0 if way > 0 else half, half)
        rings[4 * way] = go(table.at[at, rows], table.at[at, rows], device(dz=2 * way))
        core_share(-2 * way)
    for way in (1, -1):
        rings[way].wait_recv()
        core_share(-way)

    sq_arrived()
    square_row = sq_own[0]
    for j in range(1, NX * NY):
        square_row = square_row + sq_in[j]
    inverse = lax.rsqrt(square_row / features + EPS)
    scale[mine] = inverse
    scale_arrived = go_all(
        (scale.at[mine], scale.at[mine], device(dz=dz, dc=dc)) for dz, dc in group_zc
    )
    means = own * as_columns(jnp.broadcast_to(inverse, (8, LANE)))[0:ROWS, 0:1]

    keys_all = group[BLOCKS : BLOCKS + 8, :]
    keys = as_columns(jnp.where(c == 0, keys_all, pltpu.roll(keys_all, 6, 0)))
    cents = NX * cent_ref.shape[0]
    r = lax.broadcasted_iota(jnp.int32, (cents, LANE), 0)
    per = cent_ref.shape[0]
    r = z * (cents * NC) + lax.div(r, per) * (per * NC) + c * per + lax.rem(r, per)
    cent_key = r.astype(jnp.float32)
    spread_key = [jnp.broadcast_to(keys[0:ROWS, t : t + 1], (ROWS, LANE)) for t in range(2)]
    parts = [
        (0, cents, cent_key, 0), (cents, cents, cent_key, 1),
        (2 * cents, ROWS, spread_key[0], 0), (2 * cents + ROWS, ROWS, spread_key[1], 1),
    ]
    weight[...] = jnp.zeros_like(weight)
    for b in range(BLOCKS):
        many = counts[b : b + 1, :]
        for at, n, key, t in parts:
            line = BLOCKS + 2 * (b % NC) + t
            same = jnp.where(key == info_z[b // NC, line : line + 1, :], 1.0, 0.0)
            match[at : at + n, b * LANE : (b + 1) * LANE] = same.astype(jnp.bfloat16)
            weight[at : at + n, :] += same * many
    summed = jnp.sum(weight[...], axis=1, keepdims=True)
    weight[...] = jnp.broadcast_to(summed, weight.shape)
    first_row = 2 * cents
    wrows[...] = as_rows(
        [summed[first_row : first_row + ROWS], summed[first_row + ROWS : first_row + 2 * ROWS]], pad
    )

    for way in (1, -1):
        rings[3 * way].wait_recv()
        core_share(-3 * way)
    rings[4].wait_recv()
    rings[-4].wait_recv()
    core_share(4)

    scale_arrived()
    for b in range(BLOCKS):
        scale2[b : b + 1, :] = scale[b]
    factor = as_columns(counts[...] * scale2[...])
    for pair in pairs:
        pair.wait_recv()
    for b in range(BLOCKS):
        rows = table[b] * factor[0:ROWS, b : b + 1]
        for piece in range(3):
            near = rows.astype(jnp.bfloat16)
            scaled[b * LANE : b * LANE + ROWS, piece * LANE : (piece + 1) * LANE] = near
            rows = rows - near.astype(jnp.float32)
    tot = jnp.dot(match[...], scaled[...], preferred_element_type=jnp.float32)
    tot = tot[:, 0:LANE] + (tot[:, LANE : 2 * LANE] + tot[:, 2 * LANE : 3 * LANE])

    columns = []
    for t in range(2):
        at = first_row + t * ROWS
        many = weight[at : at + ROWS, :]
        g = tot[at : at + ROWS] * jnp.where(many > 0, 1.0 / jnp.maximum(many, 1.0), 0.0)
        d = means - g
        for v in (d * d, d * g, g * g):
            columns.append(jnp.sum(v, axis=1, keepdims=True))
    chosen = jnp.where(weight[cents : 2 * cents, :] > 0, tot[cents : 2 * cents], tot[0:cents])
    sel[...] = chosen
    squares = jnp.sum(chosen * chosen, axis=1, keepdims=True)
    columns.append(jnp.concatenate([squares, jnp.zeros((ROWS - cents, 1), jnp.float32)], 0))
    final_own[...] = as_rows(columns, pad)
    final_arrived = go_all(
        (final_own, final_in.at[dx * NY + dy], device(dx=dx, dy=dy)) for dx, dy in group_xy
    )
    sel_arrived = go_all(
        (sel.at[pl.ds(pl.multiple_of(xat(dx) * per, per), per)], sel_in.at[x], device(dx=dx))
        for dx in (2, 1, 3)
    )
    here = pl.ds(pl.multiple_of(x * per, per), per)
    sel_in[x] = sel[here, :]

    final_arrived()
    last_sum = final_own[...]
    for j in range(1, NX * NY):
        last_sum = last_sum + final_in[j]
    for t in range(2):
        far, mixed, length = (last_sum[3 * t + j : 3 * t + j + 1] for j in range(3))
        many = wrows[t : t + 1, :]
        s = many * lax.rsqrt(many * many * (length / features) + EPS) - 1.0
        value = (far - 2.0 * s * mixed + s * s * length) / features
        value = pltpu.roll(jnp.broadcast_to(value, (8, LANE)), LANE - x * OWN, 1)
        spread_ref[t : t + 1, :] = value[0:1, 0:OWN]
    lens[...] = as_columns(last_sum)
    length = lens[here, 6:7]
    inverse = lax.rsqrt(length / features + EPS)
    first = weight[here, :]
    second = weight[pl.ds(pl.multiple_of(x * per + cents, per), per), :]
    keep = jnp.maximum(first, second) > 0
    sel_arrived()
    for b in range(NX):
        at = slice(b * LANE, (b + 1) * LANE)
        cent_ref[:, at] = jnp.where(keep, sel_in[b] * inverse, init_ref[:, at])

    for wait in sent:
        wait()


COPIES = 7 + 7 + 8 + 18 + 2 + 5 + 8 + 8 + 15 + 15 + 15 + 3


def per_device(features, embeddings, sample_owner, lloyd_assign, init_centroids):
    samples, width = embeddings.shape
    per = init_centroids.shape[0]
    depth = 2048
    f32, bf16 = jnp.float32, jnp.bfloat16
    vm = pltpu.VMEM
    cents = NX * per
    lines = 2 * (cents + ROWS)
    scratch = [
        vm((1, samples), jnp.int32),
        vm((2, OWN), jnp.int32),
        vm((per, width), f32),
        vm((samples, width), bf16),
        vm((NZ, NX, ROWS, LANE), f32),
        vm((NZ, NX, ROWS, LANE), f32),
        vm((NZ, NX, ROWS, LANE), f32),
        vm((NZ, 3, ROWS, LANE), f32),
        vm((2, NX, ROWS, LANE), f32),
        vm((NZ, ROWS, LANE), f32),
        vm((1, samples), jnp.int32),
        vm((8, LANE), f32),
        vm((24, LANE), f32),
        vm((NX * NC, 24, LANE), f32),
        vm((24, LANE), f32),
        vm((NZ, 24, LANE), f32),
        vm((BLOCKS, LANE), f32),
        vm((lines, BLOCKS * LANE), bf16),
        vm((lines, LANE), f32),
        vm((LANE, LANE), f32),
        vm((8, LANE), f32),
        vm((BLOCKS, ROWS, LANE), f32),
        vm((1, 1, LANE), f32),
        vm((NX * NY, 1, LANE), f32),
        vm((BLOCKS, 1, LANE), f32),
        vm((BLOCKS, LANE), f32),
        vm((BLOCKS * LANE, 3 * LANE), bf16),
        vm((8, LANE), f32),
        vm((NX * NY, 8, LANE), f32),
        vm((cents, LANE), f32),
        vm((NX, per, LANE), f32),
        vm((LANE, 8), f32),
        pltpu.SemaphoreType.DMA((samples // depth + 3,)),
        pltpu.SemaphoreType.DMA((COPIES,)),
        pltpu.SemaphoreType.DMA((COPIES,)),
    ]
    in_vmem = pl.BlockSpec(memory_space=pltpu.VMEM)

    def body(*refs):
        kernel(depth, width, features, *refs)

    packed = pl.pallas_call(
        body,
        name="recluster",
        out_shape=(vm((per, width), f32), vm((2, OWN), f32)),
        in_specs=[pl.BlockSpec(memory_space=pl.ANY)] * 4,
        out_specs=(in_vmem, in_vmem),
        scratch_shapes=scratch,
        compiler_params=pltpu.CompilerParams(
            collective_id=0, has_side_effects=True, vmem_limit_bytes=60 << 20
        ),
    )(sample_owner.reshape(1, samples), lloyd_assign, init_centroids, embeddings)

    def hand_out(cent_in, spread_in, cent_out, spread_out, sem):
        copies = [
            pltpu.make_async_copy(cent_in, cent_out, sem.at[0]),
            pltpu.make_async_copy(spread_in, spread_out, sem.at[1]),
        ]
        for copy in copies:
            copy.start()
        for copy in copies:
            copy.wait()

    anywhere = pl.BlockSpec(memory_space=pl.ANY)
    return pl.pallas_call(
        hand_out,
        name="hand_out",
        out_shape=(
            jax.ShapeDtypeStruct((per, width), f32),
            jax.ShapeDtypeStruct((2, OWN), f32),
        ),
        in_specs=[in_vmem] * 2,
        out_specs=(anywhere, anywhere),
        scratch_shapes=[pltpu.SemaphoreType.DMA((2,))],
    )(*(pltpu.with_memory_space_constraint(v, pltpu.VMEM) for v in packed))


def solution(mesh):
    def run(embeddings, sample_owner, lloyd_assign, init_centroids):
        features = embeddings.shape[1]
        return jax.shard_map(
            lambda *args: per_device(features, *args),
            mesh=mesh,
            in_specs=(P("dp", "feat"), P("dp"), P(None, "dp"), P("dp", "feat")),
            out_specs=(P("dp", "feat"), P(None, "dp")),
            check_vma=False,
        )(embeddings, sample_owner, lloyd_assign, init_centroids)

    return run
```

```python
import jax
import jax.numpy as jnp
from jax import lax
from jax.experimental import pallas as pl
from jax.experimental.pallas import tpu as pltpu
from jax.sharding import PartitionSpec as P

EPS = 1e-06
MESH = pl.DeviceIdType.MESH

NZ, NX, NC, NY = 8, 4, 2, 4
OWN = 24
ROWS = NX * OWN
BLOCKS = NZ * NC
LANE = 128
ORDER = (4, 3, 1, -1, -3, 2, -2, 0)


def position(owner):
    slab = lax.shift_right_logical(owner * 21846, 22)
    left = owner - slab * (NX * NC * OWN)
    column = lax.shift_right_logical(left * 1366, 16)
    inner = left - column * (NC * OWN)
    core = jnp.where(inner >= OWN, 1, 0)
    block = slab * NC + core
    return block, column * OWN + inner - core * OWN


def as_rows(columns, pad_ref):
    pad_ref[...] = jnp.zeros_like(pad_ref)
    lane = lax.broadcasted_iota(jnp.int32, (ROWS, LANE), 1)
    filled = jnp.zeros((ROWS, LANE), jnp.float32)
    for j, column in enumerate(columns):
        filled = jnp.where(lane == j, column, filled)
    pad_ref[0:ROWS, :] = filled
    return jnp.transpose(pad_ref[...])[0:8, :]


def as_columns(tile):
    return jnp.transpose(tile)


def kernel(
    depth, width, features,
    owner_hbm, assign_hbm, init_hbm, emb_hbm,
    cent_ref, spread_ref,
    owner_ref, assign_ref, init_ref,
    emb, part, other, other_in, xin, zslab, zin,
    prow, tile, info, info_x, group, info_z, counts, match, weight, pad, wrows,
    table, sq_own, sq_in, scale, scale2, scaled, final_own, final_in, sel, sel_in, lens,
    load_sem, send_sem, recv_sem,
):
    dp, y = lax.axis_index("dp"), lax.axis_index("feat")
    z = lax.div(dp, NX * NC)
    x = lax.div(dp - z * (NX * NC), NC)
    c = dp - z * (NX * NC) - x * NC

    def around(at, size):
        steps = [at]
        for d in range(1, size):
            steps.append(jnp.where(at + d >= size, at + (d - size), at + d))
        return steps

    z_at, x_at, c_at, y_at = around(z, NZ), around(x, NX), around(c, NC), around(y, NY)
    z_first = [at * (NX * NC) for at in z_at]
    x_first = [at * NC for at in x_at]

    def zat(d):
        return z_at[d % NZ]

    def xat(d):
        return x_at[d % NX]

    def device(dz=0, dx=0, dc=0, dy=0):
        return (z_first[dz % NZ] + (x_first[dx % NX] + c_at[dc % NC]), y_at[dy % NY])

    used = [0]
    sent = []

    def go(src, dst, to):
        slot = used[0]
        used[0] += 1
        copy = pltpu.make_async_remote_copy(
            src_ref=src, dst_ref=dst, send_sem=send_sem.at[slot], recv_sem=recv_sem.at[slot],
            device_id=to, device_id_type=MESH,
        )
        copy.start()
        sent.append(copy.wait_send)
        return copy

    def go_all(makes):
        copies = [go(*make) for make in makes]

        def wait():
            for copy in copies:
                copy.wait_recv()

        return wait

    group_xc = [(dx, dc) for dx in (2, 1, 3, 0) for dc in range(NC) if (dx, dc) != (0, 0)]
    group_xy = [
        (dx, dy) for dx in (2, 1, 3, 0) for dy in (2, 1, 3, 0) if (dx, dy) != (0, 0)
    ]
    group_zc = [
        (dz, dc) for dz in (4, 3, 5, 2, 6, 1, 7, 0) for dc in range(NC) if (dz, dc) != (0, 0)
    ]

    chunks = emb.shape[0] // depth
    loads = [
        pltpu.make_async_copy(
            emb_hbm.at[pl.ds(k * depth, depth)], emb.at[pl.ds(k * depth, depth)], load_sem.at[k]
        )
        for k in range(chunks)
    ]
    small = [
        pltpu.make_async_copy(src, dst, load_sem.at[chunks + k])
        for k, (src, dst) in enumerate(
            ((owner_hbm, owner_ref), (assign_hbm, assign_ref), (init_hbm, init_ref))
        )
    ]
    for load in small + loads:
        load.start()

    barrier = pltpu.get_barrier_semaphore()

    greeted = {(dz, 0, dc, 0) for dz, dc in group_zc}
    greeted |= {(0, dx, 0, dy) for dx, dy in group_xy} | {(0, dx, dc, 0) for dx, dc in group_xc}
    for steps in sorted(greeted, key=lambda v: (-sum(min(a, b - a) for a, b in zip(v, (NZ, NX, NC, NY))), v)):
        pl.semaphore_signal(barrier, inc=1, device_id=device(*steps), device_id_type=MESH)

    tile[...] = jnp.zeros_like(tile)
    part[...] = jnp.zeros_like(part)
    other[...] = jnp.zeros_like(other)
    for load in small:
        load.wait()
    block, place = position(owner_ref[...])
    prow[...] = block * ROWS + place

    def count():
        samples = owner_ref.shape[1]
        block, place = position(owner_ref[...])
        high = lax.broadcasted_iota(jnp.int32, (BLOCKS, samples), 0) == block
        low = lax.broadcasted_iota(jnp.int32, (LANE, samples), 0) == place
        info[0:BLOCKS, :] = lax.dot_general(
            jnp.where(high, 1.0, 0.0).astype(jnp.bfloat16),
            jnp.where(low, 1.0, 0.0).astype(jnp.bfloat16),
            (((1,), (1,)), ((), ())), preferred_element_type=jnp.float32,
        )
        tile[0:2, 0:OWN] = assign_ref[...].astype(jnp.float32)
        placed = pltpu.roll(tile[...], x * OWN, 1)
        info[BLOCKS : BLOCKS + 8, :] = jnp.where(c == 0, placed, pltpu.roll(placed, 2, 0))
        info_x[0] = info[...]
        return go_all(
            (info, info_x.at[dx * NC + dc], device(dx=dx, dc=dc)) for dx, dc in group_xc
        )

    def sums(bases, into, size, waits=()):
        row = lax.broadcasted_iota(jnp.int32, (ROWS, size), 0)

        def step(k):
            at = pl.ds(pl.multiple_of(k * size, size), size)
            p = prow[:, at]
            hot = jnp.concatenate(
                [jnp.where(row == p - base, 1.0, 0.0).astype(jnp.bfloat16) for base in bases], 0
            )
            got = jnp.dot(hot, emb[at, :], preferred_element_type=jnp.float32)
            for j, ref in enumerate(into):
                for b in range(NX):
                    ref[b] += got[j * ROWS : (j + 1) * ROWS, b * LANE : (b + 1) * LANE]

        def turn(k, carry):
            step(k)
            return carry

        if waits:
            for k, load in enumerate(waits):
                load.wait()
                step(k)
        else:
            lax.fori_loop(0, emb.shape[0] // size, turn, 0)

    cross = {}

    def work(*slabs):
        bases, into = [], []
        for s in slabs:
            base = zat(ORDER[s]) * (NC * ROWS)
            bases += [base + (1 - c) * ROWS, base + c * ROWS]
            into += [other.at[s], part.at[s]]
        sums(bases, into, depth if 0 in slabs else 2 * depth, loads if 0 in slabs else ())

    def give(s):
        cross[s] = go(other.at[s], other_in.at[s], device(dc=1))

    def meet(s):
        cross[s].wait_recv()
        part[s] += other_in[s]

    xs = {}

    def way_of(s):
        return 1 if s == 1 else -1

    def x_start(s):
        way = way_of(s)
        xs[s, 0] = go(part.at[s, xat(2)], xin.at[s, 0], device(dx=way))
        xs[s, 1] = go(part.at[s, xat(-way)], xin.at[s, 1], device(dx=-way))

    def x_mid(s):
        way = way_of(s)
        xs[s, 0].wait_recv()
        part[s, xat(way)] += xin[s, 0]
        xs[s, 2] = go(part.at[s, xat(way)], xin.at[s, 2], device(dx=way))

    def x_direct(s):
        for k, d in enumerate((2, 1, -1)):
            xs[s, k] = go(part.at[s, xat(d)], xin.at[s, k], device(dx=d))

    zs = {}
    hops = {4: 2, 3: 1}

    def x_end(s):
        d = ORDER[s]
        if (s, 0) in direct:
            xs[s, 0].wait_recv()
        xs[s, 1].wait_recv()
        xs[s, 2].wait_recv()
        total = part[s, x] + xin[s, 1] + xin[s, 2]
        if (s, 0) in direct:
            total = total + xin[s, 0]
        for far in (4, 3) if d == 2 else ():
            zs[far].wait_recv()
            total = total + zin[ORDER.index(far)]
        part[s, x] = total
        if d != 0:
            zs[d] = go(part.at[s, x], zin.at[s], device(dz=hops.get(d, d)))

    direct = {(6, 0)}

    work(0)
    pl.semaphore_wait(barrier, len(greeted))
    give(0)
    arrived = count()

    whole_slab = {}

    def z_whole(s):
        d = ORDER[s]
        whole_slab[s] = go(part.at[s], zslab.at[s - 2], device(dz=d))

    work(1)
    give(1)
    meet(0)
    x_start(0)
    work(2)
    give(2)
    meet(1)
    x_start(1)
    work(3)
    give(3)
    meet(2)
    z_whole(2)
    work(4)
    give(4)
    meet(3)
    z_whole(3)
    x_mid(0)
    arrived()
    whole = info_x[0]
    for j in range(1, NX * NC):
        whole = whole + info_x[j]
    group[...] = whole
    info_z[z] = whole
    arrived_z = go_all(
        (group, info_z.at[z], device(dz=dz)) for dz in (4, 3, 5, 2, 6, 1, 7)
    )
    work(5)
    give(5)
    meet(4)
    x_start(4)
    x_mid(1)
    work(6)
    give(6)
    meet(5)
    x_start(5)
    work(7)
    give(7)
    meet(6)
    x_direct(6)
    x_end(0)
    x_mid(4)
    cross[7].wait_recv()
    whole_slab[2].wait_recv()
    whole_slab[3].wait_recv()
    part[7] += other_in[7] + zslab[0] + zslab[1]
    x_start(7)
    x_end(1)
    x_mid(5)
    x_mid(7)
    x_end(4)
    x_end(6)
    x_end(5)
    x_end(7)
    own = part[7, x]
    for d in (-3, 2, -2):
        zs[d].wait_recv()
        own = own + zin[ORDER.index(d)]

    mine = z * NC + c
    table[mine] = own
    rings, pairs = {}, []

    def blk(dz):
        return zat(dz) * NC + c

    def core_share(dz):
        at = blk(dz)
        pairs.append(go(table.at[at], table.at[at], device(dc=1)))

    square = jnp.sum(own * own, axis=1, keepdims=True)
    sq_own[0] = as_rows([square], pad)[0:1, :]
    sq_arrived = go_all(
        (sq_own.at[0], sq_in.at[dx * NY + dy], device(dx=dx, dy=dy)) for dx, dy in group_xy
    )

    for dz in (2, -2, 1, -1):
        rings[dz] = go(table.at[mine], table.at[mine], device(dz=dz))
    core_share(0)

    arrived_z()
    total = info_z[0, 0:BLOCKS]
    for j in range(1, NZ):
        total = total + info_z[j, 0:BLOCKS]
    counts[...] = total

    scaled[...] = jnp.zeros_like(scaled)

    half = ROWS // 2
    for way in (1, -1):
        rings[2 * way].wait_recv()
        at = blk(-2 * way)
        rings[3 * way] = go(table.at[at], table.at[at], device(dz=way))
        rows = pl.ds(0 if way > 0 else half, half)
        rings[4 * way] = go(table.at[at, rows], table.at[at, rows], device(dz=2 * way))
        core_share(-2 * way)
    for way in (1, -1):
        rings[way].wait_recv()
        core_share(-way)

    sq_arrived()
    square_row = sq_own[0]
    for j in range(1, NX * NY):
        square_row = square_row + sq_in[j]
    inverse = lax.rsqrt(square_row / features + EPS)
    scale[mine] = inverse
    scale_arrived = go_all(
        (scale.at[mine], scale.at[mine], device(dz=dz, dc=dc)) for dz, dc in group_zc
    )
    means = own * as_columns(jnp.broadcast_to(inverse, (8, LANE)))[0:ROWS, 0:1]

    keys_all = group[BLOCKS : BLOCKS + 8, :]
    keys = as_columns(jnp.where(c == 0, keys_all, pltpu.roll(keys_all, 6, 0)))
    cents = NX * cent_ref.shape[0]
    r = lax.broadcasted_iota(jnp.int32, (cents, LANE), 0)
    per = cent_ref.shape[0]
    r = z * (cents * NC) + lax.div(r, per) * (per * NC) + c * per + lax.rem(r, per)
    cent_key = r.astype(jnp.float32)
    spread_key = [jnp.broadcast_to(keys[0:ROWS, t : t + 1], (ROWS, LANE)) for t in range(2)]
    parts = [
        (0, cents, cent_key, 0), (cents, cents, cent_key, 1),
        (2 * cents, ROWS, spread_key[0], 0), (2 * cents + ROWS, ROWS, spread_key[1], 1),
    ]
    weight[...] = jnp.zeros_like(weight)
    for b in range(BLOCKS):
        many = counts[b : b + 1, :]
        for at, n, key, t in parts:
            line = BLOCKS + 2 * (b % NC) + t
            same = jnp.where(key == info_z[b // NC, line : line + 1, :], 1.0, 0.0)
            match[at : at + n, b * LANE : (b + 1) * LANE] = same.astype(jnp.bfloat16)
            weight[at : at + n, :] += same * many
    summed = jnp.sum(weight[...], axis=1, keepdims=True)
    weight[...] = jnp.broadcast_to(summed, weight.shape)
    first_row = 2 * cents
    wrows[...] = as_rows(
        [summed[first_row : first_row + ROWS], summed[first_row + ROWS : first_row + 2 * ROWS]], pad
    )

    for way in (1, -1):
        rings[3 * way].wait_recv()
        core_share(-3 * way)
    rings[4].wait_recv()
    rings[-4].wait_recv()
    core_share(4)

    scale_arrived()
    for b in range(BLOCKS):
        scale2[b : b + 1, :] = scale[b]
    factor = as_columns(counts[...] * scale2[...])
    for pair in pairs:
        pair.wait_recv()
    for b in range(BLOCKS):
        rows = table[b] * factor[0:ROWS, b : b + 1]
        for piece in range(3):
            near = rows.astype(jnp.bfloat16)
            scaled[b * LANE : b * LANE + ROWS, piece * LANE : (piece + 1) * LANE] = near
            rows = rows - near.astype(jnp.float32)
    tot = jnp.dot(match[...], scaled[...], preferred_element_type=jnp.float32)
    tot = tot[:, 0:LANE] + (tot[:, LANE : 2 * LANE] + tot[:, 2 * LANE : 3 * LANE])

    columns = []
    for t in range(2):
        at = first_row + t * ROWS
        many = weight[at : at + ROWS, :]
        g = tot[at : at + ROWS] * jnp.where(many > 0, 1.0 / jnp.maximum(many, 1.0), 0.0)
        d = means - g
        for v in (d * d, d * g, g * g):
            columns.append(jnp.sum(v, axis=1, keepdims=True))
    chosen = jnp.where(weight[cents : 2 * cents, :] > 0, tot[cents : 2 * cents], tot[0:cents])
    sel[...] = chosen
    squares = jnp.sum(chosen * chosen, axis=1, keepdims=True)
    columns.append(jnp.concatenate([squares, jnp.zeros((ROWS - cents, 1), jnp.float32)], 0))
    final_own[...] = as_rows(columns, pad)
    final_arrived = go_all(
        (final_own, final_in.at[dx * NY + dy], device(dx=dx, dy=dy)) for dx, dy in group_xy
    )
    sel_arrived = go_all(
        (sel.at[pl.ds(pl.multiple_of(xat(dx) * per, per), per)], sel_in.at[x], device(dx=dx))
        for dx in (2, 1, 3)
    )
    here = pl.ds(pl.multiple_of(x * per, per), per)
    sel_in[x] = sel[here, :]

    final_arrived()
    last_sum = final_own[...]
    for j in range(1, NX * NY):
        last_sum = last_sum + final_in[j]
    for t in range(2):
        far, mixed, length = (last_sum[3 * t + j : 3 * t + j + 1] for j in range(3))
        many = wrows[t : t + 1, :]
        s = many * lax.rsqrt(many * many * (length / features) + EPS) - 1.0
        value = (far - 2.0 * s * mixed + s * s * length) / features
        value = pltpu.roll(jnp.broadcast_to(value, (8, LANE)), LANE - x * OWN, 1)
        spread_ref[t : t + 1, :] = value[0:1, 0:OWN]
    lens[...] = as_columns(last_sum)
    length = lens[here, 6:7]
    inverse = lax.rsqrt(length / features + EPS)
    first = weight[here, :]
    second = weight[pl.ds(pl.multiple_of(x * per + cents, per), per), :]
    keep = jnp.maximum(first, second) > 0
    sel_arrived()
    for b in range(NX):
        at = slice(b * LANE, (b + 1) * LANE)
        cent_ref[:, at] = jnp.where(keep, sel_in[b] * inverse, init_ref[:, at])

    for wait in sent:
        wait()


COPIES = 7 + 7 + 8 + 18 + 2 + 5 + 8 + 8 + 15 + 15 + 15 + 3


def per_device(features, embeddings, sample_owner, lloyd_assign, init_centroids):
    samples, width = embeddings.shape
    per = init_centroids.shape[0]
    depth = 1024
    f32, bf16 = jnp.float32, jnp.bfloat16
    vm = pltpu.VMEM
    cents = NX * per
    lines = 2 * (cents + ROWS)
    scratch = [
        vm((1, samples), jnp.int32),
        vm((2, OWN), jnp.int32),
        vm((per, width), f32),
        vm((samples, width), bf16),
        vm((NZ, NX, ROWS, LANE), f32),
        vm((NZ, NX, ROWS, LANE), f32),
        vm((NZ, NX, ROWS, LANE), f32),
        vm((NZ, 3, ROWS, LANE), f32),
        vm((2, NX, ROWS, LANE), f32),
        vm((NZ, ROWS, LANE), f32),
        vm((1, samples), jnp.int32),
        vm((8, LANE), f32),
        vm((24, LANE), f32),
        vm((NX * NC, 24, LANE), f32),
        vm((24, LANE), f32),
        vm((NZ, 24, LANE), f32),
        vm((BLOCKS, LANE), f32),
        vm((lines, BLOCKS * LANE), bf16),
        vm((lines, LANE), f32),
        vm((LANE, LANE), f32),
        vm((8, LANE), f32),
        vm((BLOCKS, ROWS, LANE), f32),
        vm((1, 1, LANE), f32),
        vm((NX * NY, 1, LANE), f32),
        vm((BLOCKS, 1, LANE), f32),
        vm((BLOCKS, LANE), f32),
        vm((BLOCKS * LANE, 3 * LANE), bf16),
        vm((8, LANE), f32),
        vm((NX * NY, 8, LANE), f32),
        vm((cents, LANE), f32),
        vm((NX, per, LANE), f32),
        vm((LANE, 8), f32),
        pltpu.SemaphoreType.DMA((samples // depth + 3,)),
        pltpu.SemaphoreType.DMA((COPIES,)),
        pltpu.SemaphoreType.DMA((COPIES,)),
    ]
    in_vmem = pl.BlockSpec(memory_space=pltpu.VMEM)

    def body(*refs):
        kernel(depth, width, features, *refs)

    packed = pl.pallas_call(
        body,
        name="recluster",
        out_shape=(vm((per, width), f32), vm((2, OWN), f32)),
        in_specs=[pl.BlockSpec(memory_space=pl.ANY)] * 4,
        out_specs=(in_vmem, in_vmem),
        scratch_shapes=scratch,
        compiler_params=pltpu.CompilerParams(
            collective_id=0, has_side_effects=True, vmem_limit_bytes=60 << 20
        ),
    )(sample_owner.reshape(1, samples), lloyd_assign, init_centroids, embeddings)

    def hand_out(cent_in, spread_in, cent_out, spread_out, sem):
        copies = [
            pltpu.make_async_copy(cent_in, cent_out, sem.at[0]),
            pltpu.make_async_copy(spread_in, spread_out, sem.at[1]),
        ]
        for copy in copies:
            copy.start()
        for copy in copies:
            copy.wait()

    anywhere = pl.BlockSpec(memory_space=pl.ANY)
    return pl.pallas_call(
        hand_out,
        name="hand_out",
        out_shape=(
            jax.ShapeDtypeStruct((per, width), f32),
            jax.ShapeDtypeStruct((2, OWN), f32),
        ),
        in_specs=[in_vmem] * 2,
        out_specs=(anywhere, anywhere),
        scratch_shapes=[pltpu.SemaphoreType.DMA((2,))],
    )(*(pltpu.with_memory_space_constraint(v, pltpu.VMEM) for v in packed))


def solution(mesh):
    def run(embeddings, sample_owner, lloyd_assign, init_centroids):
        features = embeddings.shape[1]
        return jax.shard_map(
            lambda *args: per_device(features, *args),
            mesh=mesh,
            in_specs=(P("dp", "feat"), P("dp"), P(None, "dp"), P("dp", "feat")),
            out_specs=(P("dp", "feat"), P(None, "dp")),
            check_vma=False,
        )(embeddings, sample_owner, lloyd_assign, init_centroids)

    return run
```
